32 devices in a mesh: dp: 4 (over z), mp: 8 (over y, x, core).
Axes of the slice: x: 2, y: 2, z: 4, core: 2. Of those that a mesh axis runs over, the one named last changes fastest.
Arguments:
- features: bfloat16 [256, 256, 1, 16, 64], P('mp', None, None, 'dp'), may hold values from -6 to 6
- out_grad: bfloat16 [256, 256, 1, 16, 64], P('mp', None, None, 'dp'), may hold values from -6 to 6
- spectral_weight: bfloat16 [16, 32, 32, 64, 128], P('dp', 'mp'), may hold values from -1.5 to 1.5
- local_weight: bfloat16 [64, 64], replicated, may hold values from -0.75 to 0.75
Outputs:
- layer_out: bfloat16 [256, 256, 1, 16, 64], P('mp', None, None, 'dp')
- feature_grad: bfloat16 [256, 256, 1, 16, 64], P('mp', None, None, 'dp')
- spectral_grad: float32 [16, 32, 32, 64, 128], P('dp', 'mp')
- local_grad: float32 [64, 64], replicated
The draws below stay inside these ranges and needn't reach their ends.
All inputs are finite; a program needn't handle non-finite values.
Results may differ from the reference program's by a relative error of at most 0.03.
Values may be sent and summed in bfloat16 or wider, within the bound.
No kernel may reach another device: no remote copies, remote signals or barrier semaphores. Data moves between devices by JAX's collectives and lax.ppermute only.
A program may use at most 192 MiB of HBM per device.

```python
import math
import jax
import jax.numpy as jnp
from jax import lax

NX = 256
NY = 256
C = 64
KX = 32
KY = 32
KZ_DEV = 4
SNAP = 1
KZ = 16
N_DP = 4
N_MP = 8


def shard_levels(rng, shape, split, least, top_value):
    loudness, own = 1.0, jax.random.fold_in(rng, 6)
    for axis_at, blocks in split:
        steps = jnp.exp(jax.random.uniform(jax.random.fold_in(own, axis_at), (blocks,), jnp.float32, least / len(split), top_value / len(split)))
        loudness = loudness * jnp.repeat(steps, shape[axis_at] // blocks).reshape([-1 if axis == axis_at else 1 for axis in range(len(shape))])
    return loudness


def gaussian(own_key, dims, scale, most, pieces=(), held_as=jnp.bfloat16):
    loudness = shard_levels(own_key, dims, pieces, -0.22, 0.18) if pieces else 1.0
    drawn = jax.random.normal(own_key, dims, jnp.float32) * scale * loudness
    return jnp.minimum(jnp.maximum(drawn, -most), most).astype(held_as)


def setup_inputs(seed: int = 0) -> dict:
    keys = jax.random.split(jax.random.key(seed), 5)
    features = gaussian(keys[0], (NX, NY, SNAP, KZ, C), 1.0, 6.0, ((0, 8), (3, 4)))
    out_grad = gaussian(keys[1], (NX, NY, SNAP, KZ, C), 1.0, 6.0, ((0, 8), (3, 4)))
    spectral_weight = gaussian(keys[2], (KZ, KY, KX, C, 2 * C), (C // 4) ** -0.5, 1.5, ((0, 4), (1, 8)))
    local_weight = gaussian(keys[3], (C, C), C ** -0.5, 0.75)
    return dict(features=features, out_grad=out_grad, spectral_weight=spectral_weight, local_weight=local_weight)


HIGHEST = lax.Precision.HIGHEST

def make_tables(slab_count):
    y_index = jnp.arange(NY, dtype=jnp.int32)
    k_index = jnp.arange(KY, dtype=jnp.int32)
    y_angle = 2.0 * math.pi / NY * (k_index[:, None] * y_index[None, :] % NY).astype(jnp.float32)
    y_scale = 1.0 / math.sqrt(NY)
    y_table = jnp.stack([jnp.cos(y_angle) * y_scale, -jnp.sin(y_angle) * y_scale]).astype(jnp.bfloat16)
    k_weight = jnp.where(k_index == 0, 1.0, 2.0).astype(jnp.float32)
    y_back = (jnp.transpose(y_table.astype(jnp.float32), (2, 0, 1)) * k_weight).astype(jnp.bfloat16)
    stored_index = jnp.arange(NX, dtype=jnp.int32)
    slab_rows = NX // slab_count
    x_index = stored_index % slab_rows * slab_count + stored_index // slab_rows
    frequency = jnp.arange(KX, dtype=jnp.int32) - KX // 2
    x_angle = 2.0 * math.pi / NX * (frequency[:, None] * x_index[None, :] % NX).astype(jnp.float32)
    x_scale = 1.0 / math.sqrt(NX)
    x_cosine = jnp.cos(x_angle) * x_scale
    x_sine = jnp.sin(x_angle) * x_scale
    x_table = jnp.stack([jnp.stack([x_cosine, x_sine], 1), jnp.stack([-x_sine, x_cosine], 1)]).astype(jnp.bfloat16)
    x_back = jnp.transpose(x_table, (2, 3, 0, 1))
    return (y_table, y_back, x_table, x_back)

def contract(form, left, right):
    return jnp.einsum(form, left.astype(jnp.float32), right.astype(jnp.float32), precision=HIGHEST)

def block_weights(weights):
    channels = weights.shape[-1] // 2
    w_real = weights[..., :channels]
    w_imag = weights[..., channels:]
    upper = jnp.concatenate([w_real, w_imag], -1)
    lower = jnp.concatenate([-w_imag, w_real], -1)
    return jnp.concatenate([upper, lower], -2)

def to_items(coeffs, snaps, zcount):
    mode_rows, _, kx_count, columns = coeffs.shape
    channels = columns // (snaps * zcount)
    shaped = coeffs.reshape(mode_rows, 2, kx_count, snaps, zcount, channels).transpose(4, 0, 2, 3, 1, 5)
    return shaped.reshape(zcount, mode_rows * kx_count, snaps, 2 * channels)

def from_items(mode_items, mode_rows, snaps):
    zcount, total, _, double = mode_items.shape
    channels = double // 2
    kx_count = total // mode_rows
    shaped = mode_items.reshape(zcount, mode_rows, kx_count, snaps, 2, channels).transpose(1, 4, 2, 3, 0, 5)
    return shaped.reshape(mode_rows, 2, kx_count, snaps * zcount * channels)

def combine(gram_blocks, mode_rows):
    channels = gram_blocks.shape[-1] // 2
    top_left = gram_blocks[..., :channels, :channels]
    top_right = gram_blocks[..., :channels, channels:]
    low_left = gram_blocks[..., channels:, :channels]
    low_right = gram_blocks[..., channels:, channels:]
    joined = jnp.concatenate([top_left + low_right, top_right - low_left], -1)
    return joined.reshape(gram_blocks.shape[0], mode_rows, -1, channels, 2 * channels)

def activation(values):
    return jax.nn.gelu(values, approximate=True)

def layer_block(features, out_grad, spectral_weight, local_weight, tables):
    y_table, y_back, x_table, x_back = tables
    grid_x, grid_y, snaps, zcount, channels = features.shape
    columns = snaps * zcount * channels
    flat_field = features.reshape(grid_x, grid_y, columns)
    spectrum_y = contract('xyq,rky->xrkq', flat_field, y_table).astype(jnp.bfloat16)
    mode_coeffs = contract('ojrx,xrkq->kojq', x_table, spectrum_y).astype(jnp.bfloat16)
    blocks = block_weights(spectral_weight).reshape(zcount, KY * KX, 2 * channels, 2 * channels)
    mode_items = to_items(mode_coeffs, snaps, zcount)
    mixed_items = contract('zmpi,zmio->zmpo', mode_items, blocks).astype(jnp.bfloat16)
    mixed_modes = from_items(mixed_items, KY, snaps)
    grid_rows = contract('rxoj,kojq->xrkq', x_back, mixed_modes).astype(jnp.bfloat16)
    local_part = jnp.dot(features.reshape(-1, channels), local_weight, preferred_element_type=jnp.float32)
    preact = contract('yrk,xrkq->xyq', y_back, grid_rows) + local_part.reshape(grid_x, grid_y, columns)
    output, pullback = jax.vjp(activation, preact)
    preact_grad = pullback(out_grad.reshape(grid_x, grid_y, columns).astype(jnp.float32))[0].astype(jnp.bfloat16)
    local_term = jnp.dot(features.reshape(-1, channels).T, preact_grad.reshape(-1, channels), preferred_element_type=jnp.float32)
    rows_grad = contract('yrk,xyq->xrkq', y_back, preact_grad).astype(jnp.bfloat16)
    mixed_grad = contract('ojrx,xrkq->kojq', x_table, rows_grad).astype(jnp.bfloat16)
    grad_items = to_items(mixed_grad, snaps, zcount)
    gram_blocks = contract('zmpi,zmpo->zmio', mode_items, grad_items)
    weight_part = combine(gram_blocks, KY)
    back_items = contract('zmpo,zmio->zmpi', grad_items, blocks).astype(jnp.bfloat16)
    modes_grad = from_items(back_items, KY, snaps)
    spectrum_grad = contract('rxoj,kojq->xrkq', x_back, modes_grad).astype(jnp.bfloat16)
    local_back = jnp.dot(preact_grad.reshape(-1, channels), local_weight.T, preferred_element_type=jnp.float32)
    back_field = contract('rky,xrkq->xyq', y_table, spectrum_grad) + local_back.reshape(grid_x, grid_y, columns)
    return (output.astype(jnp.bfloat16).reshape(features.shape), back_field.astype(jnp.bfloat16).reshape(features.shape), weight_part, local_term)

def reference(features, out_grad, spectral_weight, local_weight):
    tables = make_tables(N_MP)

    def scan_step(state_carry, block_index):
        outputs, gradients, weight_total, local_total = state_carry
        first_row = (block_index * KZ_DEV).astype(jnp.int32)
        field_block = lax.dynamic_slice_in_dim(features, first_row, KZ_DEV, 3)
        grad_block = lax.dynamic_slice_in_dim(out_grad, first_row, KZ_DEV, 3)
        weight_block = lax.dynamic_slice_in_dim(spectral_weight, first_row, KZ_DEV, 0)
        out_block, back_block, weight_part, local_term = layer_block(field_block, grad_block, weight_block, local_weight, tables)
        outputs = lax.dynamic_update_slice_in_dim(outputs, out_block, first_row, 3)
        gradients = lax.dynamic_update_slice_in_dim(gradients, back_block, first_row, 3)
        weight_total = lax.dynamic_update_slice_in_dim(weight_total, weight_part, first_row, 0)
        return ((outputs, gradients, weight_total, local_total + local_term), None)
    initial = (jnp.zeros(features.shape, jnp.bfloat16), jnp.zeros(features.shape, jnp.bfloat16), jnp.zeros((KZ, KY, KX, C, 2 * C), jnp.float32), jnp.zeros((C, C), jnp.float32))
    final, _ = lax.scan(scan_step, initial, jnp.arange(N_DP, dtype=jnp.int32))
    grad_scale = 1.0 / math.sqrt(NX * NY * SNAP * KZ)
    return (final[0], final[1], final[2], final[3] * grad_scale)
```

```python
import functools
import math

import jax
import jax.numpy as jnp
import ml_dtypes
import numpy as np
from jax import lax
from jax.experimental import pallas as pl
from jax.experimental.pallas import tpu as pltpu
from jax.sharding import PartitionSpec as P

NX = 256
NY = 256
KX = 32
KY = 32
F32 = jnp.float32
BF16 = jnp.bfloat16
ROOT = math.sqrt(2.0 / math.pi)
CUBE = 0.044715


def to_bf16(values):
    return values.astype(np.float32).astype(ml_dtypes.bfloat16)


def y_tables(count):
    block = KY // count
    k_index = np.arange(KY)
    angle = 2.0 * math.pi / NY * (k_index[:, None] * np.arange(NY)[None, :] % NY)
    table = to_bf16(np.stack([np.cos(angle), -np.sin(angle)]) / math.sqrt(NY)).astype(np.float32)
    weight = np.where(k_index == 0, 1.0, 2.0)[None, :, None]

    def ordered(values):
        shaped = values.reshape(2, count // 2, 2, block, NY).transpose(2, 1, 0, 3, 4)
        return to_bf16(shaped.reshape(2 * KY, NY))

    return ordered(table), ordered(table * weight)


def x_tables(count):
    block = KY // count
    rows = NX // count
    stored = np.arange(NX)
    x_index = stored % rows * count + stored // rows
    frequency = np.arange(KX) - KX // 2
    angle = 2.0 * math.pi / NX * (frequency[:, None] * x_index[None, :] % NX)
    cosine = np.cos(angle) / math.sqrt(NX)
    sine = np.sin(angle) / math.sqrt(NX)
    table = np.stack([np.stack([cosine, sine], 1), np.stack([-sine, cosine], 1)])
    per = table.reshape(2, KX, 2, count, rows).transpose(3, 0, 1, 4, 2)
    spread = np.einsum("nojxr,ab->noajxrb", per, np.eye(block))
    spread = to_bf16(spread.reshape(count, 2 * block * KX, rows * 2 * block))
    return spread, np.ascontiguousarray(spread.transpose(0, 2, 1))


def dot(left, right):
    return lax.dot_general(left, right, (((1,), (0,)), ((), ())), preferred_element_type=F32)


def dot_nt(left, right):
    return lax.dot_general(left, right, (((1,), (1,)), ((), ())), preferred_element_type=F32)


def whole(shape):
    zeros = (0,) * len(shape)
    return pl.BlockSpec(shape, lambda *_: zeros)


def call(kernel, here, operands, grid, in_specs, out_specs, out_shape, scratch=(), flops=0, moved=0, name=None):
    return pl.pallas_call(
        kernel,
        out_shape=out_shape,
        grid_spec=pltpu.PrefetchScalarGridSpec(
            num_scalar_prefetch=1,
            grid=grid,
            in_specs=in_specs,
            out_specs=out_specs,
            scratch_shapes=list(scratch),
        ),
        compiler_params=pltpu.CompilerParams(
            dimension_semantics=("arbitrary",) * len(grid), vmem_limit_bytes=40 << 20
        ),
        cost_estimate=pl.CostEstimate(flops=flops, bytes_accessed=moved, transcendentals=0),
        name=name,
    )(here, *operands)


def store_spectrum(here, parts, keep_ref, send_ref):
    chips, width, _ = keep_ref.shape
    unit = width // len(parts)
    half = chips * unit
    own_first = here[0] % 2 == 0
    kept = [jnp.where(own_first, part[:half], part[half:]) for part in parts]
    sent = [jnp.where(own_first, part[half:], part[:half]) for part in parts]
    for chip in range(chips):
        rows = slice(chip * unit, (chip + 1) * unit)
        keep_ref[chip] = jnp.concatenate([part[rows] for part in kept], 0).astype(BF16)
        send_ref[chip] = jnp.concatenate([part[rows] for part in sent], 0).astype(BF16)


def forward_y(here, field_ref, table_ref, keep_ref, send_ref):
    table = table_ref[...]
    parts = [dot_nt(table, field_ref[x]) for x in range(field_ref.shape[0])]
    store_spectrum(here, parts, keep_ref, send_ref)


def forward_x(here, keep_ref, got_ref, own_ref, other_ref, *outs):
    chip = here[0] // 2
    for step, out in enumerate(outs):
        at = chip ^ step
        out[...] = (dot(own_ref[0], keep_ref[at]) + dot(other_ref[0], got_ref[at])).astype(BF16)


def total(refs):
    values = [ref[...].astype(F32) for ref in refs]
    while len(values) > 1:
        values = [a + b for a, b in zip(values[::2], values[1::2])]
    return values[0].astype(BF16).astype(F32)


def half_sign(shape):
    lane = lax.broadcasted_iota(jnp.int32, shape, 1)
    return jnp.where(lane % 128 < 64, -1.0, 1.0)


def low_half(shape):
    return lax.broadcasted_iota(jnp.int32, shape, 1) < 64


def mix_forward(count, zs, here, *refs):
    terms, (w_ref, out_ref, spread_ref, coeff, prod) = refs[:count], refs[count:]
    i, jc = pl.program_id(0), pl.program_id(1)
    per = w_ref.shape[2]
    modes = coeff.shape[0] // 2
    first = (i * pl.num_programs(1) + jc) * per

    @pl.when(first == 0)
    def _():
        coeff[...] = total(terms)

    shape = (2 * zs, zs * 64)
    row = lax.broadcasted_iota(jnp.int32, shape, 0)
    keep = lax.broadcasted_iota(jnp.int32, shape, 1) // 64 == row % zs
    is_real = row < zs
    for pair in range(per // 2):
        lefts, weights = [], []
        for sub in range(2):
            at = first + 2 * pair + sub
            real = jnp.broadcast_to(coeff[pl.ds(at, 1), :], shape)
            imag = jnp.broadcast_to(coeff[pl.ds(modes + at, 1), :], shape)
            lefts.append(jnp.where(keep, jnp.where(is_real, real, imag), 0.0))
            weights.append(w_ref[:, 0, 2 * pair + sub].reshape(zs * 64, 128))
        left = jnp.concatenate(lefts, 0).astype(BF16)
        base = pl.multiple_of((first + 2 * pair) * 2 * zs, 4 * zs)
        spread_ref[pl.ds(base, 4 * zs), :] = left
        got = dot(left, jnp.concatenate(weights, 1))
        prod[pl.ds(base, 2 * zs), :] = got[: 2 * zs, :128]
        prod[pl.ds(base + 2 * zs, 2 * zs), :] = got[2 * zs :, 128:]

    @pl.when(first + per == modes)
    def _():
        sign = half_sign((modes, 128))
        low = low_half((modes, 128))
        for tile in range(zs // 2):
            rows = []
            for z in (2 * tile, 2 * tile + 1):
                real = prod[pl.ds(z, modes, stride=2 * zs), :]
                imag = prod[pl.ds(zs + z, modes, stride=2 * zs), :]
                rows.append(real + sign * pltpu.roll(imag, 64, 1))
            lanes = slice(tile * 128, (tile + 1) * 128)
            out_ref[:modes, lanes] = jnp.where(low, rows[0], pltpu.roll(rows[1], 64, 1)).astype(BF16)
            out_ref[modes:, lanes] = jnp.where(low, pltpu.roll(rows[0], 64, 1), rows[1]).astype(BF16)


def mix_backward(count, zs, here, *refs):
    terms, (w_ref, out_ref, pair_ref, prod) = refs[:count], refs[count:]
    i, jc = pl.program_id(0), pl.program_id(1)
    per = w_ref.shape[2]
    modes = prod.shape[1] // (2 * zs)
    first = (i * pl.num_programs(1) + jc) * per

    @pl.when(first == 0)
    def _():
        grad = total(terms)
        sign = half_sign((modes, 128))
        low = low_half((modes, 128))
        for tile in range(zs // 2):
            lanes = slice(tile * 128, (tile + 1) * 128)
            real, imag = grad[:modes, lanes], grad[modes:, lanes]
            even = jnp.where(low, real, pltpu.roll(imag, 64, 1))
            odd = jnp.where(low, pltpu.roll(real, 64, 1), imag)
            for z, value in ((2 * tile, even), (2 * tile + 1, odd)):
                pair_ref[pl.ds(z, modes, stride=2 * zs), :] = value
                pair_ref[pl.ds(zs + z, modes, stride=2 * zs), :] = -sign * pltpu.roll(value, 64, 1)

    for mode in range(per):
        base = pl.multiple_of((first + mode) * 2 * zs, 2 * zs)
        left = pair_ref[pl.ds(base, 2 * zs), :].astype(BF16)
        got = dot_nt(left, w_ref[:, 0, mode].reshape(zs * 64, 128))
        for tile in range(zs // 2):
            prod[tile, pl.ds(base, 2 * zs), :] = got[:, tile * 128 : (tile + 1) * 128]

    @pl.when(first + per == modes)
    def _():
        low = low_half((modes, 128))
        for part in range(2):
            for tile in range(zs // 2):
                at = part * zs + 2 * tile
                even = prod[tile, pl.ds(at, modes, stride=2 * zs), :]
                odd = prod[tile, pl.ds(at + 1, modes, stride=2 * zs), :]
                out_ref[part * modes : (part + 1) * modes, tile * 128 : (tile + 1) * 128] = jnp.where(
                    low, even, odd
                ).astype(BF16)


def gram(zs, here, spread_ref, pair_ref, out_ref):
    i, jc = pl.program_id(0), pl.program_id(1)
    per = out_ref.shape[2]
    group = 4
    unit = 2 * zs
    first = (i * pl.num_programs(1) + jc) * per
    shape = (group * unit, 128)
    owner = lax.broadcasted_iota(jnp.int32, shape, 0) // unit
    for at in range(0, per, group):
        base = pl.multiple_of((first + at) * unit, group * unit)
        left = jnp.transpose(spread_ref[pl.ds(base, group * unit), :].astype(F32)).astype(BF16)
        grad = pair_ref[pl.ds(base, group * unit), :]
        right = jnp.concatenate([jnp.where(owner == t, grad, 0.0) for t in range(group)], 1)
        got = dot(left, right.astype(BF16))
        for t in range(group):
            out_ref[:, 0, at + t] = got[:, t * 128 : (t + 1) * 128].reshape(zs, 64, 128)


def grid_rows(here, blocks, x_ref, rows):
    chips = rows.shape[1]
    core, chip = here[0] % 2, here[0] // 2
    for slot, block in enumerate(blocks):
        at_core = core if slot < chips else 1 - core
        rows[at_core, chip ^ (slot % chips)] = dot(x_ref[0], block[...])


def row_at(rows, count, x):
    cores, chips, height, _ = rows.shape
    per = height // (pl.num_programs(0) * count)
    start = pl.multiple_of(pl.program_id(0) * (count * per), count * per)
    step = [rows[core, chip, pl.ds(start, count * per), :] for core in range(cores) for chip in range(chips)]
    joined = jnp.concatenate([value[x * per : (x + 1) * per] for value in step], 0)
    return jnp.transpose(joined).astype(BF16)


def middle(count, here, *refs):
    blocks, rest = refs[:count], refs[count:]
    x_ref, y_ref, mixing_ref, field_ref, cot_ref = rest[:5]
    out_ref, grad_ref, keep_ref, send_ref, rows = rest[5:]

    @pl.when(pl.program_id(0) == 0)
    def _():
        grid_rows(here, blocks, x_ref, rows)

    table = y_ref[...]
    mixing = mixing_ref[...]
    parts = []
    for x in range(field_ref.shape[0]):
        p = dot(row_at(rows, field_ref.shape[0], x), table) + dot(mixing, field_ref[x])
        square = p * p
        t = jnp.tanh(p * (ROOT + ROOT * CUBE * square))
        half = 0.5 + 0.5 * t
        out_ref[x] = (p * half).astype(BF16)
        slope = half + p * (1.0 - t * t) * (0.5 * ROOT + 1.5 * ROOT * CUBE * square)
        grad = (cot_ref[x].astype(F32) * slope).astype(BF16)
        grad_ref[x] = grad
        parts.append(dot_nt(table, grad))
    store_spectrum(here, parts, keep_ref, send_ref)


def local_sum(here, field_ref, grad_ref, out_ref, acc):
    step = pl.program_id(0)

    @pl.when(step == 0)
    def _():
        acc[...] = jnp.zeros_like(acc)

    got = dot_nt(field_ref[0], grad_ref[0])
    for x in range(1, field_ref.shape[0]):
        got += dot_nt(field_ref[x], grad_ref[x])
    acc[...] += got

    @pl.when(step == pl.num_programs(0) - 1)
    def _():
        value = acc[...]
        parts = [value[at : at + 64, at : at + 64] for at in range(0, value.shape[0], 64)]
        while len(parts) > 1:
            parts = [a + b for a, b in zip(parts[::2], parts[1::2])]
        out_ref[...] = parts[0]


def last(count, here, *refs):
    blocks, rest = refs[:count], refs[count:]
    x_ref, y_ref, mixing_ref, grad_ref, out_ref, rows = rest

    @pl.when(pl.program_id(0) == 0)
    def _():
        grid_rows(here, blocks, x_ref, rows)

    table = y_ref[...]
    mixing = mixing_ref[...]
    for x in range(grad_ref.shape[0]):
        value = dot(row_at(rows, grad_ref.shape[0], x), table) + dot(mixing, grad_ref[x])
        out_ref[x] = value.astype(BF16)


def flip(axis, size, bit):
    return functools.partial(lax.ppermute, axis_name=axis, perm=[(at, at ^ bit) for at in range(size)])


def exchange_sum(value, axis, size):
    parts = [value] + [flip(axis, size, bit)(value) for bit in range(1, size)]
    while len(parts) > 1:
        parts = [a + b for a, b in zip(parts[::2], parts[1::2])]
    return parts[0]


def body(features, out_grad, spectral_weight, local_weight):
    count = lax.axis_size("mp")
    dp_count = lax.axis_size("dp")
    chips = count // 2
    rows_here, grid_y, snaps, zs, channels = features.shape
    mode_rows = spectral_weight.shape[1]
    columns = snaps * zs * channels
    modes = mode_rows * KX
    unit = 2 * mode_rows
    here = lax.axis_index("mp").astype(jnp.int32).reshape(1)

    y_plain, y_weighted = y_tables(count)
    x_forward, x_back = x_tables(count)

    def inner(array):
        return jnp.transpose(array, (0, 2, 3, 4, 1)).reshape(rows_here, columns, grid_y)

    def outer(array):
        shaped = array.reshape(rows_here, snaps, zs, channels, grid_y)
        return jnp.transpose(shaped, (0, 4, 1, 2, 3))

    field, cot = inner(features), inner(out_grad)
    eye = jnp.eye(snaps * zs, dtype=BF16)
    mixing = jnp.kron(eye, local_weight)
    mixing_t = jnp.kron(eye, local_weight.T)

    chunk = 4
    steps = rows_here // chunk
    field_spec = pl.BlockSpec((chunk, columns, grid_y), lambda g, _: (g, 0, 0))
    field_shape = jax.ShapeDtypeStruct((rows_here, columns, grid_y), BF16)
    half_spec = pl.BlockSpec((chips, chunk * unit, columns), lambda g, _: (0, g, 0))
    half_shape = jax.ShapeDtypeStruct((chips, rows_here * unit, columns), BF16)
    y_spec = whole((2 * KY, grid_y))
    mode_shape = jax.ShapeDtypeStruct((2 * modes, columns), BF16)
    mode_spec = whole((2 * modes, columns))
    mixing_spec = whole((columns, columns))
    field_bytes = rows_here * columns * grid_y * 2
    mode_bytes = 4 * modes * columns

    def to_chips(keep, send):
        got = flip("mp", count, 1)(send)
        x_spec = (1, 2 * modes, rows_here * unit)
        outs = call(
            forward_x,
            here,
            (keep, got, x_forward, x_forward),
            (1,),
            [
                whole(keep.shape),
                whole(keep.shape),
                pl.BlockSpec(x_spec, lambda g, m: (m[0], 0, 0)),
                pl.BlockSpec(x_spec, lambda g, m: (m[0] ^ 1, 0, 0)),
            ],
            [mode_spec] * chips,
            [mode_shape] * chips,
            flops=8 * chips * modes * rows_here * unit * columns,
            moved=mode_bytes * 3 * chips,
            name="forward_x",
        )
        return [outs[0]] + [flip("mp", count, 2 * bit)(outs[bit]) for bit in range(1, chips)]

    def to_all(block):
        mine = [block] + [flip("mp", count, 2 * bit)(block) for bit in range(1, chips)]
        return mine + [flip("mp", count, 1)(value) for value in mine]

    per = 8
    mode_grid = (mode_rows, KX // per)
    weight_spec = pl.BlockSpec((zs, 1, per, channels, 2 * channels), lambda i, j, _: (0, i, j, 0, 0))
    spread_shape = (modes * 2 * zs, columns)
    pair_shape = (modes * 2 * zs, 2 * channels)
    weight_bytes = zs * modes * channels * 2 * channels * 2

    keep, send = call(
        forward_y,
        here,
        (field, y_plain),
        (steps,),
        [field_spec, y_spec],
        [half_spec] * 2,
        [half_shape] * 2,
        flops=field_bytes * 2 * KY,
        moved=field_bytes + mode_bytes * count,
        name="forward_y",
    )
    terms = to_chips(keep, send)
    mixed, spread = call(
        functools.partial(mix_forward, chips, zs),
        here,
        (*terms, spectral_weight),
        mode_grid,
        [mode_spec] * chips + [weight_spec],
        [mode_spec, whole(spread_shape)],
        [mode_shape, jax.ShapeDtypeStruct(spread_shape, BF16)],
        [pltpu.VMEM((2 * modes, columns), F32), pltpu.VMEM(pair_shape, F32)],
        flops=weight_bytes * 8,
        moved=weight_bytes + mode_bytes * chips,
        name="mix_forward",
    )
    blocks = to_all(mixed)
    x_back_spec = pl.BlockSpec((1, rows_here * unit, 2 * modes), lambda g, m: (m[0], 0, 0))
    rows_scratch = pltpu.VMEM((2, chips, rows_here * unit, columns), F32)
    output, preact_grad, keep, send = call(
        functools.partial(middle, count),
        here,
        (*blocks, x_back, y_weighted, mixing_t, field, cot),
        (steps,),
        [mode_spec] * count + [x_back_spec, y_spec, mixing_spec, field_spec, field_spec],
        [field_spec, field_spec, half_spec, half_spec],
        [field_shape, field_shape, half_shape, half_shape],
        [rows_scratch],
        flops=field_bytes * (4 * KY + columns),
        moved=field_bytes * 4 + mode_bytes * count * 2,
        name="middle",
    )
    terms = to_chips(keep, send)
    local_term = call(
        local_sum,
        here,
        (field, preact_grad),
        (steps,),
        [field_spec] * 2,
        whole((channels, channels)),
        jax.ShapeDtypeStruct((channels, channels), F32),
        [pltpu.VMEM((columns, columns), F32)],
        flops=field_bytes * columns,
        moved=field_bytes * 2,
        name="local_sum",
    )
    back, pairs = call(
        functools.partial(mix_backward, chips, zs),
        here,
        (*terms, spectral_weight),
        mode_grid,
        [mode_spec] * chips + [weight_spec],
        [mode_spec, whole(pair_shape)],
        [mode_shape, jax.ShapeDtypeStruct(pair_shape, F32)],
        [pltpu.VMEM((zs // 2, modes * 2 * zs, 128), F32)],
        flops=weight_bytes * 8,
        moved=weight_bytes + mode_bytes * chips,
        name="mix_backward",
    )
    blocks = to_all(back)
    spectral_grad = call(
        functools.partial(gram, zs),
        here,
        (spread, pairs),
        mode_grid,
        [whole(spread_shape), whole(pair_shape)],
        weight_spec,
        jax.ShapeDtypeStruct(spectral_weight.shape, F32),
        flops=weight_bytes * 8,
        moved=weight_bytes * 2,
        name="gram",
    )
    grad_scale = 1.0 / math.sqrt(NX * NY * snaps * dp_count * zs)
    local_grad = exchange_sum(exchange_sum(local_term, "mp", count), "dp", dp_count) * grad_scale
    back_field = call(
        functools.partial(last, count),
        here,
        (*blocks, x_back, y_plain, mixing, preact_grad),
        (steps,),
        [mode_spec] * count + [x_back_spec, y_spec, mixing_spec, field_spec],
        field_spec,
        field_shape,
        [rows_scratch],
        flops=field_bytes * (2 * KY + columns),
        moved=field_bytes * 2 + mode_bytes * count,
        name="last",
    )
    return (outer(output), outer(back_field), spectral_grad, local_grad)


def solution(mesh):
    placed = (
        P("mp", None, None, "dp", None),
        P("mp", None, None, "dp", None),
        P("dp", "mp", None, None, None),
        P(),
    )
    return jax.shard_map(
        body,
        mesh=mesh,
        in_specs=placed,
        out_specs=(
            P("mp", None, None, "dp", None),
            P("mp", None, None, "dp", None),
            P("dp", "mp", None, None, None),
            P(),
        ),
        check_vma=False,
    )
```

```python
import functools
import math

import jax
import jax.numpy as jnp
import ml_dtypes
import numpy as np
from jax import lax
from jax.experimental import pallas as pl
from jax.experimental.pallas import tpu as pltpu
from jax.sharding import PartitionSpec as P

NX = 256
NY = 256
KX = 32
KY = 32
F32 = jnp.float32
BF16 = jnp.bfloat16
ROOT = math.sqrt(2.0 / math.pi)
CUBE = 0.044715
VMEM = 52 << 20


def to_bf16(values):
    return values.astype(np.float32).astype(ml_dtypes.bfloat16)


def y_tables(count):
    block = KY // count
    k_index = np.arange(KY)
    angle = 2.0 * math.pi / NY * (k_index[:, None] * np.arange(NY)[None, :] % NY)
    table = to_bf16(np.stack([np.cos(angle), -np.sin(angle)]) / math.sqrt(NY)).astype(np.float32)
    weight = np.where(k_index == 0, 1.0, 2.0)[None, :, None]

    def ordered(values):
        shaped = values.reshape(2, count // 2, 2, block, NY).transpose(2, 1, 0, 3, 4)
        return to_bf16(shaped.reshape(2 * KY, NY))

    return ordered(table), ordered(table * weight)


def x_tables(count):
    block = KY // count
    rows = NX // count
    stored = np.arange(NX)
    x_index = stored % rows * count + stored // rows
    frequency = np.arange(KX) - KX // 2
    angle = 2.0 * math.pi / NX * (frequency[:, None] * x_index[None, :] % NX)
    cosine = np.cos(angle) / math.sqrt(NX)
    sine = np.sin(angle) / math.sqrt(NX)
    table = np.stack([np.stack([cosine, sine], 1), np.stack([-sine, cosine], 1)])
    per = table.reshape(2, KX, 2, count, rows).transpose(3, 0, 1, 4, 2)
    spread = np.einsum("nojxr,ab->noajxrb", per, np.eye(block))
    spread = to_bf16(spread.reshape(count, 2 * block * KX, rows * 2 * block))
    return spread, np.ascontiguousarray(spread.transpose(0, 2, 1))


def dot(left, right):
    return lax.dot_general(left, right, (((1,), (0,)), ((), ())), preferred_element_type=F32)


def dot_nt(left, right):
    return lax.dot_general(left, right, (((1,), (1,)), ((), ())), preferred_element_type=F32)


def streamed(ref, buffer, sem, at, steps, axis, size):
    def copy(step):
        where = [slice(None)] * axis + [pl.ds(step % (KX // size) * size, size)]
        where[1] = pl.ds(step // (KX // size), 1)
        return pltpu.make_async_copy(ref.at[tuple(where)], buffer.at[step], sem.at[step])

    @pl.when(at == 0)
    def _():
        for step in range(steps):
            copy(step).start()

    copy(at).wait()
    return buffer.at[at]


def whole(shape):
    zeros = (0,) * len(shape)
    return pl.BlockSpec(shape, lambda *_: zeros)


def call(kernel, here, operands, grid, in_specs, out_specs, out_shape, scratch=(), flops=0, moved=0, name=None, aliases=None):
    return pl.pallas_call(
        kernel,
        out_shape=out_shape,
        grid_spec=pltpu.PrefetchScalarGridSpec(
            num_scalar_prefetch=1,
            grid=grid,
            in_specs=in_specs,
            out_specs=out_specs,
            scratch_shapes=list(scratch),
        ),
        compiler_params=pltpu.CompilerParams(
            dimension_semantics=("arbitrary",) * len(grid), vmem_limit_bytes=VMEM
        ),
        cost_estimate=pl.CostEstimate(flops=flops, bytes_accessed=moved, transcendentals=0),
        name=name,
        input_output_aliases=aliases or {},
    )(here, *operands)


def store_spectrum(here, parts, keep_ref, send_ref):
    chips, width, _ = keep_ref.shape
    unit = width // len(parts)
    half = chips * unit
    own_first = here[0] % 2 == 0
    kept = [jnp.where(own_first, part[:half], part[half:]) for part in parts]
    sent = [jnp.where(own_first, part[half:], part[:half]) for part in parts]
    for chip in range(chips):
        rows = slice(chip * unit, (chip + 1) * unit)
        keep_ref[chip] = jnp.concatenate([part[rows] for part in kept], 0).astype(BF16)
        send_ref[chip] = jnp.concatenate([part[rows] for part in sent], 0).astype(BF16)


def forward_y(here, field_ref, table_ref, keep_ref, send_ref):
    table = table_ref[...]
    parts = [dot_nt(table, field_ref[x]) for x in range(field_ref.shape[0])]
    store_spectrum(here, parts, keep_ref, send_ref)


def forward_x(here, keep_ref, got_ref, own_ref, other_ref, *outs):
    chip = here[0] // 2
    for step, out in enumerate(outs):
        at = chip ^ step
        out[...] = (dot(own_ref[0], keep_ref[at]) + dot(other_ref[0], got_ref[at])).astype(BF16)


def total(refs):
    values = [ref[...].astype(F32) for ref in refs]
    while len(values) > 1:
        values = [a + b for a, b in zip(values[::2], values[1::2])]
    return values[0].astype(BF16).astype(F32)


def half_sign(shape):
    lane = lax.broadcasted_iota(jnp.int32, shape, 1)
    return jnp.where(lane % 128 < 64, -1.0, 1.0)


def low_half(shape):
    return lax.broadcasted_iota(jnp.int32, shape, 1) < 64


def mix_forward(count, zs, here, *refs):
    terms, (w_hbm, out_ref, spread_ref, coeff, prod, buffer, sem) = refs[:count], refs[count:]
    step = pl.program_id(0)
    per = buffer.shape[3]
    modes = coeff.shape[0] // 2
    first = step * per
    w_ref = streamed(w_hbm, buffer, sem, step, buffer.shape[0], 2, per)

    @pl.when(first == 0)
    def _():
        coeff[...] = total(terms)

    shape = (2 * zs, zs * 64)
    row = lax.broadcasted_iota(jnp.int32, shape, 0)
    keep = lax.broadcasted_iota(jnp.int32, shape, 1) // 64 == row % zs
    is_real = row < zs
    for pair in range(per // 2):
        lefts, weights = [], []
        for sub in range(2):
            at = first + 2 * pair + sub
            real = jnp.broadcast_to(coeff[pl.ds(at, 1), :], shape)
            imag = jnp.broadcast_to(coeff[pl.ds(modes + at, 1), :], shape)
            lefts.append(jnp.where(keep, jnp.where(is_real, real, imag), 0.0))
            weights.append(w_ref[:, 0, 2 * pair + sub].reshape(zs * 64, 128))
        left = jnp.concatenate(lefts, 0).astype(BF16)
        base = pl.multiple_of((first + 2 * pair) * 2 * zs, 4 * zs)
        spread_ref[pl.ds(base, 4 * zs), :] = left
        got = dot(left, jnp.concatenate(weights, 1))
        prod[pl.ds(base, 2 * zs), :] = got[: 2 * zs, :128]
        prod[pl.ds(base + 2 * zs, 2 * zs), :] = got[2 * zs :, 128:]

    @pl.when(first + per == modes)
    def _():
        sign = half_sign((modes, 128))
        low = low_half((modes, 128))
        for tile in range(zs // 2):
            rows = []
            for z in (2 * tile, 2 * tile + 1):
                real = prod[pl.ds(z, modes, stride=2 * zs), :]
                imag = prod[pl.ds(zs + z, modes, stride=2 * zs), :]
                rows.append(real + sign * pltpu.roll(imag, 64, 1))
            lanes = slice(tile * 128, (tile + 1) * 128)
            out_ref[:modes, lanes] = jnp.where(low, rows[0], pltpu.roll(rows[1], 64, 1)).astype(BF16)
            out_ref[modes:, lanes] = jnp.where(low, pltpu.roll(rows[0], 64, 1), rows[1]).astype(BF16)


def mix_backward(count, zs, here, *refs):
    terms, locals_ = refs[:count], refs[count:-6]
    w_hbm, out_ref, pair_ref, prod, buffer, sem = refs[-6:]
    step = pl.program_id(0)
    per = buffer.shape[3]
    modes = prod.shape[1] // (2 * zs)
    first = step * per
    w_ref = streamed(w_hbm, buffer, sem, step, buffer.shape[0], 2, per)

    @pl.when(first == 0)
    def _():
        parts = [ref[...] for ref in locals_]
        while len(parts) > 1:
            parts = [a + b for a, b in zip(parts[::2], parts[1::2])]
        extra = 64 // zs
        value = jnp.concatenate([parts[0][at * extra : (at + 1) * extra] for at in range(zs)], 1)
        coarse = value.astype(BF16)
        out_ref[2 * modes : 2 * modes + extra] = coarse
        out_ref[2 * modes + extra :] = (value - coarse.astype(F32)).astype(BF16)
        grad = total(terms)
        sign = half_sign((modes, 128))
        low = low_half((modes, 128))
        for tile in range(zs // 2):
            lanes = slice(tile * 128, (tile + 1) * 128)
            real, imag = grad[:modes, lanes], grad[modes:, lanes]
            even = jnp.where(low, real, pltpu.roll(imag, 64, 1))
            odd = jnp.where(low, pltpu.roll(real, 64, 1), imag)
            for z, value in ((2 * tile, even), (2 * tile + 1, odd)):
                pair_ref[pl.ds(z, modes, stride=2 * zs), :] = value
                pair_ref[pl.ds(zs + z, modes, stride=2 * zs), :] = -sign * pltpu.roll(value, 64, 1)

    for mode in range(per):
        base = pl.multiple_of((first + mode) * 2 * zs, 2 * zs)
        left = pair_ref[pl.ds(base, 2 * zs), :].astype(BF16)
        got = dot_nt(left, w_ref[:, 0, mode].reshape(zs * 64, 128))
        for tile in range(zs // 2):
            prod[tile, pl.ds(base, 2 * zs), :] = got[:, tile * 128 : (tile + 1) * 128]

    @pl.when(first + per == modes)
    def _():
        low = low_half((modes, 128))
        for part in range(2):
            for tile in range(zs // 2):
                at = part * zs + 2 * tile
                even = prod[tile, pl.ds(at, modes, stride=2 * zs), :]
                odd = prod[tile, pl.ds(at + 1, modes, stride=2 * zs), :]
                out_ref[part * modes : (part + 1) * modes, tile * 128 : (tile + 1) * 128] = jnp.where(
                    low, even, odd
                ).astype(BF16)


def gram(zs, start, here, spread_ref, pair_ref, *refs):
    out_ref = refs[-1]
    per = out_ref.shape[2]
    group = 4
    unit = 2 * zs
    first = (start + pl.program_id(0)) * per
    shape = (group * unit, 128)
    owner = lax.broadcasted_iota(jnp.int32, shape, 0) // unit
    for at in range(0, per, group):
        base = pl.multiple_of((first + at) * unit, group * unit)
        left = jnp.transpose(spread_ref[pl.ds(base, group * unit), :].astype(F32)).astype(BF16)
        grad = pair_ref[pl.ds(base, group * unit), :]
        right = jnp.concatenate([jnp.where(owner == t, grad, 0.0) for t in range(group)], 1)
        got = dot(left, right.astype(BF16))
        for t in range(group):
            out_ref[:, 0, at + t] = got[:, t * 128 : (t + 1) * 128].reshape(zs, 64, 128)


def grid_rows(here, blocks, x_ref, rows):
    chips = rows.shape[1]
    core, chip = here[0] % 2, here[0] // 2
    for slot, block in enumerate(blocks):
        at_core = core if slot < chips else 1 - core
        rows[at_core, chip ^ (slot % chips)] = dot(x_ref[0], block[...])


def row_at(rows, count, x):
    cores, chips, height, _ = rows.shape
    per = height // (pl.num_programs(0) * count)
    start = pl.multiple_of(pl.program_id(0) * (count * per), count * per)
    step = [rows[core, chip, pl.ds(start, count * per), :] for core in range(cores) for chip in range(chips)]
    joined = jnp.concatenate([value[x * per : (x + 1) * per] for value in step], 0)
    return jnp.transpose(joined).astype(BF16)


def block_mixing(weight, zs):
    rows = jnp.concatenate([weight] * zs, 1)
    full = jnp.concatenate([rows] * zs, 0)
    row = lax.broadcasted_iota(jnp.int32, full.shape, 0) // 64
    lane = lax.broadcasted_iota(jnp.int32, full.shape, 1) // 64
    return jnp.where(row == lane, full, 0.0).astype(BF16)


def middle(count, here, *refs):
    blocks, rest = refs[:count], refs[count:]
    x_ref, y_ref, weight_ref, field_ref, cot_ref = rest[:5]
    out_ref, grad_ref, keep_ref, send_ref, term_ref, rows, mixing, acc = rest[5:]
    step = pl.program_id(0)
    size = field_ref.shape[0]
    columns = field_ref.shape[1]
    zs = columns // 64

    @pl.when(step == 0)
    def _():
        grid_rows(here, blocks, x_ref, rows)
        mixing[...] = block_mixing(jnp.transpose(weight_ref[...].astype(F32)), zs)
        acc[...] = jnp.zeros_like(acc)

    table = y_ref[...]
    lefts = [row_at(rows, size, x) for x in range(size)]
    low = low_half((64, 128))
    parts, sums = [], []

    def reduce(x):
        got = dot_nt(jnp.concatenate([table, field_ref[x]], 0), grad_ref[x])
        parts.append(got[: 2 * KY])
        for tile in range(zs // 2):
            lanes = slice(tile * 128, (tile + 1) * 128)
            at = 2 * KY + tile * 128
            sums.append((lanes, jnp.where(low, got[at : at + 64, lanes], got[at + 64 : at + 128, lanes])))

    for x in range(size):
        for at in range(0, columns, 64):
            part = slice(at, at + 64)
            p = dot(lefts[x][part], table) + dot(mixing[part, :], field_ref[x])
            square = p * p
            t = jnp.tanh(p * (ROOT + ROOT * CUBE * square))
            half = 0.5 + 0.5 * t
            out_ref[x, part] = (p * half).astype(BF16)
            slope = half + p * (1.0 - t * t) * (0.5 * ROOT + 1.5 * ROOT * CUBE * square)
            grad_ref[x, part] = (cot_ref[x, part].astype(F32) * slope).astype(BF16)
        if x:
            reduce(x - 1)
    reduce(size - 1)
    store_spectrum(here, parts, keep_ref, send_ref)
    for lanes, value in sums:
        acc[:, lanes] += value

    @pl.when(step == pl.num_programs(0) - 1)
    def _():
        value = acc[...]
        parts = [value[:, at : at + 64] for at in range(0, columns, 64)]
        while len(parts) > 1:
            parts = [a + b for a, b in zip(parts[::2], parts[1::2])]
        term_ref[...] = parts[0]


def last(count, scale, here, *refs):
    blocks, rest = refs[:count], refs[count:]
    x_ref, y_ref, weight_ref, grad_ref, out_ref, local_ref, rows, mixing = rest
    columns = grad_ref.shape[1]
    size = grad_ref.shape[0]

    @pl.when(pl.program_id(0) == 0)
    def _():
        height = x_ref.shape[2]
        extra = 64 * 64 // columns
        grid_rows(here, [block.at[pl.ds(0, height)] for block in blocks], x_ref, rows)
        mixing[...] = block_mixing(weight_ref[...].astype(F32), columns // 64)
        parts = [
            block[pl.ds(height, extra), :].astype(F32) + block[pl.ds(height + extra, extra), :].astype(F32)
            for block in blocks
        ]
        while len(parts) > 1:
            parts = [a + b for a, b in zip(parts[::2], parts[1::2])]
        for at in range(columns // 64):
            local_ref[at * extra : (at + 1) * extra, :] = parts[0][:, at * 64 : (at + 1) * 64] * scale

    table = y_ref[...]
    lefts = [row_at(rows, size, x) for x in range(size)]
    for x in range(size):
        for at in range(0, columns, 64):
            part = slice(at, at + 64)
            value = dot(lefts[x][part], table) + dot(mixing[part, :], grad_ref[x])
            out_ref[x, part] = value.astype(BF16)


def flip(axis, size, bit):
    return functools.partial(lax.ppermute, axis_name=axis, perm=[(at, at ^ bit) for at in range(size)])


def body(features, out_grad, spectral_weight, local_weight):
    count = lax.axis_size("mp")
    dp_count = lax.axis_size("dp")
    chips = count // 2
    rows_here, grid_y, snaps, zs, channels = features.shape
    mode_rows = spectral_weight.shape[1]
    columns = snaps * zs * channels
    modes = mode_rows * KX
    unit = 2 * mode_rows
    here = lax.axis_index("mp").astype(jnp.int32).reshape(1)

    y_plain, y_weighted = y_tables(count)
    x_forward, x_back = x_tables(count)

    def inner(array):
        return jnp.transpose(array, (0, 2, 3, 4, 1)).reshape(rows_here, columns, grid_y)

    def outer(array):
        shaped = array.reshape(rows_here, snaps, zs, channels, grid_y)
        return jnp.transpose(shaped, (0, 4, 1, 2, 3))

    field, cot = inner(features), inner(out_grad)
    wide, chunk = min(16, rows_here), min(8, rows_here)

    def field_spec(size):
        return pl.BlockSpec((size, columns, grid_y), lambda g, _: (g, 0, 0))

    def half_spec(size):
        return pl.BlockSpec((chips, size * unit, columns), lambda g, _: (0, g, 0))

    field_shape = jax.ShapeDtypeStruct((rows_here, columns, grid_y), BF16)
    half_shape = jax.ShapeDtypeStruct((chips, rows_here * unit, columns), BF16)
    y_spec = whole((2 * KY, grid_y))
    mode_shape = jax.ShapeDtypeStruct((2 * modes, columns), BF16)
    mode_spec = whole((2 * modes, columns))
    weight_small = whole((channels, channels))
    small_shape = jax.ShapeDtypeStruct((channels, channels), F32)
    mixing_scratch = pltpu.VMEM((columns, columns), BF16)
    extra = 2 * channels * channels // columns
    back_spec = whole((2 * modes + extra, columns))
    back_shape = jax.ShapeDtypeStruct((2 * modes + extra, columns), BF16)
    field_bytes = rows_here * columns * grid_y * 2
    mode_bytes = 4 * modes * columns

    def to_chips(keep, send):
        got = flip("mp", count, 1)(send)
        x_spec = (1, 2 * modes, rows_here * unit)
        outs = call(
            forward_x,
            here,
            (keep, got, x_forward, x_forward),
            (1,),
            [
                whole(keep.shape),
                whole(keep.shape),
                pl.BlockSpec(x_spec, lambda g, m: (m[0], 0, 0)),
                pl.BlockSpec(x_spec, lambda g, m: (m[0] ^ 1, 0, 0)),
            ],
            [mode_spec] * chips,
            [mode_shape] * chips,
            flops=8 * chips * modes * rows_here * unit * columns,
            moved=mode_bytes * 3 * chips,
            name="forward_x",
        )
        return [outs[0]] + [flip("mp", count, 2 * bit)(outs[bit]) for bit in range(1, chips)]

    def to_all(block):
        mine = [block] + [flip("mp", count, 2 * bit)(block) for bit in range(1, chips)]
        return mine + [flip("mp", count, 1)(value) for value in mine]

    per = 16
    mode_steps = modes // per
    weight_spec = pl.BlockSpec(memory_space=pl.ANY)
    weight_scratch = [
        pltpu.VMEM((mode_steps, zs, 1, per, channels, 2 * channels), BF16),
        pltpu.SemaphoreType.DMA((mode_steps,)),
    ]
    spread_shape = (modes * 2 * zs, columns)
    pair_shape = (modes * 2 * zs, 2 * channels)
    weight_bytes = zs * modes * channels * 2 * channels * 2

    keep, send = call(
        forward_y,
        here,
        (field, y_plain),
        (rows_here // wide,),
        [field_spec(wide), y_spec],
        [half_spec(wide)] * 2,
        [half_shape] * 2,
        flops=field_bytes * 2 * KY,
        moved=field_bytes + mode_bytes * count,
        name="forward_y",
    )
    terms = to_chips(keep, send)
    mixed, spread = call(
        functools.partial(mix_forward, chips, zs),
        here,
        (*terms, spectral_weight),
        (mode_steps,),
        [mode_spec] * chips + [weight_spec],
        [mode_spec, whole(spread_shape)],
        [mode_shape, jax.ShapeDtypeStruct(spread_shape, BF16)],
        [pltpu.VMEM((2 * modes, columns), F32), pltpu.VMEM(pair_shape, F32)] + weight_scratch,
        flops=weight_bytes * 8,
        moved=weight_bytes + mode_bytes * chips,
        name="mix_forward",
    )
    blocks = to_all(mixed)
    x_back_spec = pl.BlockSpec((1, rows_here * unit, 2 * modes), lambda g, m: (m[0], 0, 0))
    rows_scratch = pltpu.VMEM((2, chips, rows_here * unit, columns), F32)
    output, preact_grad, keep, send, local_term = call(
        functools.partial(middle, count),
        here,
        (*blocks, x_back, y_weighted, local_weight, field, cot),
        (rows_here // chunk,),
        [mode_spec] * count + [x_back_spec, y_spec, weight_small] + [field_spec(chunk)] * 2,
        [field_spec(chunk)] * 2 + [half_spec(chunk)] * 2 + [weight_small],
        [field_shape, field_shape, half_shape, half_shape, small_shape],
        [rows_scratch, mixing_scratch, pltpu.VMEM((channels, columns), F32)],
        flops=field_bytes * (4 * KY + 2 * columns),
        moved=field_bytes * 4 + mode_bytes * count * 2,
        name="middle",
    )
    terms = to_chips(keep, send)
    locals_ = [local_term] + [flip("dp", dp_count, bit)(local_term) for bit in range(1, dp_count)]
    back, pairs = call(
        functools.partial(mix_backward, chips, zs),
        here,
        (*terms, *locals_, spectral_weight),
        (mode_steps,),
        [mode_spec] * chips + [weight_small] * dp_count + [weight_spec],
        [back_spec, whole(pair_shape)],
        [back_shape, jax.ShapeDtypeStruct(pair_shape, F32)],
        [pltpu.VMEM((zs // 2, modes * 2 * zs, 128), F32)] + weight_scratch,
        flops=weight_bytes * 8,
        moved=weight_bytes + mode_bytes * chips,
        name="mix_backward",
    )
    def gram_part(start, size, before):
        spec = pl.BlockSpec((zs, 1, KX, channels, 2 * channels), lambda g, _: (0, g + start, 0, 0, 0))
        return call(
            functools.partial(gram, zs, start),
            here,
            (spread, pairs, *before),
            (size,),
            [whole(spread_shape), whole(pair_shape)] + [pl.BlockSpec(memory_space=pl.ANY)] * len(before),
            spec,
            jax.ShapeDtypeStruct(spectral_weight.shape, F32),
            flops=weight_bytes * 4,
            moved=weight_bytes,
            name="gram",
            aliases={3: 0} if before else {},
        )

    mine = [back] + [flip("mp", count, 2 * bit)(back) for bit in range(1, chips)]
    spectral_grad = gram_part(0, mode_rows // 2, ())
    *others, spectral_grad = lax.optimization_barrier((*mine[1:], spectral_grad))
    blocks = [back, *others] + [flip("mp", count, 1)(value) for value in (back, *others)]
    spectral_grad = gram_part(mode_rows // 2, mode_rows - mode_rows // 2, (spectral_grad,))
    scale = 1.0 / math.sqrt(NX * NY * snaps * dp_count * zs)
    back_field, local_grad = call(
        functools.partial(last, count, scale),
        here,
        (*blocks, x_back, y_plain, local_weight, preact_grad),
        (rows_here // wide,),
        [back_spec] * count + [x_back_spec, y_spec, weight_small, field_spec(wide)],
        [field_spec(wide), weight_small],
        [field_shape, small_shape],
        [rows_scratch, mixing_scratch],
        flops=field_bytes * (2 * KY + columns),
        moved=field_bytes * 2 + mode_bytes * count,
        name="last",
    )
    return (outer(output), outer(back_field), spectral_grad, local_grad)


def solution(mesh):
    placed = (
        P("mp", None, None, "dp", None),
        P("mp", None, None, "dp", None),
        P("dp", "mp", None, None, None),
        P(),
    )
    return jax.shard_map(
        body,
        mesh=mesh,
        in_specs=placed,
        out_specs=(
            P("mp", None, None, "dp", None),
            P("mp", None, None, "dp", None),
            P("dp", "mp", None, None, None),
            P(),
        ),
        check_vma=False,
    )
```

```python
import functools
import math

import jax
import jax.numpy as jnp
import ml_dtypes
import numpy as np
from jax import lax
from jax.experimental import pallas as pl
from jax.experimental.pallas import tpu as pltpu
from jax.sharding import PartitionSpec as P

NX = 256
NY = 256
KX = 32
KY = 32
F32 = jnp.float32
BF16 = jnp.bfloat16
ROOT = math.sqrt(2.0 / math.pi)
CUBE = 0.044715
VMEM = 52 << 20


def to_bf16(values):
    return values.astype(np.float32).astype(ml_dtypes.bfloat16)


def y_tables(count):
    block = KY // count
    k_index = np.arange(KY)
    angle = 2.0 * math.pi / NY * (k_index[:, None] * np.arange(NY)[None, :] % NY)
    table = to_bf16(np.stack([np.cos(angle), -np.sin(angle)]) / math.sqrt(NY)).astype(np.float32)
    weight = np.where(k_index == 0, 1.0, 2.0)[None, :, None]

    def ordered(values):
        shaped = values.reshape(2, count // 2, 2, block, NY).transpose(2, 1, 0, 3, 4)
        return to_bf16(shaped.reshape(2 * KY, NY))

    return ordered(table), ordered(table * weight)


def x_tables(count):
    block = KY // count
    rows = NX // count
    stored = np.arange(NX)
    x_index = stored % rows * count + stored // rows
    frequency = np.arange(KX) - KX // 2
    angle = 2.0 * math.pi / NX * (frequency[:, None] * x_index[None, :] % NX)
    cosine = np.cos(angle) / math.sqrt(NX)
    sine = np.sin(angle) / math.sqrt(NX)
    table = np.stack([np.stack([cosine, sine], 1), np.stack([-sine, cosine], 1)])
    per = table.reshape(2, KX, 2, count, rows).transpose(3, 0, 1, 4, 2)
    spread = np.einsum("nojxr,ab->noajxrb", per, np.eye(block))
    spread = to_bf16(spread.reshape(count, 2 * block * KX, rows * 2 * block))
    return spread, np.ascontiguousarray(spread.transpose(0, 2, 1))


def dot(left, right):
    return lax.dot_general(left, right, (((1,), (0,)), ((), ())), preferred_element_type=F32)


def dot_nt(left, right):
    return lax.dot_general(left, right, (((1,), (1,)), ((), ())), preferred_element_type=F32)


def streamed(ref, buffer, sem, at, steps, axis, size):
    def copy(step):
        where = [slice(None)] * axis + [pl.ds(step % (KX // size) * size, size)]
        where[1] = pl.ds(step // (KX // size), 1)
        return pltpu.make_async_copy(ref.at[tuple(where)], buffer.at[step], sem.at[step])

    @pl.when(at == 0)
    def _():
        for step in range(steps):
            copy(step).start()

    copy(at).wait()
    return buffer.at[at]


def whole(shape):
    zeros = (0,) * len(shape)
    return pl.BlockSpec(shape, lambda *_: zeros)


def call(kernel, here, operands, grid, in_specs, out_specs, out_shape, scratch=(), flops=0, moved=0, name=None, aliases=None, limit=VMEM):
    return pl.pallas_call(
        kernel,
        out_shape=out_shape,
        grid_spec=pltpu.PrefetchScalarGridSpec(
            num_scalar_prefetch=1,
            grid=grid,
            in_specs=in_specs,
            out_specs=out_specs,
            scratch_shapes=list(scratch),
        ),
        compiler_params=pltpu.CompilerParams(
            dimension_semantics=("arbitrary",) * len(grid), vmem_limit_bytes=limit
        ),
        cost_estimate=pl.CostEstimate(flops=flops, bytes_accessed=moved, transcendentals=0),
        name=name,
        input_output_aliases=aliases or {},
    )(here, *operands)


def store_spectrum(here, parts, keep_ref, send_ref):
    chips, width, _ = keep_ref.shape
    unit = width // len(parts)
    half = chips * unit
    own_first = here[0] % 2 == 0
    kept = [jnp.where(own_first, part[:half], part[half:]) for part in parts]
    sent = [jnp.where(own_first, part[half:], part[:half]) for part in parts]
    for chip in range(chips):
        rows = slice(chip * unit, (chip + 1) * unit)
        keep_ref[chip] = jnp.concatenate([part[rows] for part in kept], 0).astype(BF16)
        send_ref[chip] = jnp.concatenate([part[rows] for part in sent], 0).astype(BF16)


def forward_y(here, field_ref, table_ref, keep_ref, send_ref):
    table = table_ref[...]
    parts = [dot_nt(table, field_ref[x]) for x in range(field_ref.shape[0])]
    store_spectrum(here, parts, keep_ref, send_ref)


def forward_x(here, keep_ref, got_ref, own_ref, other_ref, *outs):
    chip = here[0] // 2
    for step, out in enumerate(outs):
        at = chip ^ step
        out[...] = (dot(own_ref[0], keep_ref[at]) + dot(other_ref[0], got_ref[at])).astype(BF16)


def total(refs):
    values = [ref[...].astype(F32) for ref in refs]
    while len(values) > 1:
        values = [a + b for a, b in zip(values[::2], values[1::2])]
    return values[0].astype(BF16).astype(F32)


def half_sign(shape):
    lane = lax.broadcasted_iota(jnp.int32, shape, 1)
    return jnp.where(lane % 128 < 64, -1.0, 1.0)


def low_half(shape):
    return lax.broadcasted_iota(jnp.int32, shape, 1) < 64


def mix_forward(count, zs, here, *refs):
    terms, (w_hbm, out_ref, spread_ref, coeff, prod, buffer, sem) = refs[:count], refs[count:]
    step = pl.program_id(0)
    per = buffer.shape[3]
    modes = coeff.shape[0] // 2
    first = step * per
    w_ref = streamed(w_hbm, buffer, sem, step, buffer.shape[0], 2, per)

    @pl.when(first == 0)
    def _():
        coeff[...] = total(terms)

    shape = (2 * zs, zs * 64)
    row = lax.broadcasted_iota(jnp.int32, shape, 0)
    keep = lax.broadcasted_iota(jnp.int32, shape, 1) // 64 == row % zs
    is_real = row < zs
    for pair in range(per // 2):
        lefts, weights = [], []
        for sub in range(2):
            at = first + 2 * pair + sub
            real = jnp.broadcast_to(coeff[pl.ds(at, 1), :], shape)
            imag = jnp.broadcast_to(coeff[pl.ds(modes + at, 1), :], shape)
            lefts.append(jnp.where(keep, jnp.where(is_real, real, imag), 0.0))
            weights.append(w_ref[:, 0, 2 * pair + sub].reshape(zs * 64, 128))
        left = jnp.concatenate(lefts, 0).astype(BF16)
        base = pl.multiple_of((first + 2 * pair) * 2 * zs, 4 * zs)
        spread_ref[pl.ds(base, 4 * zs), :] = left
        got = dot(left, jnp.concatenate(weights, 1))
        prod[pl.ds(base, 2 * zs), :] = got[: 2 * zs, :128]
        prod[pl.ds(base + 2 * zs, 2 * zs), :] = got[2 * zs :, 128:]

    @pl.when(first + per == modes)
    def _():
        sign = half_sign((modes, 128))
        low = low_half((modes, 128))
        for tile in range(zs // 2):
            rows = []
            for z in (2 * tile, 2 * tile + 1):
                real = prod[pl.ds(z, modes, stride=2 * zs), :]
                imag = prod[pl.ds(zs + z, modes, stride=2 * zs), :]
                rows.append(real + sign * pltpu.roll(imag, 64, 1))
            lanes = slice(tile * 128, (tile + 1) * 128)
            out_ref[:modes, lanes] = jnp.where(low, rows[0], pltpu.roll(rows[1], 64, 1)).astype(BF16)
            out_ref[modes:, lanes] = jnp.where(low, pltpu.roll(rows[0], 64, 1), rows[1]).astype(BF16)


def mix_backward(count, zs, here, *refs):
    terms, locals_ = refs[:count], refs[count:-6]
    w_hbm, out_ref, pair_ref, prod, buffer, sem = refs[-6:]
    step = pl.program_id(0)
    per = buffer.shape[3]
    modes = prod.shape[1] // (2 * zs)
    first = step * per
    w_ref = streamed(w_hbm, buffer, sem, step, buffer.shape[0], 2, per)

    @pl.when(first == 0)
    def _():
        parts = [ref[...] for ref in locals_]
        while len(parts) > 1:
            parts = [a + b for a, b in zip(parts[::2], parts[1::2])]
        extra = 64 // zs
        value = jnp.concatenate([parts[0][at * extra : (at + 1) * extra] for at in range(zs)], 1)
        coarse = value.astype(BF16)
        out_ref[2 * modes : 2 * modes + extra] = coarse
        out_ref[2 * modes + extra :] = (value - coarse.astype(F32)).astype(BF16)
        grad = total(terms)
        sign = half_sign((modes, 128))
        low = low_half((modes, 128))
        for tile in range(zs // 2):
            lanes = slice(tile * 128, (tile + 1) * 128)
            real, imag = grad[:modes, lanes], grad[modes:, lanes]
            even = jnp.where(low, real, pltpu.roll(imag, 64, 1))
            odd = jnp.where(low, pltpu.roll(real, 64, 1), imag)
            for z, value in ((2 * tile, even), (2 * tile + 1, odd)):
                pair_ref[pl.ds(z, modes, stride=2 * zs), :] = value
                pair_ref[pl.ds(zs + z, modes, stride=2 * zs), :] = -sign * pltpu.roll(value, 64, 1)

    for mode in range(per):
        base = pl.multiple_of((first + mode) * 2 * zs, 2 * zs)
        left = pair_ref[pl.ds(base, 2 * zs), :].astype(BF16)
        got = dot_nt(left, w_ref[:, 0, mode].reshape(zs * 64, 128))
        for tile in range(zs // 2):
            prod[tile, pl.ds(base, 2 * zs), :] = got[:, tile * 128 : (tile + 1) * 128]

    @pl.when(first + per == modes)
    def _():
        low = low_half((modes, 128))
        for part in range(2):
            for tile in range(zs // 2):
                at = part * zs + 2 * tile
                even = prod[tile, pl.ds(at, modes, stride=2 * zs), :]
                odd = prod[tile, pl.ds(at + 1, modes, stride=2 * zs), :]
                out_ref[part * modes : (part + 1) * modes, tile * 128 : (tile + 1) * 128] = jnp.where(
                    low, even, odd
                ).astype(BF16)


def gram(zs, start, here, spread_ref, pair_ref, *refs):
    out_ref = refs[-1]
    per = out_ref.shape[2]
    group = 4
    unit = 2 * zs
    first = (start + pl.program_id(0)) * per
    shape = (group * unit, 128)
    owner = lax.broadcasted_iota(jnp.int32, shape, 0) // unit
    for at in range(0, per, group):
        base = pl.multiple_of((first + at) * unit, group * unit)
        left = jnp.transpose(spread_ref[pl.ds(base, group * unit), :].astype(F32)).astype(BF16)
        grad = pair_ref[pl.ds(base, group * unit), :]
        right = jnp.concatenate([jnp.where(owner == t, grad, 0.0) for t in range(group)], 1)
        got = dot(left, right.astype(BF16))
        for t in range(group):
            out_ref[:, 0, at + t] = got[:, t * 128 : (t + 1) * 128].reshape(zs, 64, 128)


def grid_rows(here, blocks, x_ref, rows):
    chips = rows.shape[1]
    core, chip = here[0] % 2, here[0] // 2
    for slot, block in enumerate(blocks):
        at_core = core if slot < chips else 1 - core
        rows[at_core, chip ^ (slot % chips)] = dot(x_ref[0], block[...])


def row_at(rows, count, x):
    cores, chips, height, _ = rows.shape
    per = height // (pl.num_programs(0) * count)
    start = pl.multiple_of(pl.program_id(0) * (count * per), count * per)
    step = [rows[core, chip, pl.ds(start, count * per), :] for core in range(cores) for chip in range(chips)]
    joined = jnp.concatenate([value[x * per : (x + 1) * per] for value in step], 0)
    return jnp.transpose(joined).astype(BF16)


def middle(count, here, *refs):
    blocks, rest = refs[:count], refs[count:]
    x_ref, y_ref, weight_ref, field_ref, cot_ref = rest[:5]
    out_ref, grad_ref, keep_ref, send_ref, term_ref, rows, mixing, acc = rest[5:]
    step = pl.program_id(0)
    size = field_ref.shape[0]
    columns = field_ref.shape[1]
    zs = columns // 64

    @pl.when(step == 0)
    def _():
        grid_rows(here, blocks, x_ref, rows)
        mixing[...] = jnp.transpose(weight_ref[...].astype(F32)).astype(BF16)
        acc[...] = jnp.zeros_like(acc)

    table = y_ref[...]
    lefts = [row_at(rows, size, x) for x in range(size)]
    low = low_half((64, 128))
    parts, sums = [], []

    def reduce(x):
        got = dot_nt(jnp.concatenate([table, field_ref[x]], 0), grad_ref[x])
        parts.append(got[: 2 * KY])
        for tile in range(zs // 2):
            lanes = slice(tile * 128, (tile + 1) * 128)
            at = 2 * KY + tile * 128
            sums.append((lanes, jnp.where(low, got[at : at + 64, lanes], got[at + 64 : at + 128, lanes])))

    for x in range(size):
        for at in range(0, columns, 64):
            part = slice(at, at + 64)
            p = dot(lefts[x][part], table) + dot(mixing[...], field_ref[x, part])
            square = p * p
            t = jnp.tanh(p * (ROOT + ROOT * CUBE * square))
            half = 0.5 + 0.5 * t
            out_ref[x, part] = (p * half).astype(BF16)
            slope = half + p * (1.0 - t * t) * (0.5 * ROOT + 1.5 * ROOT * CUBE * square)
            grad_ref[x, part] = (cot_ref[x, part].astype(F32) * slope).astype(BF16)
        if x:
            reduce(x - 1)
    reduce(size - 1)
    store_spectrum(here, parts, keep_ref, send_ref)
    for lanes, value in sums:
        acc[:, lanes] += value

    @pl.when(step == pl.num_programs(0) - 1)
    def _():
        value = acc[...]
        parts = [value[:, at : at + 64] for at in range(0, columns, 64)]
        while len(parts) > 1:
            parts = [a + b for a, b in zip(parts[::2], parts[1::2])]
        term_ref[...] = parts[0]


def last(count, scale, here, *refs):
    blocks, rest = refs[:count], refs[count:]
    x_ref, y_ref, weight_ref, grad_ref, out_ref, local_ref, rows = rest
    columns = grad_ref.shape[1]
    size = grad_ref.shape[0]

    @pl.when(pl.program_id(0) == 0)
    def _():
        height = x_ref.shape[2]
        extra = 64 * 64 // columns
        grid_rows(here, [block.at[pl.ds(0, height)] for block in blocks], x_ref, rows)
        parts = [
            block[pl.ds(height, extra), :].astype(F32) + block[pl.ds(height + extra, extra), :].astype(F32)
            for block in blocks
        ]
        while len(parts) > 1:
            parts = [a + b for a, b in zip(parts[::2], parts[1::2])]
        for at in range(columns // 64):
            local_ref[at * extra : (at + 1) * extra, :] = parts[0][:, at * 64 : (at + 1) * 64] * scale

    table = y_ref[...]
    weight = weight_ref[...]
    lefts = [row_at(rows, size, x) for x in range(size)]
    for x in range(size):
        for at in range(0, columns, 64):
            part = slice(at, at + 64)
            value = dot(lefts[x][part], table) + dot(weight, grad_ref[x, part])
            out_ref[x, part] = value.astype(BF16)


def flip(axis, size, bit):
    return functools.partial(lax.ppermute, axis_name=axis, perm=[(at, at ^ bit) for at in range(size)])


def body(features, out_grad, spectral_weight, local_weight):
    count = lax.axis_size("mp")
    dp_count = lax.axis_size("dp")
    chips = count // 2
    rows_here, grid_y, snaps, zs, channels = features.shape
    mode_rows = spectral_weight.shape[1]
    columns = snaps * zs * channels
    modes = mode_rows * KX
    unit = 2 * mode_rows
    here = lax.axis_index("mp").astype(jnp.int32).reshape(1)

    y_plain, y_weighted = y_tables(count)
    x_forward, x_back = x_tables(count)

    def inner(array):
        return jnp.transpose(array, (0, 2, 3, 4, 1)).reshape(rows_here, columns, grid_y)

    def outer(array):
        shaped = array.reshape(rows_here, snaps, zs, channels, grid_y)
        return jnp.transpose(shaped, (0, 4, 1, 2, 3))

    field, cot = inner(features), inner(out_grad)
    wide, chunk = min(16, rows_here), min(8, rows_here)

    def field_spec(size):
        return pl.BlockSpec((size, columns, grid_y), lambda g, _: (g, 0, 0))

    def half_spec(size):
        return pl.BlockSpec((chips, size * unit, columns), lambda g, _: (0, g, 0))

    field_shape = jax.ShapeDtypeStruct((rows_here, columns, grid_y), BF16)
    half_shape = jax.ShapeDtypeStruct((chips, rows_here * unit, columns), BF16)
    y_spec = whole((2 * KY, grid_y))
    mode_shape = jax.ShapeDtypeStruct((2 * modes, columns), BF16)
    mode_spec = whole((2 * modes, columns))
    weight_small = whole((channels, channels))
    small_shape = jax.ShapeDtypeStruct((channels, channels), F32)
    mixing_scratch = pltpu.VMEM((channels, channels), BF16)
    extra = 2 * channels * channels // columns
    back_spec = whole((2 * modes + extra, columns))
    back_shape = jax.ShapeDtypeStruct((2 * modes + extra, columns), BF16)
    field_bytes = rows_here * columns * grid_y * 2
    mode_bytes = 4 * modes * columns

    def to_chips(keep, send):
        got = flip("mp", count, 1)(send)
        x_spec = (1, 2 * modes, rows_here * unit)
        outs = call(
            forward_x,
            here,
            (keep, got, x_forward, x_forward),
            (1,),
            [
                whole(keep.shape),
                whole(keep.shape),
                pl.BlockSpec(x_spec, lambda g, m: (m[0], 0, 0)),
                pl.BlockSpec(x_spec, lambda g, m: (m[0] ^ 1, 0, 0)),
            ],
            [mode_spec] * chips,
            [mode_shape] * chips,
            flops=8 * chips * modes * rows_here * unit * columns,
            moved=mode_bytes * 3 * chips,
            name="forward_x",
            limit=8 << 20,
        )
        return [outs[0]] + [flip("mp", count, 2 * bit)(outs[bit]) for bit in range(1, chips)]

    def to_all(block):
        mine = [block] + [flip("mp", count, 2 * bit)(block) for bit in range(1, chips)]
        return mine + [flip("mp", count, 1)(value) for value in mine]

    per = 16
    mode_steps = modes // per
    weight_spec = pl.BlockSpec(memory_space=pl.ANY)
    weight_scratch = [
        pltpu.VMEM((mode_steps, zs, 1, per, channels, 2 * channels), BF16),
        pltpu.SemaphoreType.DMA((mode_steps,)),
    ]
    spread_shape = (modes * 2 * zs, columns)
    pair_shape = (modes * 2 * zs, 2 * channels)
    weight_bytes = zs * modes * channels * 2 * channels * 2

    keep, send = call(
        forward_y,
        here,
        (field, y_plain),
        (rows_here // wide,),
        [field_spec(wide), y_spec],
        [half_spec(wide)] * 2,
        [half_shape] * 2,
        flops=field_bytes * 2 * KY,
        moved=field_bytes + mode_bytes * count,
        name="forward_y",
    )
    terms = to_chips(keep, send)
    mixed, spread = call(
        functools.partial(mix_forward, chips, zs),
        here,
        (*terms, spectral_weight),
        (mode_steps,),
        [mode_spec] * chips + [weight_spec],
        [mode_spec, whole(spread_shape)],
        [mode_shape, jax.ShapeDtypeStruct(spread_shape, BF16)],
        [pltpu.VMEM((2 * modes, columns), F32), pltpu.VMEM(pair_shape, F32)] + weight_scratch,
        flops=weight_bytes * 8,
        moved=weight_bytes + mode_bytes * chips,
        name="mix_forward",
    )
    blocks = to_all(mixed)
    x_back_spec = pl.BlockSpec((1, rows_here * unit, 2 * modes), lambda g, m: (m[0], 0, 0))
    rows_scratch = pltpu.VMEM((2, chips, rows_here * unit, columns), F32)
    output, preact_grad, keep, send, local_term = call(
        functools.partial(middle, count),
        here,
        (*blocks, x_back, y_weighted, local_weight, field, cot),
        (rows_here // chunk,),
        [mode_spec] * count + [x_back_spec, y_spec, weight_small] + [field_spec(chunk)] * 2,
        [field_spec(chunk)] * 2 + [half_spec(chunk)] * 2 + [weight_small],
        [field_shape, field_shape, half_shape, half_shape, small_shape],
        [rows_scratch, mixing_scratch, pltpu.VMEM((channels, columns), F32)],
        flops=field_bytes * (4 * KY + 2 * columns),
        moved=field_bytes * 4 + mode_bytes * count * 2,
        name="middle",
    )
    terms = to_chips(keep, send)
    bit = 1
    while 2 * bit < dp_count:
        local_term = local_term + flip("dp", dp_count, bit)(local_term)
        bit *= 2
    locals_ = [local_term] + ([flip("dp", dp_count, bit)(local_term)] if bit < dp_count else [])
    back, pairs = call(
        functools.partial(mix_backward, chips, zs),
        here,
        (*terms, *locals_, spectral_weight),
        (mode_steps,),
        [mode_spec] * chips + [weight_small] * len(locals_) + [weight_spec],
        [back_spec, whole(pair_shape)],
        [back_shape, jax.ShapeDtypeStruct(pair_shape, F32)],
        [pltpu.VMEM((zs // 2, modes * 2 * zs, 128), F32)] + weight_scratch,
        flops=weight_bytes * 8,
        moved=weight_bytes + mode_bytes * chips,
        name="mix_backward",
    )
    def gram_part(start, size, before):
        spec = pl.BlockSpec((zs, 1, KX, channels, 2 * channels), lambda g, _: (0, g + start, 0, 0, 0))
        return call(
            functools.partial(gram, zs, start),
            here,
            (spread, pairs, *before),
            (size,),
            [whole(spread_shape), whole(pair_shape)] + [pl.BlockSpec(memory_space=pl.ANY)] * len(before),
            spec,
            jax.ShapeDtypeStruct(spectral_weight.shape, F32),
            flops=weight_bytes * 4,
            moved=weight_bytes,
            name="gram",
            aliases={3: 0} if before else {},
        )

    mine = [back] + [flip("mp", count, 2 * bit)(back) for bit in range(1, chips)]
    spectral_grad = gram_part(0, mode_rows // 2, ())
    *others, spectral_grad = lax.optimization_barrier((*mine[1:], spectral_grad))
    blocks = [back, *others] + [flip("mp", count, 1)(value) for value in (back, *others)]
    spectral_grad = gram_part(mode_rows // 2, mode_rows - mode_rows // 2, (spectral_grad,))
    scale = 1.0 / math.sqrt(NX * NY * snaps * dp_count * zs)
    back_field, local_grad = call(
        functools.partial(last, count, scale),
        here,
        (*blocks, x_back, y_plain, local_weight, preact_grad),
        (rows_here // wide,),
        [back_spec] * count + [x_back_spec, y_spec, weight_small, field_spec(wide)],
        [field_spec(wide), weight_small],
        [field_shape, small_shape],
        [rows_scratch],
        flops=field_bytes * (2 * KY + columns),
        moved=field_bytes * 2 + mode_bytes * count,
        name="last",
    )
    return (outer(output), outer(back_field), spectral_grad, local_grad)


def solution(mesh):
    placed = (
        P("mp", None, None, "dp", None),
        P("mp", None, None, "dp", None),
        P("dp", "mp", None, None, None),
        P(),
    )
    return jax.shard_map(
        body,
        mesh=mesh,
        in_specs=placed,
        out_specs=(
            P("mp", None, None, "dp", None),
            P("mp", None, None, "dp", None),
            P("dp", "mp", None, None, None),
            P(),
        ),
        check_vma=False,
    )
```

```python
import functools
import math

import jax
import jax.numpy as jnp
import ml_dtypes
import numpy as np
from jax import lax
from jax.experimental import pallas as pl
from jax.experimental.pallas import tpu as pltpu
from jax.sharding import PartitionSpec as P

NX = 256
NY = 256
KX = 32
KY = 32
F32 = jnp.float32
BF16 = jnp.bfloat16
ROOT = math.sqrt(2.0 / math.pi)
CUBE = 0.044715
VMEM = 52 << 20


def to_bf16(values):
    return values.astype(np.float32).astype(ml_dtypes.bfloat16)


def y_tables(count):
    block = KY // count
    k_index = np.arange(KY)
    angle = 2.0 * math.pi / NY * (k_index[:, None] * np.arange(NY)[None, :] % NY)
    table = to_bf16(np.stack([np.cos(angle), -np.sin(angle)]) / math.sqrt(NY)).astype(np.float32)
    weight = np.where(k_index == 0, 1.0, 2.0)[None, :, None]

    def ordered(values):
        shaped = values.reshape(2, count // 2, 2, block, NY).transpose(2, 1, 0, 3, 4)
        return to_bf16(shaped.reshape(2 * KY, NY))

    return ordered(table), ordered(table * weight)


def x_tables(count):
    block = KY // count
    rows = NX // count
    stored = np.arange(NX)
    x_index = stored % rows * count + stored // rows
    frequency = np.arange(KX) - KX // 2
    angle = 2.0 * math.pi / NX * (frequency[:, None] * x_index[None, :] % NX)
    cosine = np.cos(angle) / math.sqrt(NX)
    sine = np.sin(angle) / math.sqrt(NX)
    table = np.stack([np.stack([cosine, sine], 1), np.stack([-sine, cosine], 1)])
    per = table.reshape(2, KX, 2, count, rows).transpose(3, 0, 1, 4, 2)
    spread = np.einsum("nojxr,ab->noajxrb", per, np.eye(block))
    spread = to_bf16(spread.reshape(count, 2 * block * KX, rows * 2 * block))
    return spread, np.ascontiguousarray(spread.transpose(0, 2, 1))


def dot(left, right):
    return lax.dot_general(left, right, (((1,), (0,)), ((), ())), preferred_element_type=F32)


def dot_nt(left, right):
    return lax.dot_general(left, right, (((1,), (1,)), ((), ())), preferred_element_type=F32)


def streamed(ref, buffer, sem, at, steps, axis, size):
    def copy(step):
        where = [slice(None)] * axis + [pl.ds(step % (KX // size) * size, size)]
        where[1] = pl.ds(step // (KX // size), 1)
        return pltpu.make_async_copy(ref.at[tuple(where)], buffer.at[step], sem.at[step])

    @pl.when(at == 0)
    def _():
        for step in range(steps):
            copy(step).start()

    copy(at).wait()
    return buffer.at[at]


def whole(shape):
    zeros = (0,) * len(shape)
    return pl.BlockSpec(shape, lambda *_: zeros)


def call(kernel, here, operands, grid, in_specs, out_specs, out_shape, scratch=(), flops=0, moved=0, name=None, aliases=None, limit=VMEM):
    return pl.pallas_call(
        kernel,
        out_shape=out_shape,
        grid_spec=pltpu.PrefetchScalarGridSpec(
            num_scalar_prefetch=1,
            grid=grid,
            in_specs=in_specs,
            out_specs=out_specs,
            scratch_shapes=list(scratch),
        ),
        compiler_params=pltpu.CompilerParams(
            dimension_semantics=("arbitrary",) * len(grid), vmem_limit_bytes=limit
        ),
        cost_estimate=pl.CostEstimate(flops=flops, bytes_accessed=moved, transcendentals=0),
        name=name,
        input_output_aliases=aliases or {},
    )(here, *operands)


def store_spectrum(here, parts, keep_ref, send_ref):
    chips, width, _ = keep_ref.shape
    unit = width // len(parts)
    half = chips * unit
    own_first = here[0] % 2 == 0
    kept = [jnp.where(own_first, part[:half], part[half:]) for part in parts]
    sent = [jnp.where(own_first, part[half:], part[:half]) for part in parts]
    for chip in range(chips):
        rows = slice(chip * unit, (chip + 1) * unit)
        keep_ref[chip] = jnp.concatenate([part[rows] for part in kept], 0).astype(BF16)
        send_ref[chip] = jnp.concatenate([part[rows] for part in sent], 0).astype(BF16)


def forward_y(count, here, field_hbm, keep_ref, send_ref, buffer, table, sem):
    step = pl.program_id(0)
    steps, size = buffer.shape[:2]

    def copy(at):
        return pltpu.make_async_copy(field_hbm.at[pl.ds(at * size, size)], buffer.at[at], sem.at[at])

    @pl.when(step == 0)
    def _():
        for at in range(steps):
            copy(at).start()
        block = KY // count
        row = lax.broadcasted_iota(jnp.int32, table.shape, 0)
        y = lax.broadcasted_iota(jnp.int32, table.shape, 1)
        core, chip = row // KY, row % KY // (2 * block)
        k = (2 * chip + core) * block + row % block
        turn = (k * y + row // block % 2 * (NY // 4)) % NY
        angle = (2.0 * math.pi / NY) * turn.astype(F32)
        table[...] = (jnp.cos(angle) * (1.0 / math.sqrt(NY))).astype(BF16)

    copy(step).wait()
    value = table[...]
    parts = [dot_nt(value, buffer[step, x]) for x in range(size)]
    store_spectrum(here, parts, keep_ref, send_ref)


def forward_x(here, keep_ref, got_ref, own_ref, other_ref, *outs):
    chip = here[0] // 2
    for step, out in enumerate(outs):
        at = chip ^ step
        out[...] = (dot(own_ref[0], keep_ref[at]) + dot(other_ref[0], got_ref[at])).astype(BF16)


def total(refs):
    values = [ref[...].astype(F32) for ref in refs]
    while len(values) > 1:
        values = [a + b for a, b in zip(values[::2], values[1::2])]
    return values[0].astype(BF16).astype(F32)


def half_sign(shape):
    lane = lax.broadcasted_iota(jnp.int32, shape, 1)
    return jnp.where(lane % 128 < 64, -1.0, 1.0)


def low_half(shape):
    return lax.broadcasted_iota(jnp.int32, shape, 1) < 64


def mix_forward(count, zs, here, *refs):
    terms, (w_hbm, out_ref, spread_ref, coeff, prod, buffer, sem) = refs[:count], refs[count:]
    step = pl.program_id(0)
    per = buffer.shape[3]
    modes = coeff.shape[0] // 2
    first = step * per
    w_ref = streamed(w_hbm, buffer, sem, step, buffer.shape[0], 2, per)

    @pl.when(first == 0)
    def _():
        coeff[...] = total(terms)

    shape = (2 * zs, zs * 64)
    row = lax.broadcasted_iota(jnp.int32, shape, 0)
    keep = lax.broadcasted_iota(jnp.int32, shape, 1) // 64 == row % zs
    is_real = row < zs
    for pair in range(per // 2):
        lefts, weights = [], []
        for sub in range(2):
            at = first + 2 * pair + sub
            real = jnp.broadcast_to(coeff[pl.ds(at, 1), :], shape)
            imag = jnp.broadcast_to(coeff[pl.ds(modes + at, 1), :], shape)
            lefts.append(jnp.where(keep, jnp.where(is_real, real, imag), 0.0))
            weights.append(w_ref[:, 0, 2 * pair + sub].reshape(zs * 64, 128))
        left = jnp.concatenate(lefts, 0).astype(BF16)
        base = pl.multiple_of((first + 2 * pair) * 2 * zs, 4 * zs)
        spread_ref[pl.ds(base, 4 * zs), :] = left
        got = dot(left, jnp.concatenate(weights, 1))
        prod[pl.ds(base, 2 * zs), :] = got[: 2 * zs, :128]
        prod[pl.ds(base + 2 * zs, 2 * zs), :] = got[2 * zs :, 128:]

    @pl.when(first + per == modes)
    def _():
        sign = half_sign((modes, 128))
        low = low_half((modes, 128))
        for tile in range(zs // 2):
            rows = []
            for z in (2 * tile, 2 * tile + 1):
                real = prod[pl.ds(z, modes, stride=2 * zs), :]
                imag = prod[pl.ds(zs + z, modes, stride=2 * zs), :]
                rows.append(real + sign * pltpu.roll(imag, 64, 1))
            lanes = slice(tile * 128, (tile + 1) * 128)
            out_ref[:modes, lanes] = jnp.where(low, rows[0], pltpu.roll(rows[1], 64, 1)).astype(BF16)
            out_ref[modes:, lanes] = jnp.where(low, pltpu.roll(rows[0], 64, 1), rows[1]).astype(BF16)


def mix_backward(count, zs, here, *refs):
    terms, locals_ = refs[:count], refs[count:-6]
    w_hbm, out_ref, pair_ref, prod, buffer, sem = refs[-6:]
    step = pl.program_id(0)
    per = buffer.shape[3]
    modes = prod.shape[1] // (2 * zs)
    first = step * per
    w_ref = streamed(w_hbm, buffer, sem, step, buffer.shape[0], 2, per)

    @pl.when(first == 0)
    def _():
        parts = [ref[...] for ref in locals_]
        while len(parts) > 1:
            parts = [a + b for a, b in zip(parts[::2], parts[1::2])]
        extra = 64 // zs
        value = jnp.concatenate([parts[0][at * extra : (at + 1) * extra] for at in range(zs)], 1)
        coarse = value.astype(BF16)
        out_ref[2 * modes : 2 * modes + extra] = coarse
        out_ref[2 * modes + extra :] = (value - coarse.astype(F32)).astype(BF16)
        grad = total(terms)
        sign = half_sign((modes, 128))
        low = low_half((modes, 128))
        for tile in range(zs // 2):
            lanes = slice(tile * 128, (tile + 1) * 128)
            real, imag = grad[:modes, lanes], grad[modes:, lanes]
            even = jnp.where(low, real, pltpu.roll(imag, 64, 1))
            odd = jnp.where(low, pltpu.roll(real, 64, 1), imag)
            for z, value in ((2 * tile, even), (2 * tile + 1, odd)):
                pair_ref[pl.ds(z, modes, stride=2 * zs), :] = value
                pair_ref[pl.ds(zs + z, modes, stride=2 * zs), :] = -sign * pltpu.roll(value, 64, 1)

    for mode in range(per):
        base = pl.multiple_of((first + mode) * 2 * zs, 2 * zs)
        left = pair_ref[pl.ds(base, 2 * zs), :].astype(BF16)
        got = dot_nt(left, w_ref[:, 0, mode].reshape(zs * 64, 128))
        for tile in range(zs // 2):
            prod[tile, pl.ds(base, 2 * zs), :] = got[:, tile * 128 : (tile + 1) * 128]

    @pl.when(first + per == modes)
    def _():
        low = low_half((modes, 128))
        for part in range(2):
            for tile in range(zs // 2):
                at = part * zs + 2 * tile
                even = prod[tile, pl.ds(at, modes, stride=2 * zs), :]
                odd = prod[tile, pl.ds(at + 1, modes, stride=2 * zs), :]
                out_ref[part * modes : (part + 1) * modes, tile * 128 : (tile + 1) * 128] = jnp.where(
                    low, even, odd
                ).astype(BF16)


def gram(zs, start, here, spread_ref, pair_ref, *refs):
    out_hbm, buffer, sem = refs[-3:]
    step = pl.program_id(0)
    steps, per = buffer.shape[0], buffer.shape[3]
    group = 4
    unit = 2 * zs
    first = (start + step) * per
    out_ref = buffer.at[step]
    shape = (group * unit, 128)
    owner = lax.broadcasted_iota(jnp.int32, shape, 0) // unit

    def copy(step):
        rows = pl.ds((start + step) * per // KX, 1)
        return pltpu.make_async_copy(
            buffer.at[step], out_hbm.at[:, rows, pl.ds((start + step) * per % KX, per)], sem.at[step]
        )

    for at in range(0, per, group):
        base = pl.multiple_of((first + at) * unit, group * unit)
        left = jnp.transpose(spread_ref[pl.ds(base, group * unit), :].astype(F32)).astype(BF16)
        grad = pair_ref[pl.ds(base, group * unit), :]
        right = jnp.concatenate([jnp.where(owner == t, grad, 0.0) for t in range(group)], 1)
        got = dot(left, right.astype(BF16))
        for t in range(group):
            out_ref[:, 0, at + t] = got[:, t * 128 : (t + 1) * 128].reshape(zs, 64, 128)
    copy(step).start()

    @pl.when(step == steps - 1)
    def _():
        for at in range(steps):
            copy(at).wait()


def grid_rows(here, blocks, x_ref, rows):
    chips = rows.shape[1]
    core, chip = here[0] % 2, here[0] // 2
    for slot, block in enumerate(blocks):
        at_core = core if slot < chips else 1 - core
        rows[at_core, chip ^ (slot % chips)] = dot(x_ref[0], block[...])


def row_at(rows, count, x):
    cores, chips, height, _ = rows.shape
    per = height // (pl.num_programs(0) * count)
    start = pl.multiple_of(pl.program_id(0) * (count * per), count * per)
    step = [rows[core, chip, pl.ds(start, count * per), :] for core in range(cores) for chip in range(chips)]
    joined = jnp.concatenate([value[x * per : (x + 1) * per] for value in step], 0)
    return jnp.transpose(joined).astype(BF16)


def middle(count, here, *refs):
    blocks, rest = refs[:count], refs[count:]
    x_ref, y_ref, weight_ref, field_ref, cot_ref = rest[:5]
    out_ref, grad_ref, keep_ref, send_ref, term_ref, rows, mixing, acc = rest[5:]
    step = pl.program_id(0)
    size = field_ref.shape[0]
    columns = field_ref.shape[1]
    zs = columns // 64

    @pl.when(step == 0)
    def _():
        grid_rows(here, blocks, x_ref, rows)
        mixing[...] = jnp.transpose(weight_ref[...].astype(F32)).astype(BF16)
        acc[...] = jnp.zeros_like(acc)

    table = y_ref[...]
    lefts = [row_at(rows, size, x) for x in range(size)]
    low = low_half((64, 128))
    parts, sums = [], []

    def reduce(x):
        got = dot_nt(jnp.concatenate([table, field_ref[x]], 0), grad_ref[x])
        parts.append(got[: 2 * KY])
        for tile in range(zs // 2):
            lanes = slice(tile * 128, (tile + 1) * 128)
            at = 2 * KY + tile * 128
            sums.append((lanes, jnp.where(low, got[at : at + 64, lanes], got[at + 64 : at + 128, lanes])))

    for x in range(size):
        for at in range(0, columns, 64):
            part = slice(at, at + 64)
            p = dot(lefts[x][part], table) + dot(mixing[...], field_ref[x, part])
            square = p * p
            t = jnp.tanh(p * (ROOT + ROOT * CUBE * square))
            half = 0.5 + 0.5 * t
            out_ref[x, part] = (p * half).astype(BF16)
            slope = half + p * (1.0 - t * t) * (0.5 * ROOT + 1.5 * ROOT * CUBE * square)
            grad_ref[x, part] = (cot_ref[x, part].astype(F32) * slope).astype(BF16)
        if x:
            reduce(x - 1)
    reduce(size - 1)
    store_spectrum(here, parts, keep_ref, send_ref)
    for lanes, value in sums:
        acc[:, lanes] += value

    @pl.when(step == pl.num_programs(0) - 1)
    def _():
        value = acc[...]
        parts = [value[:, at : at + 64] for at in range(0, columns, 64)]
        while len(parts) > 1:
            parts = [a + b for a, b in zip(parts[::2], parts[1::2])]
        term_ref[...] = parts[0]


def last(count, scale, here, *refs):
    blocks, rest = refs[:count], refs[count:]
    x_ref, y_ref, weight_ref, grad_ref, out_ref, local_ref, rows = rest
    columns = grad_ref.shape[1]
    size = grad_ref.shape[0]

    @pl.when(pl.program_id(0) == 0)
    def _():
        height = x_ref.shape[2]
        extra = 64 * 64 // columns
        grid_rows(here, [block.at[pl.ds(0, height)] for block in blocks], x_ref, rows)
        parts = [
            block[pl.ds(height, extra), :].astype(F32) + block[pl.ds(height + extra, extra), :].astype(F32)
            for block in blocks
        ]
        while len(parts) > 1:
            parts = [a + b for a, b in zip(parts[::2], parts[1::2])]
        for at in range(columns // 64):
            local_ref[at * extra : (at + 1) * extra, :] = parts[0][:, at * 64 : (at + 1) * 64] * scale

    table = y_ref[...]
    weight = weight_ref[...]
    lefts = [row_at(rows, size, x) for x in range(size)]
    for x in range(size):
        for at in range(0, columns, 64):
            part = slice(at, at + 64)
            value = dot(lefts[x][part], table) + dot(weight, grad_ref[x, part])
            out_ref[x, part] = value.astype(BF16)


def flip(axis, size, bit):
    return functools.partial(lax.ppermute, axis_name=axis, perm=[(at, at ^ bit) for at in range(size)])


def body(features, out_grad, spectral_weight, local_weight):
    count = lax.axis_size("mp")
    dp_count = lax.axis_size("dp")
    chips = count // 2
    rows_here, grid_y, snaps, zs, channels = features.shape
    mode_rows = spectral_weight.shape[1]
    columns = snaps * zs * channels
    modes = mode_rows * KX
    unit = 2 * mode_rows
    here = lax.axis_index("mp").astype(jnp.int32).reshape(1)

    y_plain, y_weighted = y_tables(count)
    x_forward, x_back = x_tables(count)

    def inner(array):
        return jnp.transpose(array, (0, 2, 3, 4, 1)).reshape(rows_here, columns, grid_y)

    def outer(array):
        shaped = array.reshape(rows_here, snaps, zs, channels, grid_y)
        return jnp.transpose(shaped, (0, 4, 1, 2, 3))

    field, cot = inner(features), inner(out_grad)
    wide, chunk = min(16, rows_here), min(8, rows_here)

    def field_spec(size):
        return pl.BlockSpec((size, columns, grid_y), lambda g, _: (g, 0, 0))

    def half_spec(size):
        return pl.BlockSpec((chips, size * unit, columns), lambda g, _: (0, g, 0))

    field_shape = jax.ShapeDtypeStruct((rows_here, columns, grid_y), BF16)
    half_shape = jax.ShapeDtypeStruct((chips, rows_here * unit, columns), BF16)
    y_spec = whole((2 * KY, grid_y))
    mode_shape = jax.ShapeDtypeStruct((2 * modes, columns), BF16)
    mode_spec = whole((2 * modes, columns))
    weight_small = whole((channels, channels))
    small_shape = jax.ShapeDtypeStruct((channels, channels), F32)
    mixing_scratch = pltpu.VMEM((channels, channels), BF16)
    extra = 2 * channels * channels // columns
    back_spec = whole((2 * modes + extra, columns))
    back_shape = jax.ShapeDtypeStruct((2 * modes + extra, columns), BF16)
    field_bytes = rows_here * columns * grid_y * 2
    mode_bytes = 4 * modes * columns

    def to_chips(keep, send):
        got = flip("mp", count, 1)(send)
        x_spec = (1, 2 * modes, rows_here * unit)
        outs = call(
            forward_x,
            here,
            (keep, got, x_forward, x_forward),
            (1,),
            [
                whole(keep.shape),
                whole(keep.shape),
                pl.BlockSpec(x_spec, lambda g, m: (m[0], 0, 0)),
                pl.BlockSpec(x_spec, lambda g, m: (m[0] ^ 1, 0, 0)),
            ],
            [mode_spec] * chips,
            [mode_shape] * chips,
            flops=8 * chips * modes * rows_here * unit * columns,
            moved=mode_bytes * 3 * chips,
            name="forward_x",
            limit=8 << 20,
        )
        return [outs[0]] + [flip("mp", count, 2 * bit)(outs[bit]) for bit in range(1, chips)]

    def to_all(block):
        mine = [block] + [flip("mp", count, 2 * bit)(block) for bit in range(1, chips)]
        return mine + [flip("mp", count, 1)(value) for value in mine]

    per = 16
    mode_steps = modes // per
    weight_spec = pl.BlockSpec(memory_space=pl.ANY)
    weight_scratch = [
        pltpu.VMEM((mode_steps, zs, 1, per, channels, 2 * channels), BF16),
        pltpu.SemaphoreType.DMA((mode_steps,)),
    ]
    spread_shape = (modes * 2 * zs, columns)
    pair_shape = (modes * 2 * zs, 2 * channels)
    weight_bytes = zs * modes * channels * 2 * channels * 2

    keep, send = call(
        functools.partial(forward_y, count),
        here,
        (field,),
        (rows_here // chunk,),
        [pl.BlockSpec(memory_space=pltpu.HBM)],
        [half_spec(chunk)] * 2,
        [half_shape] * 2,
        [
            pltpu.VMEM((rows_here // chunk, chunk, columns, grid_y), BF16),
            pltpu.VMEM((2 * KY, grid_y), BF16),
            pltpu.SemaphoreType.DMA((rows_here // chunk,)),
        ],
        flops=field_bytes * 2 * KY,
        moved=field_bytes + mode_bytes * count,
        name="forward_y",
    )
    terms = to_chips(keep, send)
    mixed, spread = call(
        functools.partial(mix_forward, chips, zs),
        here,
        (*terms, spectral_weight),
        (mode_steps,),
        [mode_spec] * chips + [weight_spec],
        [mode_spec, whole(spread_shape)],
        [mode_shape, jax.ShapeDtypeStruct(spread_shape, BF16)],
        [pltpu.VMEM((2 * modes, columns), F32), pltpu.VMEM(pair_shape, F32)] + weight_scratch,
        flops=weight_bytes * 8,
        moved=weight_bytes + mode_bytes * chips,
        name="mix_forward",
    )
    blocks = to_all(mixed)
    x_back_spec = pl.BlockSpec((1, rows_here * unit, 2 * modes), lambda g, m: (m[0], 0, 0))
    rows_scratch = pltpu.VMEM((2, chips, rows_here * unit, columns), F32)
    output, preact_grad, keep, send, local_term = call(
        functools.partial(middle, count),
        here,
        (*blocks, x_back, y_weighted, local_weight, field, cot),
        (rows_here // chunk,),
        [mode_spec] * count + [x_back_spec, y_spec, weight_small] + [field_spec(chunk)] * 2,
        [field_spec(chunk)] * 2 + [half_spec(chunk)] * 2 + [weight_small],
        [field_shape, field_shape, half_shape, half_shape, small_shape],
        [rows_scratch, mixing_scratch, pltpu.VMEM((channels, columns), F32)],
        flops=field_bytes * (4 * KY + 2 * columns),
        moved=field_bytes * 4 + mode_bytes * count * 2,
        name="middle",
    )
    terms = to_chips(keep, send)
    bit = 1
    while 2 * bit < dp_count:
        local_term = local_term + flip("dp", dp_count, bit)(local_term)
        bit *= 2
    locals_ = [local_term] + ([flip("dp", dp_count, bit)(local_term)] if bit < dp_count else [])
    back, pairs = call(
        functools.partial(mix_backward, chips, zs),
        here,
        (*terms, *locals_, spectral_weight),
        (mode_steps,),
        [mode_spec] * chips + [weight_small] * len(locals_) + [weight_spec],
        [back_spec, whole(pair_shape)],
        [back_shape, jax.ShapeDtypeStruct(pair_shape, F32)],
        [pltpu.VMEM((zs // 2, modes * 2 * zs, 128), F32)] + weight_scratch,
        flops=weight_bytes * 8,
        moved=weight_bytes + mode_bytes * chips,
        name="mix_backward",
    )
    gram_steps = modes // 8
    early = gram_steps * 5 // 8

    def gram_part(start, steps, before):
        per = 8
        return call(
            functools.partial(gram, zs, start),
            here,
            (spread, pairs, *before),
            (steps,),
            [whole(spread_shape), whole(pair_shape)] + [pl.BlockSpec(memory_space=pl.ANY)] * len(before),
            pl.BlockSpec(memory_space=pl.ANY),
            jax.ShapeDtypeStruct(spectral_weight.shape, F32),
            [
                pltpu.VMEM((steps, zs, 1, per, channels, 2 * channels), F32),
                pltpu.SemaphoreType.DMA((steps,)),
            ],
            flops=weight_bytes * 4,
            moved=weight_bytes,
            name="gram",
            aliases={3: 0} if before else {},
        )

    mine = [back] + [flip("mp", count, 2 * bit)(back) for bit in range(1, chips)]
    spectral_grad = gram_part(0, early, ())
    *others, spectral_grad = lax.optimization_barrier((*mine[1:], spectral_grad))
    blocks = [back, *others] + [flip("mp", count, 1)(value) for value in (back, *others)]
    spectral_grad = gram_part(early, gram_steps - early, (spectral_grad,))
    scale = 1.0 / math.sqrt(NX * NY * snaps * dp_count * zs)
    back_field, local_grad = call(
        functools.partial(last, count, scale),
        here,
        (*blocks, x_back, y_plain, local_weight, preact_grad),
        (rows_here // wide,),
        [back_spec] * count + [x_back_spec, y_spec, weight_small, field_spec(wide)],
        [field_spec(wide), weight_small],
        [field_shape, small_shape],
        [rows_scratch],
        flops=field_bytes * (2 * KY + columns),
        moved=field_bytes * 2 + mode_bytes * count,
        name="last",
    )
    return (outer(output), outer(back_field), spectral_grad, local_grad)


def solution(mesh):
    placed = (
        P("mp", None, None, "dp", None),
        P("mp", None, None, "dp", None),
        P("dp", "mp", None, None, None),
        P(),
    )
    return jax.shard_map(
        body,
        mesh=mesh,
        in_specs=placed,
        out_specs=(
            P("mp", None, None, "dp", None),
            P("mp", None, None, "dp", None),
            P("dp", "mp", None, None, None),
            P(),
        ),
        check_vma=False,
    )
```

```python
import functools
import math

import jax
import jax.numpy as jnp
import ml_dtypes
import numpy as np
from jax import lax
from jax.experimental import pallas as pl
from jax.experimental.pallas import tpu as pltpu
from jax.sharding import PartitionSpec as P

NX = 256
NY = 256
KX = 32
KY = 32
F32 = jnp.float32
BF16 = jnp.bfloat16
ROOT = math.sqrt(2.0 / math.pi)
CUBE = 0.044715
VMEM = 52 << 20


def to_bf16(values):
    return values.astype(np.float32).astype(ml_dtypes.bfloat16)


def y_tables(count):
    block = KY // count
    k_index = np.arange(KY)
    angle = 2.0 * math.pi / NY * (k_index[:, None] * np.arange(NY)[None, :] % NY)
    table = to_bf16(np.stack([np.cos(angle), -np.sin(angle)]) / math.sqrt(NY)).astype(np.float32)
    weight = np.where(k_index == 0, 1.0, 2.0)[None, :, None]

    def ordered(values):
        shaped = values.reshape(2, count // 2, 2, block, NY).transpose(2, 1, 0, 3, 4)
        return to_bf16(shaped.reshape(2 * KY, NY))

    return ordered(table), ordered(table * weight)


def x_tables(count):
    block = KY // count
    rows = NX // count
    stored = np.arange(NX)
    x_index = stored % rows * count + stored // rows
    frequency = np.arange(KX) - KX // 2
    angle = 2.0 * math.pi / NX * (frequency[:, None] * x_index[None, :] % NX)
    cosine = np.cos(angle) / math.sqrt(NX)
    sine = np.sin(angle) / math.sqrt(NX)
    table = np.stack([np.stack([cosine, sine], 1), np.stack([-sine, cosine], 1)])
    per = table.reshape(2, KX, 2, count, rows).transpose(3, 0, 1, 4, 2)
    spread = np.einsum("nojxr,ab->noajxrb", per, np.eye(block))
    spread = to_bf16(spread.reshape(count, 2 * block * KX, rows * 2 * block))
    return spread, np.ascontiguousarray(spread.transpose(0, 2, 1))


def dot(left, right):
    return lax.dot_general(left, right, (((1,), (0,)), ((), ())), preferred_element_type=F32)


def dot_nt(left, right):
    return lax.dot_general(left, right, (((1,), (1,)), ((), ())), preferred_element_type=F32)


def streamed(ref, buffer, sem, at, steps, axis, size):
    def copy(step):
        where = [slice(None)] * axis + [pl.ds(step % (KX // size) * size, size)]
        where[1] = pl.ds(step // (KX // size), 1)
        return pltpu.make_async_copy(ref.at[tuple(where)], buffer.at[step], sem.at[step])

    @pl.when(at == 0)
    def _():
        for step in range(steps):
            copy(step).start()

    copy(at).wait()
    return buffer.at[at]


def whole(shape):
    zeros = (0,) * len(shape)
    return pl.BlockSpec(shape, lambda *_: zeros)


def call(kernel, here, operands, grid, in_specs, out_specs, out_shape, scratch=(), flops=0, moved=0, name=None, aliases=None, limit=VMEM):
    return pl.pallas_call(
        kernel,
        out_shape=out_shape,
        grid_spec=pltpu.PrefetchScalarGridSpec(
            num_scalar_prefetch=1,
            grid=grid,
            in_specs=in_specs,
            out_specs=out_specs,
            scratch_shapes=list(scratch),
        ),
        compiler_params=pltpu.CompilerParams(
            dimension_semantics=("arbitrary",) * len(grid), vmem_limit_bytes=limit
        ),
        cost_estimate=pl.CostEstimate(flops=flops, bytes_accessed=moved, transcendentals=0),
        name=name,
        input_output_aliases=aliases or {},
    )(here, *operands)


def store_spectrum(here, parts, keep_ref, send_ref):
    chips, width, _ = keep_ref.shape
    unit = width // len(parts)
    half = chips * unit
    own_first = here[0] % 2 == 0
    kept = [jnp.where(own_first, part[:half], part[half:]) for part in parts]
    sent = [jnp.where(own_first, part[half:], part[:half]) for part in parts]
    for chip in range(chips):
        rows = slice(chip * unit, (chip + 1) * unit)
        keep_ref[chip] = jnp.concatenate([part[rows] for part in kept], 0).astype(BF16)
        send_ref[chip] = jnp.concatenate([part[rows] for part in sent], 0).astype(BF16)


def forward_y(count, here, field_hbm, keep_ref, send_ref, buffer, table, sem):
    step = pl.program_id(0)
    steps, size = buffer.shape[:2]

    def copy(at):
        return pltpu.make_async_copy(field_hbm.at[pl.ds(at * size, size)], buffer.at[at], sem.at[at])

    @pl.when(step == 0)
    def _():
        for at in range(steps):
            copy(at).start()
        block = KY // count
        row = lax.broadcasted_iota(jnp.int32, table.shape, 0)
        y = lax.broadcasted_iota(jnp.int32, table.shape, 1)
        core, chip = row // KY, row % KY // (2 * block)
        k = (2 * chip + core) * block + row % block
        turn = (k * y + row // block % 2 * (NY // 4)) % NY
        angle = (2.0 * math.pi / NY) * turn.astype(F32)
        table[...] = (jnp.cos(angle) * (1.0 / math.sqrt(NY))).astype(BF16)

    copy(step).wait()
    value = table[...]
    parts = [dot_nt(value, buffer[step, x]) for x in range(size)]
    store_spectrum(here, parts, keep_ref, send_ref)


def forward_x(here, keep_ref, got_ref, own_ref, other_ref, *outs):
    chip = here[0] // 2
    for step, out in enumerate(outs):
        at = chip ^ step
        out[...] = (dot(own_ref[0], keep_ref[at]) + dot(other_ref[0], got_ref[at])).astype(BF16)


def total(refs):
    values = [ref[...].astype(F32) for ref in refs]
    while len(values) > 1:
        values = [a + b for a, b in zip(values[::2], values[1::2])]
    return values[0].astype(BF16).astype(F32)


def half_sign(shape):
    lane = lax.broadcasted_iota(jnp.int32, shape, 1)
    return jnp.where(lane % 128 < 64, -1.0, 1.0)


def low_half(shape):
    return lax.broadcasted_iota(jnp.int32, shape, 1) < 64


def mix_forward(count, zs, here, *refs):
    terms, (w_hbm, out_ref, spread_ref, coeff, prod, buffer, sem) = refs[:count], refs[count:]
    step = pl.program_id(0)
    per = buffer.shape[3]
    modes = coeff.shape[0] // 2
    first = step * per
    w_ref = streamed(w_hbm, buffer, sem, step, buffer.shape[0], 2, per)

    @pl.when(first == 0)
    def _():
        coeff[...] = total(terms)

    shape = (2 * zs, zs * 64)
    row = lax.broadcasted_iota(jnp.int32, shape, 0)
    keep = lax.broadcasted_iota(jnp.int32, shape, 1) // 64 == row % zs
    is_real = row < zs
    for pair in range(per // 2):
        lefts, weights = [], []
        for sub in range(2):
            at = first + 2 * pair + sub
            real = jnp.broadcast_to(coeff[pl.ds(at, 1), :], shape)
            imag = jnp.broadcast_to(coeff[pl.ds(modes + at, 1), :], shape)
            lefts.append(jnp.where(keep, jnp.where(is_real, real, imag), 0.0))
            weights.append(w_ref[:, 0, 2 * pair + sub].reshape(zs * 64, 128))
        left = jnp.concatenate(lefts, 0).astype(BF16)
        base = pl.multiple_of((first + 2 * pair) * 2 * zs, 4 * zs)
        spread_ref[pl.ds(base, 4 * zs), :] = left
        got = dot(left, jnp.concatenate(weights, 1))
        prod[pl.ds(base, 2 * zs), :] = got[: 2 * zs, :128]
        prod[pl.ds(base + 2 * zs, 2 * zs), :] = got[2 * zs :, 128:]

    @pl.when(first + per == modes)
    def _():
        sign = half_sign((modes, 128))
        low = low_half((modes, 128))
        for tile in range(zs // 2):
            rows = []
            for z in (2 * tile, 2 * tile + 1):
                real = prod[pl.ds(z, modes, stride=2 * zs), :]
                imag = prod[pl.ds(zs + z, modes, stride=2 * zs), :]
                rows.append(real + sign * pltpu.roll(imag, 64, 1))
            lanes = slice(tile * 128, (tile + 1) * 128)
            out_ref[:modes, lanes] = jnp.where(low, rows[0], pltpu.roll(rows[1], 64, 1)).astype(BF16)
            out_ref[modes:, lanes] = jnp.where(low, pltpu.roll(rows[0], 64, 1), rows[1]).astype(BF16)


def mix_backward(count, zs, here, *refs):
    terms, locals_ = refs[:count], refs[count:-6]
    w_hbm, out_ref, pair_ref, prod, buffer, sem = refs[-6:]
    step = pl.program_id(0)
    per = buffer.shape[3]
    modes = prod.shape[1] // (2 * zs)
    first = step * per
    w_ref = streamed(w_hbm, buffer, sem, step, buffer.shape[0], 2, per)

    @pl.when(first == 0)
    def _():
        parts = [ref[...] for ref in locals_]
        while len(parts) > 1:
            parts = [a + b for a, b in zip(parts[::2], parts[1::2])]
        extra = 64 // zs
        value = jnp.concatenate([parts[0][at * extra : (at + 1) * extra] for at in range(zs)], 1)
        coarse = value.astype(BF16)
        out_ref[2 * modes : 2 * modes + extra] = coarse
        out_ref[2 * modes + extra :] = (value - coarse.astype(F32)).astype(BF16)
        grad = total(terms)
        sign = half_sign((modes, 128))
        low = low_half((modes, 128))
        for tile in range(zs // 2):
            lanes = slice(tile * 128, (tile + 1) * 128)
            real, imag = grad[:modes, lanes], grad[modes:, lanes]
            even = jnp.where(low, real, pltpu.roll(imag, 64, 1))
            odd = jnp.where(low, pltpu.roll(real, 64, 1), imag)
            for z, value in ((2 * tile, even), (2 * tile + 1, odd)):
                pair_ref[pl.ds(z, modes, stride=2 * zs), :] = value
                pair_ref[pl.ds(zs + z, modes, stride=2 * zs), :] = -sign * pltpu.roll(value, 64, 1)

    for mode in range(per):
        base = pl.multiple_of((first + mode) * 2 * zs, 2 * zs)
        left = pair_ref[pl.ds(base, 2 * zs), :].astype(BF16)
        got = dot_nt(left, w_ref[:, 0, mode].reshape(zs * 64, 128))
        for tile in range(zs // 2):
            prod[tile, pl.ds(base, 2 * zs), :] = got[:, tile * 128 : (tile + 1) * 128]

    @pl.when(first + per == modes)
    def _():
        low = low_half((modes, 128))
        for part in range(2):
            for tile in range(zs // 2):
                at = part * zs + 2 * tile
                even = prod[tile, pl.ds(at, modes, stride=2 * zs), :]
                odd = prod[tile, pl.ds(at + 1, modes, stride=2 * zs), :]
                out_ref[part * modes : (part + 1) * modes, tile * 128 : (tile + 1) * 128] = jnp.where(
                    low, even, odd
                ).astype(BF16)


def gram(zs, start, here, spread_ref, pair_ref, *refs):
    out_hbm, buffer, sem = refs[-3:]
    step = pl.program_id(0)
    steps, per = buffer.shape[0], buffer.shape[3]
    group = 4
    unit = 2 * zs
    first = (start + step) * per
    out_ref = buffer.at[step]
    shape = (group * unit, 128)
    owner = lax.broadcasted_iota(jnp.int32, shape, 0) // unit

    def copy(step):
        rows = pl.ds((start + step) * per // KX, 1)
        return pltpu.make_async_copy(
            buffer.at[step], out_hbm.at[:, rows, pl.ds((start + step) * per % KX, per)], sem.at[step]
        )

    for at in range(0, per, group):
        base = pl.multiple_of((first + at) * unit, group * unit)
        left = jnp.transpose(spread_ref[pl.ds(base, group * unit), :].astype(F32)).astype(BF16)
        grad = pair_ref[pl.ds(base, group * unit), :]
        right = jnp.concatenate([jnp.where(owner == t, grad, 0.0) for t in range(group)], 1)
        got = dot(left, right.astype(BF16))
        for t in range(group):
            out_ref[:, 0, at + t] = got[:, t * 128 : (t + 1) * 128].reshape(zs, 64, 128)
    copy(step).start()

    @pl.when(step == steps - 1)
    def _():
        for at in range(steps):
            copy(at).wait()


def grid_rows(here, blocks, x_ref, rows):
    chips = rows.shape[1]
    core, chip = here[0] % 2, here[0] // 2
    for slot, block in enumerate(blocks):
        at_core = core if slot < chips else 1 - core
        rows[at_core, chip ^ (slot % chips)] = dot(x_ref[0], block[...])


def row_at(rows, count, x):
    cores, chips, height, _ = rows.shape
    per = height // (pl.num_programs(0) * count)
    start = pl.multiple_of(pl.program_id(0) * (count * per), count * per)
    step = [rows[core, chip, pl.ds(start, count * per), :] for core in range(cores) for chip in range(chips)]
    joined = jnp.concatenate([value[x * per : (x + 1) * per] for value in step], 0)
    return jnp.transpose(joined).astype(BF16)


def middle(count, here, *refs):
    blocks, rest = refs[:count], refs[count:]
    x_ref, y_ref, weight_ref, field_ref, cot_ref = rest[:5]
    out_ref, grad_ref, keep_ref, send_ref, term_ref, rows, mixing, acc = rest[5:]
    step = pl.program_id(0)
    size = field_ref.shape[0]
    columns = field_ref.shape[1]
    zs = columns // 64

    @pl.when(step == 0)
    def _():
        grid_rows(here, blocks, x_ref, rows)
        mixing[...] = jnp.transpose(weight_ref[...].astype(F32)).astype(BF16)
        acc[...] = jnp.zeros_like(acc)

    table = y_ref[...]
    lefts = [row_at(rows, size, x) for x in range(size)]
    low = low_half((64, 128))
    parts, sums = [], []

    def reduce(x):
        got = dot_nt(jnp.concatenate([table, field_ref[x]], 0), grad_ref[x])
        parts.append(got[: 2 * KY])
        for tile in range(zs // 2):
            lanes = slice(tile * 128, (tile + 1) * 128)
            at = 2 * KY + tile * 128
            sums.append((lanes, jnp.where(low, got[at : at + 64, lanes], got[at + 64 : at + 128, lanes])))

    for x in range(size):
        for at in range(0, columns, 64):
            part = slice(at, at + 64)
            p = dot(lefts[x][part], table) + dot(mixing[...], field_ref[x, part])
            square = p * p
            t = jnp.tanh(p * (ROOT + ROOT * CUBE * square))
            half = 0.5 + 0.5 * t
            out_ref[x, part] = (p * half).astype(BF16)
            slope = half + p * (1.0 - t * t) * (0.5 * ROOT + 1.5 * ROOT * CUBE * square)
            grad_ref[x, part] = (cot_ref[x, part].astype(F32) * slope).astype(BF16)
        if x:
            reduce(x - 1)
    reduce(size - 1)
    store_spectrum(here, parts, keep_ref, send_ref)
    for lanes, value in sums:
        acc[:, lanes] += value

    @pl.when(step == pl.num_programs(0) - 1)
    def _():
        value = acc[...]
        parts = [value[:, at : at + 64] for at in range(0, columns, 64)]
        while len(parts) > 1:
            parts = [a + b for a, b in zip(parts[::2], parts[1::2])]
        term_ref[...] = parts[0]


def last(count, scale, here, *refs):
    blocks, rest = refs[:count], refs[count:]
    x_ref, y_ref, weight_ref, grad_ref, out_ref, local_ref, rows = rest
    columns = grad_ref.shape[1]
    size = grad_ref.shape[0]

    @pl.when(pl.program_id(0) == 0)
    def _():
        height = x_ref.shape[2]
        extra = 64 * 64 // columns
        grid_rows(here, [block.at[pl.ds(0, height)] for block in blocks], x_ref, rows)
        parts = [
            block[pl.ds(height, extra), :].astype(F32) + block[pl.ds(height + extra, extra), :].astype(F32)
            for block in blocks
        ]
        while len(parts) > 1:
            parts = [a + b for a, b in zip(parts[::2], parts[1::2])]
        for at in range(columns // 64):
            local_ref[at * extra : (at + 1) * extra, :] = parts[0][:, at * 64 : (at + 1) * 64] * scale

    table = y_ref[...]
    weight = weight_ref[...]
    lefts = [row_at(rows, size, x) for x in range(size)]
    for x in range(size):
        for at in range(0, columns, 64):
            part = slice(at, at + 64)
            value = dot(lefts[x][part], table) + dot(weight, grad_ref[x, part])
            out_ref[x, part] = value.astype(BF16)


def flip(axis, size, bit):
    return functools.partial(lax.ppermute, axis_name=axis, perm=[(at, at ^ bit) for at in range(size)])


def body(features, out_grad, spectral_weight, local_weight):
    count = lax.axis_size("mp")
    dp_count = lax.axis_size("dp")
    chips = count // 2
    rows_here, grid_y, snaps, zs, channels = features.shape
    mode_rows = spectral_weight.shape[1]
    columns = snaps * zs * channels
    modes = mode_rows * KX
    unit = 2 * mode_rows
    here = lax.axis_index("mp").astype(jnp.int32).reshape(1)

    y_plain, y_weighted = y_tables(count)
    x_forward, x_back = x_tables(count)

    def inner(array):
        return jnp.transpose(array, (0, 2, 3, 4, 1)).reshape(rows_here, columns, grid_y)

    def outer(array):
        shaped = array.reshape(rows_here, snaps, zs, channels, grid_y)
        return jnp.transpose(shaped, (0, 4, 1, 2, 3))

    field, cot = inner(features), inner(out_grad)
    wide, chunk = min(16, rows_here), min(8, rows_here)

    def field_spec(size):
        return pl.BlockSpec((size, columns, grid_y), lambda g, _: (g, 0, 0))

    def half_spec(size):
        return pl.BlockSpec((chips, size * unit, columns), lambda g, _: (0, g, 0))

    field_shape = jax.ShapeDtypeStruct((rows_here, columns, grid_y), BF16)
    half_shape = jax.ShapeDtypeStruct((chips, rows_here * unit, columns), BF16)
    y_spec = whole((2 * KY, grid_y))
    mode_shape = jax.ShapeDtypeStruct((2 * modes, columns), BF16)
    mode_spec = whole((2 * modes, columns))
    weight_small = whole((channels, channels))
    small_shape = jax.ShapeDtypeStruct((channels, channels), F32)
    mixing_scratch = pltpu.VMEM((channels, channels), BF16)
    extra = 2 * channels * channels // columns
    back_spec = whole((2 * modes + extra, columns))
    back_shape = jax.ShapeDtypeStruct((2 * modes + extra, columns), BF16)
    field_bytes = rows_here * columns * grid_y * 2
    mode_bytes = 4 * modes * columns

    def to_chips(keep, send, beside=None):
        got = flip("mp", count, 1)(send)
        x_spec = (1, 2 * modes, rows_here * unit)
        outs = call(
            forward_x,
            here,
            (keep, got, x_forward, x_forward),
            (1,),
            [
                whole(keep.shape),
                whole(keep.shape),
                pl.BlockSpec(x_spec, lambda g, m: (m[0], 0, 0)),
                pl.BlockSpec(x_spec, lambda g, m: (m[0] ^ 1, 0, 0)),
            ],
            [mode_spec] * chips,
            [mode_shape] * chips,
            flops=8 * chips * modes * rows_here * unit * columns,
            moved=mode_bytes * 3 * chips,
            name="forward_x",
            limit=8 << 20,
        )
        outs = list(outs)
        if beside is not None:
            outs[-1], beside = lax.optimization_barrier((outs[-1], beside))
        return [outs[0]] + [flip("mp", count, 2 * bit)(outs[bit]) for bit in range(1, chips)], beside

    def to_all(block):
        mine = [block] + [flip("mp", count, 2 * bit)(block) for bit in range(1, chips)]
        return mine + [flip("mp", count, 1)(value) for value in mine]

    per = 16
    mode_steps = modes // per
    weight_spec = pl.BlockSpec(memory_space=pl.ANY)
    weight_scratch = [
        pltpu.VMEM((mode_steps, zs, 1, per, channels, 2 * channels), BF16),
        pltpu.SemaphoreType.DMA((mode_steps,)),
    ]
    spread_shape = (modes * 2 * zs, columns)
    pair_shape = (modes * 2 * zs, 2 * channels)
    weight_bytes = zs * modes * channels * 2 * channels * 2

    keep, send = call(
        functools.partial(forward_y, count),
        here,
        (field,),
        (rows_here // chunk,),
        [pl.BlockSpec(memory_space=pltpu.HBM)],
        [half_spec(chunk)] * 2,
        [half_shape] * 2,
        [
            pltpu.VMEM((rows_here // chunk, chunk, columns, grid_y), BF16),
            pltpu.VMEM((2 * KY, grid_y), BF16),
            pltpu.SemaphoreType.DMA((rows_here // chunk,)),
        ],
        flops=field_bytes * 2 * KY,
        moved=field_bytes + mode_bytes * count,
        name="forward_y",
    )
    terms, _ = to_chips(keep, send)
    mixed, spread = call(
        functools.partial(mix_forward, chips, zs),
        here,
        (*terms, spectral_weight),
        (mode_steps,),
        [mode_spec] * chips + [weight_spec],
        [mode_spec, whole(spread_shape)],
        [mode_shape, jax.ShapeDtypeStruct(spread_shape, BF16)],
        [pltpu.VMEM((2 * modes, columns), F32), pltpu.VMEM(pair_shape, F32)] + weight_scratch,
        flops=weight_bytes * 8,
        moved=weight_bytes + mode_bytes * chips,
        name="mix_forward",
    )
    blocks = to_all(mixed)
    x_back_spec = pl.BlockSpec((1, rows_here * unit, 2 * modes), lambda g, m: (m[0], 0, 0))
    rows_scratch = pltpu.VMEM((2, chips, rows_here * unit, columns), F32)
    output, preact_grad, keep, send, local_term = call(
        functools.partial(middle, count),
        here,
        (*blocks, x_back, y_weighted, local_weight, field, cot),
        (rows_here // chunk,),
        [mode_spec] * count + [x_back_spec, y_spec, weight_small] + [field_spec(chunk)] * 2,
        [field_spec(chunk)] * 2 + [half_spec(chunk)] * 2 + [weight_small],
        [field_shape, field_shape, half_shape, half_shape, small_shape],
        [rows_scratch, mixing_scratch, pltpu.VMEM((channels, columns), F32)],
        flops=field_bytes * (4 * KY + 2 * columns),
        moved=field_bytes * 4 + mode_bytes * count * 2,
        name="middle",
    )
    first_got = flip("dp", dp_count, 1)(local_term) if dp_count > 1 else jnp.zeros_like(local_term)
    terms, first_got = to_chips(keep, send, first_got)
    locals_, bit = [local_term, first_got], 2
    while bit < dp_count:
        local_term = locals_[0] + locals_[1]
        locals_ = [local_term, flip("dp", dp_count, bit)(local_term)]
        bit *= 2
    back, pairs = call(
        functools.partial(mix_backward, chips, zs),
        here,
        (*terms, *locals_, spectral_weight),
        (mode_steps,),
        [mode_spec] * chips + [weight_small] * len(locals_) + [weight_spec],
        [back_spec, whole(pair_shape)],
        [back_shape, jax.ShapeDtypeStruct(pair_shape, F32)],
        [pltpu.VMEM((zs // 2, modes * 2 * zs, 128), F32)] + weight_scratch,
        flops=weight_bytes * 8,
        moved=weight_bytes + mode_bytes * chips,
        name="mix_backward",
    )
    gram_steps = modes // 8
    early = gram_steps * 5 // 8

    def gram_part(start, steps, before):
        per = 8
        return call(
            functools.partial(gram, zs, start),
            here,
            (spread, pairs, *before),
            (steps,),
            [whole(spread_shape), whole(pair_shape)] + [pl.BlockSpec(memory_space=pl.ANY)] * len(before),
            pl.BlockSpec(memory_space=pl.ANY),
            jax.ShapeDtypeStruct(spectral_weight.shape, F32),
            [
                pltpu.VMEM((steps, zs, 1, per, channels, 2 * channels), F32),
                pltpu.SemaphoreType.DMA((steps,)),
            ],
            flops=weight_bytes * 4,
            moved=weight_bytes,
            name="gram",
            aliases={3: 0} if before else {},
        )

    mine = [back] + [flip("mp", count, 2 * bit)(back) for bit in range(1, chips)]
    spectral_grad = gram_part(0, early, ())
    *others, spectral_grad = lax.optimization_barrier((*mine[1:], spectral_grad))
    blocks = [back, *others] + [flip("mp", count, 1)(value) for value in (back, *others)]
    spectral_grad = gram_part(early, gram_steps - early, (spectral_grad,))
    scale = 1.0 / math.sqrt(NX * NY * snaps * dp_count * zs)
    back_field, local_grad = call(
        functools.partial(last, count, scale),
        here,
        (*blocks, x_back, y_plain, local_weight, preact_grad),
        (rows_here // wide,),
        [back_spec] * count + [x_back_spec, y_spec, weight_small, field_spec(wide)],
        [field_spec(wide), weight_small],
        [field_shape, small_shape],
        [rows_scratch],
        flops=field_bytes * (2 * KY + columns),
        moved=field_bytes * 2 + mode_bytes * count,
        name="last",
    )
    return (outer(output), outer(back_field), spectral_grad, local_grad)


def solution(mesh):
    placed = (
        P("mp", None, None, "dp", None),
        P("mp", None, None, "dp", None),
        P("dp", "mp", None, None, None),
        P(),
    )
    return jax.shard_map(
        body,
        mesh=mesh,
        in_specs=placed,
        out_specs=(
            P("mp", None, None, "dp", None),
            P("mp", None, None, "dp", None),
            P("dp", "mp", None, None, None),
            P(),
        ),
        check_vma=False,
    )
```

```python
import functools
import math

import jax
import jax.numpy as jnp
import ml_dtypes
import numpy as np
from jax import lax
from jax.experimental import pallas as pl
from jax.experimental.pallas import tpu as pltpu
from jax.sharding import PartitionSpec as P

NX = 256
NY = 256
KX = 32
KY = 32
F32 = jnp.float32
BF16 = jnp.bfloat16
ROOT = math.sqrt(2.0 / math.pi)
CUBE = 0.044715
VMEM = 52 << 20


def to_bf16(values):
    return values.astype(np.float32).astype(ml_dtypes.bfloat16)


def y_tables(count):
    block = KY // count
    k_index = np.arange(KY)
    angle = 2.0 * math.pi / NY * (k_index[:, None] * np.arange(NY)[None, :] % NY)
    table = to_bf16(np.stack([np.cos(angle), -np.sin(angle)]) / math.sqrt(NY)).astype(np.float32)
    weight = np.where(k_index == 0, 1.0, 2.0)[None, :, None]

    def ordered(values):
        shaped = values.reshape(2, count // 2, 2, block, NY).transpose(2, 1, 0, 3, 4)
        return to_bf16(shaped.reshape(2 * KY, NY))

    return ordered(table), ordered(table * weight)


def x_tables(count):
    block = KY // count
    rows = NX // count
    stored = np.arange(NX)
    x_index = stored % rows * count + stored // rows
    frequency = np.arange(KX) - KX // 2
    angle = 2.0 * math.pi / NX * (frequency[:, None] * x_index[None, :] % NX)
    cosine = np.cos(angle) / math.sqrt(NX)
    sine = np.sin(angle) / math.sqrt(NX)
    table = np.stack([np.stack([cosine, sine], 1), np.stack([-sine, cosine], 1)])
    per = table.reshape(2, KX, 2, count, rows).transpose(3, 0, 1, 4, 2)
    spread = np.einsum("nojxr,ab->noajxrb", per, np.eye(block))
    spread = to_bf16(spread.reshape(count, 2 * block * KX, rows * 2 * block))
    return spread, np.ascontiguousarray(spread.transpose(0, 2, 1))


def dot(left, right):
    return lax.dot_general(left, right, (((1,), (0,)), ((), ())), preferred_element_type=F32)


def dot_nt(left, right):
    return lax.dot_general(left, right, (((1,), (1,)), ((), ())), preferred_element_type=F32)


def streamed(ref, buffer, sem, at, steps, axis, size):
    def copy(step):
        where = [slice(None)] * axis + [pl.ds(step % (KX // size) * size, size)]
        where[1] = pl.ds(step // (KX // size), 1)
        return pltpu.make_async_copy(ref.at[tuple(where)], buffer.at[step], sem.at[step])

    @pl.when(at == 0)
    def _():
        for step in range(steps):
            copy(step).start()

    copy(at).wait()
    return buffer.at[at]


def whole(shape):
    zeros = (0,) * len(shape)
    return pl.BlockSpec(shape, lambda *_: zeros)


def call(kernel, here, operands, grid, in_specs, out_specs, out_shape, scratch=(), flops=0, moved=0, name=None, aliases=None, limit=VMEM):
    return pl.pallas_call(
        kernel,
        out_shape=out_shape,
        grid_spec=pltpu.PrefetchScalarGridSpec(
            num_scalar_prefetch=1,
            grid=grid,
            in_specs=in_specs,
            out_specs=out_specs,
            scratch_shapes=list(scratch),
        ),
        compiler_params=pltpu.CompilerParams(
            dimension_semantics=("arbitrary",) * len(grid), vmem_limit_bytes=limit
        ),
        cost_estimate=pl.CostEstimate(flops=flops, bytes_accessed=moved, transcendentals=0),
        name=name,
        input_output_aliases=aliases or {},
    )(here, *operands)


def store_spectrum(here, parts, keep_ref, send_ref):
    chips, width, _ = keep_ref.shape
    unit = width // len(parts)
    half = chips * unit
    own_first = here[0] % 2 == 0
    kept = [jnp.where(own_first, part[:half], part[half:]) for part in parts]
    sent = [jnp.where(own_first, part[half:], part[:half]) for part in parts]
    for chip in range(chips):
        rows = slice(chip * unit, (chip + 1) * unit)
        keep_ref[chip] = jnp.concatenate([part[rows] for part in kept], 0).astype(BF16)
        send_ref[chip] = jnp.concatenate([part[rows] for part in sent], 0).astype(BF16)


def forward_y(count, here, field_hbm, keep_ref, send_ref, buffer, table, sem):
    step = pl.program_id(0)
    steps, size = buffer.shape[:2]

    def copy(at):
        return pltpu.make_async_copy(field_hbm.at[pl.ds(at * size, size)], buffer.at[at], sem.at[at])

    @pl.when(step == 0)
    def _():
        for at in range(steps):
            copy(at).start()
        block = KY // count
        row = lax.broadcasted_iota(jnp.int32, table.shape, 0)
        y = lax.broadcasted_iota(jnp.int32, table.shape, 1)
        core, chip = row // KY, row % KY // (2 * block)
        k = (2 * chip + core) * block + row % block
        turn = (k * y + row // block % 2 * (NY // 4)) % NY
        angle = (2.0 * math.pi / NY) * turn.astype(F32)
        table[...] = (jnp.cos(angle) * (1.0 / math.sqrt(NY))).astype(BF16)

    copy(step).wait()
    value = table[...]
    parts = [dot_nt(value, buffer[step, x]) for x in range(size)]
    store_spectrum(here, parts, keep_ref, send_ref)


def forward_x(here, keep_ref, got_ref, own_ref, other_ref, *outs):
    chip = here[0] // 2
    for step, out in enumerate(outs):
        at = chip ^ step
        out[...] = (dot(own_ref[0], keep_ref[at]) + dot(other_ref[0], got_ref[at])).astype(BF16)


def total(refs):
    values = [ref[...].astype(F32) for ref in refs]
    while len(values) > 1:
        values = [a + b for a, b in zip(values[::2], values[1::2])]
    return values[0].astype(BF16).astype(F32)


def half_sign(shape):
    lane = lax.broadcasted_iota(jnp.int32, shape, 1)
    return jnp.where(lane % 128 < 64, -1.0, 1.0)


def low_half(shape):
    return lax.broadcasted_iota(jnp.int32, shape, 1) < 64


def mix_forward(count, zs, here, *refs):
    terms, (w_hbm, out_ref, spread_ref, coeff, prod, buffer, sem) = refs[:count], refs[count:]
    step = pl.program_id(0)
    per = buffer.shape[3]
    modes = coeff.shape[0] // 2
    first = step * per
    w_ref = streamed(w_hbm, buffer, sem, step, buffer.shape[0], 2, per)

    @pl.when(first == 0)
    def _():
        coeff[...] = total(terms)

    shape = (2 * zs, zs * 64)
    row = lax.broadcasted_iota(jnp.int32, shape, 0)
    keep = lax.broadcasted_iota(jnp.int32, shape, 1) // 64 == row % zs
    is_real = row < zs
    for pair in range(per // 2):
        lefts, weights = [], []
        for sub in range(2):
            at = first + 2 * pair + sub
            real = jnp.broadcast_to(coeff[pl.ds(at, 1), :], shape)
            imag = jnp.broadcast_to(coeff[pl.ds(modes + at, 1), :], shape)
            lefts.append(jnp.where(keep, jnp.where(is_real, real, imag), 0.0))
            weights.append(w_ref[:, 0, 2 * pair + sub].reshape(zs * 64, 128))
        left = jnp.concatenate(lefts, 0).astype(BF16)
        base = pl.multiple_of((first + 2 * pair) * 2 * zs, 4 * zs)
        spread_ref[pl.ds(base, 4 * zs), :] = left
        got = dot(left, jnp.concatenate(weights, 1))
        prod[pl.ds(base, 2 * zs), :] = got[: 2 * zs, :128]
        prod[pl.ds(base + 2 * zs, 2 * zs), :] = got[2 * zs :, 128:]

    @pl.when(first + per == modes)
    def _():
        sign = half_sign((modes, 128))
        low = low_half((modes, 128))
        for tile in range(zs // 2):
            rows = []
            for z in (2 * tile, 2 * tile + 1):
                real = prod[pl.ds(z, modes, stride=2 * zs), :]
                imag = prod[pl.ds(zs + z, modes, stride=2 * zs), :]
                rows.append(real + sign * pltpu.roll(imag, 64, 1))
            lanes = slice(tile * 128, (tile + 1) * 128)
            out_ref[:modes, lanes] = jnp.where(low, rows[0], pltpu.roll(rows[1], 64, 1)).astype(BF16)
            out_ref[modes:, lanes] = jnp.where(low, pltpu.roll(rows[0], 64, 1), rows[1]).astype(BF16)


def mix_backward(count, zs, here, *refs):
    terms, locals_ = refs[:count], refs[count:-6]
    w_hbm, out_ref, pair_ref, prod, buffer, sem = refs[-6:]
    step = pl.program_id(0)
    per = buffer.shape[3]
    modes = prod.shape[1] // (2 * zs)
    first = step * per
    w_ref = streamed(w_hbm, buffer, sem, step, buffer.shape[0], 2, per)

    @pl.when(first == 0)
    def _():
        parts = [ref[...] for ref in locals_]
        while len(parts) > 1:
            parts = [a + b for a, b in zip(parts[::2], parts[1::2])]
        extra = 64 // zs
        value = jnp.concatenate([parts[0][at * extra : (at + 1) * extra] for at in range(zs)], 1)
        coarse = value.astype(BF16)
        out_ref[2 * modes : 2 * modes + extra] = coarse
        out_ref[2 * modes + extra :] = (value - coarse.astype(F32)).astype(BF16)
        grad = total(terms)
        sign = half_sign((modes, 128))
        low = low_half((modes, 128))
        for tile in range(zs // 2):
            lanes = slice(tile * 128, (tile + 1) * 128)
            real, imag = grad[:modes, lanes], grad[modes:, lanes]
            even = jnp.where(low, real, pltpu.roll(imag, 64, 1))
            odd = jnp.where(low, pltpu.roll(real, 64, 1), imag)
            for z, value in ((2 * tile, even), (2 * tile + 1, odd)):
                pair_ref[pl.ds(z, modes, stride=2 * zs), :] = value
                pair_ref[pl.ds(zs + z, modes, stride=2 * zs), :] = -sign * pltpu.roll(value, 64, 1)

    for mode in range(per):
        base = pl.multiple_of((first + mode) * 2 * zs, 2 * zs)
        left = pair_ref[pl.ds(base, 2 * zs), :].astype(BF16)
        got = dot_nt(left, w_ref[:, 0, mode].reshape(zs * 64, 128))
        for tile in range(zs // 2):
            prod[tile, pl.ds(base, 2 * zs), :] = got[:, tile * 128 : (tile + 1) * 128]

    @pl.when(first + per == modes)
    def _():
        low = low_half((modes, 128))
        for part in range(2):
            for tile in range(zs // 2):
                at = part * zs + 2 * tile
                even = prod[tile, pl.ds(at, modes, stride=2 * zs), :]
                odd = prod[tile, pl.ds(at + 1, modes, stride=2 * zs), :]
                out_ref[part * modes : (part + 1) * modes, tile * 128 : (tile + 1) * 128] = jnp.where(
                    low, even, odd
                ).astype(BF16)


def gram(zs, start, here, spread_ref, pair_ref, *refs):
    out_hbm, buffer, sem = refs[-3:]
    step = pl.program_id(0)
    steps, per = buffer.shape[0], buffer.shape[3]
    group = 4
    unit = 2 * zs
    first = (start + step) * per
    out_ref = buffer.at[step]
    shape = (group * unit, 128)
    owner = lax.broadcasted_iota(jnp.int32, shape, 0) // unit

    def copy(step):
        rows = pl.ds((start + step) * per // KX, 1)
        return pltpu.make_async_copy(
            buffer.at[step], out_hbm.at[:, rows, pl.ds((start + step) * per % KX, per)], sem.at[step]
        )

    for at in range(0, per, group):
        base = pl.multiple_of((first + at) * unit, group * unit)
        left = jnp.transpose(spread_ref[pl.ds(base, group * unit), :].astype(F32)).astype(BF16)
        grad = pair_ref[pl.ds(base, group * unit), :]
        right = jnp.concatenate([jnp.where(owner == t, grad, 0.0) for t in range(group)], 1)
        got = dot(left, right.astype(BF16))
        for t in range(group):
            out_ref[:, 0, at + t] = got[:, t * 128 : (t + 1) * 128].reshape(zs, 64, 128)
    copy(step).start()

    @pl.when(step == steps - 1)
    def _():
        for at in range(steps):
            copy(at).wait()


def grid_rows(here, blocks, x_ref, rows):
    chips = rows.shape[1]
    core, chip = here[0] % 2, here[0] // 2
    for slot, block in enumerate(blocks):
        at_core = core if slot < chips else 1 - core
        rows[at_core, chip ^ (slot % chips)] = dot(x_ref[0], block[...])


def row_at(rows, count, x):
    cores, chips, height, _ = rows.shape
    per = height // (pl.num_programs(0) * count)
    start = pl.multiple_of(pl.program_id(0) * (count * per), count * per)
    step = [rows[core, chip, pl.ds(start, count * per), :] for core in range(cores) for chip in range(chips)]
    joined = jnp.concatenate([value[x * per : (x + 1) * per] for value in step], 0)
    return jnp.transpose(joined).astype(BF16)


def middle(count, here, *refs):
    blocks, rest = refs[:count], refs[count:]
    x_ref, y_ref, weight_ref, field_ref, cot_ref = rest[:5]
    out_ref, grad_ref, keep_ref, send_ref, term_ref, rows, mixing, acc = rest[5:]
    step = pl.program_id(0)
    size = field_ref.shape[0]
    columns = field_ref.shape[1]
    zs = columns // 64

    @pl.when(step == 0)
    def _():
        grid_rows(here, blocks, x_ref, rows)
        mixing[...] = jnp.transpose(weight_ref[...].astype(F32)).astype(BF16)
        acc[...] = jnp.zeros_like(acc)

    table = y_ref[...]
    lefts = [row_at(rows, size, x) for x in range(size)]
    low = low_half((64, 128))
    parts, sums = [], []

    def reduce(x):
        got = dot_nt(jnp.concatenate([table, field_ref[x]], 0), grad_ref[x])
        parts.append(got[: 2 * KY])
        for tile in range(zs // 2):
            lanes = slice(tile * 128, (tile + 1) * 128)
            at = 2 * KY + tile * 128
            sums.append((lanes, jnp.where(low, got[at : at + 64, lanes], got[at + 64 : at + 128, lanes])))

    for x in range(size):
        for at in range(0, columns, 64):
            part = slice(at, at + 64)
            p = dot(lefts[x][part], table) + dot(mixing[...], field_ref[x, part])
            square = p * p
            t = jnp.tanh(p * (ROOT + ROOT * CUBE * square))
            half = 0.5 + 0.5 * t
            out_ref[x, part] = (p * half).astype(BF16)
            slope = half + p * (1.0 - t * t) * (0.5 * ROOT + 1.5 * ROOT * CUBE * square)
            grad_ref[x, part] = (cot_ref[x, part].astype(F32) * slope).astype(BF16)
        if x:
            reduce(x - 1)
    reduce(size - 1)
    store_spectrum(here, parts, keep_ref, send_ref)
    for lanes, value in sums:
        acc[:, lanes] += value

    @pl.when(step == pl.num_programs(0) - 1)
    def _():
        value = acc[...]
        parts = [value[:, at : at + 64] for at in range(0, columns, 64)]
        while len(parts) > 1:
            parts = [a + b for a, b in zip(parts[::2], parts[1::2])]
        term_ref[...] = parts[0]


def last(count, scale, here, *refs):
    blocks, rest = refs[:count], refs[count:]
    x_ref, y_ref, weight_ref, grad_ref, out_ref, local_ref, rows = rest
    columns = grad_ref.shape[1]
    size = grad_ref.shape[0]

    @pl.when(pl.program_id(0) == 0)
    def _():
        height = x_ref.shape[2]
        extra = 64 * 64 // columns
        grid_rows(here, [block.at[pl.ds(0, height)] for block in blocks], x_ref, rows)
        parts = [
            block[pl.ds(height, extra), :].astype(F32) + block[pl.ds(height + extra, extra), :].astype(F32)
            for block in blocks
        ]
        while len(parts) > 1:
            parts = [a + b for a, b in zip(parts[::2], parts[1::2])]
        for at in range(columns // 64):
            local_ref[at * extra : (at + 1) * extra, :] = parts[0][:, at * 64 : (at + 1) * 64] * scale

    table = y_ref[...]
    weight = weight_ref[...]
    lefts = [row_at(rows, size, x) for x in range(size)]
    for x in range(size):
        for at in range(0, columns, 64):
            part = slice(at, at + 64)
            value = dot(lefts[x][part], table) + dot(weight, grad_ref[x, part])
            out_ref[x, part] = value.astype(BF16)


def flip(axis, size, bit):
    return functools.partial(lax.ppermute, axis_name=axis, perm=[(at, at ^ bit) for at in range(size)])


def body(features, out_grad, spectral_weight, local_weight):
    count = lax.axis_size("mp")
    dp_count = lax.axis_size("dp")
    chips = count // 2
    rows_here, grid_y, snaps, zs, channels = features.shape
    mode_rows = spectral_weight.shape[1]
    columns = snaps * zs * channels
    modes = mode_rows * KX
    unit = 2 * mode_rows
    here = lax.axis_index("mp").astype(jnp.int32).reshape(1)

    y_plain, y_weighted = y_tables(count)
    x_forward, x_back = x_tables(count)

    def inner(array):
        return jnp.transpose(array, (0, 2, 3, 4, 1)).reshape(rows_here, columns, grid_y)

    def outer(array):
        shaped = array.reshape(rows_here, snaps, zs, channels, grid_y)
        return jnp.transpose(shaped, (0, 4, 1, 2, 3))

    field, cot = inner(features), inner(out_grad)
    wide, chunk = min(16, rows_here), min(8, rows_here)

    def field_spec(size):
        return pl.BlockSpec((size, columns, grid_y), lambda g, _: (g, 0, 0))

    def half_spec(size):
        return pl.BlockSpec((chips, size * unit, columns), lambda g, _: (0, g, 0))

    field_shape = jax.ShapeDtypeStruct((rows_here, columns, grid_y), BF16)
    half_shape = jax.ShapeDtypeStruct((chips, rows_here * unit, columns), BF16)
    y_spec = whole((2 * KY, grid_y))
    mode_shape = jax.ShapeDtypeStruct((2 * modes, columns), BF16)
    mode_spec = whole((2 * modes, columns))
    weight_small = whole((channels, channels))
    small_shape = jax.ShapeDtypeStruct((channels, channels), F32)
    mixing_scratch = pltpu.VMEM((channels, channels), BF16)
    extra = 2 * channels * channels // columns
    back_spec = whole((2 * modes + extra, columns))
    back_shape = jax.ShapeDtypeStruct((2 * modes + extra, columns), BF16)
    field_bytes = rows_here * columns * grid_y * 2
    mode_bytes = 4 * modes * columns

    def to_chips(keep, send, beside=None):
        got = flip("mp", count, 1)(send)
        x_spec = (1, 2 * modes, rows_here * unit)
        outs = call(
            forward_x,
            here,
            (keep, got, x_forward, x_forward),
            (1,),
            [
                whole(keep.shape),
                whole(keep.shape),
                pl.BlockSpec(x_spec, lambda g, m: (m[0], 0, 0)),
                pl.BlockSpec(x_spec, lambda g, m: (m[0] ^ 1, 0, 0)),
            ],
            [mode_spec] * chips,
            [mode_shape] * chips,
            flops=8 * chips * modes * rows_here * unit * columns,
            moved=mode_bytes * 3 * chips,
            name="forward_x",
            limit=8 << 20,
        )
        outs = list(outs)
        if beside is not None:
            outs[-1], beside = lax.optimization_barrier((outs[-1], beside))
        return [outs[0]] + [flip("mp", count, 2 * bit)(outs[bit]) for bit in range(1, chips)], beside

    def to_all(block):
        mine = [block] + [flip("mp", count, 2 * bit)(block) for bit in range(1, chips)]
        return mine + [flip("mp", count, 1)(value) for value in mine]

    per = 16
    mode_steps = modes // per
    weight_spec = pl.BlockSpec(memory_space=pl.ANY)
    weight_scratch = [
        pltpu.VMEM((mode_steps, zs, 1, per, channels, 2 * channels), BF16),
        pltpu.SemaphoreType.DMA((mode_steps,)),
    ]
    spread_shape = (modes * 2 * zs, columns)
    pair_shape = (modes * 2 * zs, 2 * channels)
    weight_bytes = zs * modes * channels * 2 * channels * 2

    keep, send = call(
        functools.partial(forward_y, count),
        here,
        (field,),
        (rows_here // chunk,),
        [pl.BlockSpec(memory_space=pltpu.HBM)],
        [half_spec(chunk)] * 2,
        [half_shape] * 2,
        [
            pltpu.VMEM((rows_here // chunk, chunk, columns, grid_y), BF16),
            pltpu.VMEM((2 * KY, grid_y), BF16),
            pltpu.SemaphoreType.DMA((rows_here // chunk,)),
        ],
        flops=field_bytes * 2 * KY,
        moved=field_bytes + mode_bytes * count,
        name="forward_y",
    )
    terms, _ = to_chips(keep, send)
    mixed, spread = call(
        functools.partial(mix_forward, chips, zs),
        here,
        (*terms, spectral_weight),
        (mode_steps,),
        [mode_spec] * chips + [weight_spec],
        [mode_spec, whole(spread_shape)],
        [mode_shape, jax.ShapeDtypeStruct(spread_shape, BF16)],
        [pltpu.VMEM((2 * modes, columns), F32), pltpu.VMEM(pair_shape, F32)] + weight_scratch,
        flops=weight_bytes * 8,
        moved=weight_bytes + mode_bytes * chips,
        name="mix_forward",
    )
    blocks = to_all(mixed)
    x_back_spec = pl.BlockSpec((1, rows_here * unit, 2 * modes), lambda g, m: (m[0], 0, 0))
    rows_scratch = pltpu.VMEM((2, chips, rows_here * unit, columns), F32)
    output, preact_grad, keep, send, local_term = call(
        functools.partial(middle, count),
        here,
        (*blocks, x_back, y_weighted, local_weight, field, cot),
        (rows_here // chunk,),
        [mode_spec] * count + [x_back_spec, y_spec, weight_small] + [field_spec(chunk)] * 2,
        [field_spec(chunk)] * 2 + [half_spec(chunk)] * 2 + [weight_small],
        [field_shape, field_shape, half_shape, half_shape, small_shape],
        [rows_scratch, mixing_scratch, pltpu.VMEM((channels, columns), F32)],
        flops=field_bytes * (4 * KY + 2 * columns),
        moved=field_bytes * 4 + mode_bytes * count * 2,
        name="middle",
    )
    first_got = flip("dp", dp_count, 1)(local_term) if dp_count > 1 else jnp.zeros_like(local_term)
    terms, first_got = to_chips(keep, send, first_got)
    locals_, bit = [local_term, first_got], 2
    while bit < dp_count:
        local_term = locals_[0] + locals_[1]
        locals_ = [local_term, flip("dp", dp_count, bit)(local_term)]
        bit *= 2
    back, pairs = call(
        functools.partial(mix_backward, chips, zs),
        here,
        (*terms, *locals_, spectral_weight),
        (mode_steps,),
        [mode_spec] * chips + [weight_small] * len(locals_) + [weight_spec],
        [back_spec, whole(pair_shape)],
        [back_shape, jax.ShapeDtypeStruct(pair_shape, F32)],
        [pltpu.VMEM((zs // 2, modes * 2 * zs, 128), F32)] + weight_scratch,
        flops=weight_bytes * 8,
        moved=weight_bytes + mode_bytes * chips,
        name="mix_backward",
    )
    gram_steps = modes // 8
    early = gram_steps * 3 // 4

    def gram_part(start, steps, before):
        per = 8
        return call(
            functools.partial(gram, zs, start),
            here,
            (spread, pairs, *before),
            (steps,),
            [whole(spread_shape), whole(pair_shape)] + [pl.BlockSpec(memory_space=pl.ANY)] * len(before),
            pl.BlockSpec(memory_space=pl.ANY),
            jax.ShapeDtypeStruct(spectral_weight.shape, F32),
            [
                pltpu.VMEM((steps, zs, 1, per, channels, 2 * channels), F32),
                pltpu.SemaphoreType.DMA((steps,)),
            ],
            flops=weight_bytes * 4,
            moved=weight_bytes,
            name="gram",
            aliases={3: 0} if before else {},
        )

    mine = [back] + [flip("mp", count, 2 * bit)(back) for bit in range(1, chips)]
    spectral_grad = gram_part(0, early, ())
    *others, spectral_grad = lax.optimization_barrier((*mine[1:], spectral_grad))
    blocks = [back, *others] + [flip("mp", count, 1)(value) for value in (back, *others)]
    spectral_grad = gram_part(early, gram_steps - early, (spectral_grad,))
    scale = 1.0 / math.sqrt(NX * NY * snaps * dp_count * zs)
    back_field, local_grad = call(
        functools.partial(last, count, scale),
        here,
        (*blocks, x_back, y_plain, local_weight, preact_grad),
        (rows_here // wide,),
        [back_spec] * count + [x_back_spec, y_spec, weight_small, field_spec(wide)],
        [field_spec(wide), weight_small],
        [field_shape, small_shape],
        [rows_scratch],
        flops=field_bytes * (2 * KY + columns),
        moved=field_bytes * 2 + mode_bytes * count,
        name="last",
    )
    return (outer(output), outer(back_field), spectral_grad, local_grad)


def solution(mesh):
    placed = (
        P("mp", None, None, "dp", None),
        P("mp", None, None, "dp", None),
        P("dp", "mp", None, None, None),
        P(),
    )
    return jax.shard_map(
        body,
        mesh=mesh,
        in_specs=placed,
        out_specs=(
            P("mp", None, None, "dp", None),
            P("mp", None, None, "dp", None),
            P("dp", "mp", None, None, None),
            P(),
        ),
        check_vma=False,
    )
```

```python
import functools
import math

import jax
import jax.numpy as jnp
import ml_dtypes
import numpy as np
from jax import lax
from jax.experimental import pallas as pl
from jax.experimental.pallas import tpu as pltpu
from jax.sharding import PartitionSpec as P

NX = 256
NY = 256
KX = 32
KY = 32
F32 = jnp.float32
BF16 = jnp.bfloat16
ROOT = math.sqrt(2.0 / math.pi)
CUBE = 0.044715
VMEM = 52 << 20


def to_bf16(values):
    return values.astype(np.float32).astype(ml_dtypes.bfloat16)


def y_tables(count):
    block = KY // count
    k_index = np.arange(KY)
    angle = 2.0 * math.pi / NY * (k_index[:, None] * np.arange(NY)[None, :] % NY)
    table = to_bf16(np.stack([np.cos(angle), -np.sin(angle)]) / math.sqrt(NY)).astype(np.float32)
    weight = np.where(k_index == 0, 1.0, 2.0)[None, :, None]

    def ordered(values):
        shaped = values.reshape(2, count // 2, 2, block, NY).transpose(2, 1, 0, 3, 4)
        return to_bf16(shaped.reshape(2 * KY, NY))

    return ordered(table), ordered(table * weight)


def x_tables(count):
    block = KY // count
    rows = NX // count
    stored = np.arange(NX)
    x_index = stored % rows * count + stored // rows
    frequency = np.arange(KX) - KX // 2
    angle = 2.0 * math.pi / NX * (frequency[:, None] * x_index[None, :] % NX)
    cosine = np.cos(angle) / math.sqrt(NX)
    sine = np.sin(angle) / math.sqrt(NX)
    table = np.stack([np.stack([cosine, sine], 1), np.stack([-sine, cosine], 1)])
    per = table.reshape(2, KX, 2, count, rows).transpose(3, 0, 1, 4, 2)
    spread = np.einsum("nojxr,ab->noajxrb", per, np.eye(block))
    spread = to_bf16(spread.reshape(count, 2 * block * KX, rows * 2 * block))
    return spread, np.ascontiguousarray(spread.transpose(0, 2, 1))


def dot(left, right):
    return lax.dot_general(left, right, (((1,), (0,)), ((), ())), preferred_element_type=F32)


def dot_nt(left, right):
    return lax.dot_general(left, right, (((1,), (1,)), ((), ())), preferred_element_type=F32)


def streamed(ref, buffer, sem, at, steps, axis, size):
    def copy(step):
        where = [slice(None)] * axis + [pl.ds(step % (KX // size) * size, size)]
        where[1] = pl.ds(step // (KX // size), 1)
        return pltpu.make_async_copy(ref.at[tuple(where)], buffer.at[step], sem.at[step])

    @pl.when(at == 0)
    def _():
        for step in range(steps):
            copy(step).start()

    copy(at).wait()
    return buffer.at[at]


def whole(shape):
    zeros = (0,) * len(shape)
    return pl.BlockSpec(shape, lambda *_: zeros)


def call(kernel, here, operands, grid, in_specs, out_specs, out_shape, scratch=(), flops=0, moved=0, name=None, aliases=None, limit=VMEM):
    return pl.pallas_call(
        kernel,
        out_shape=out_shape,
        grid_spec=pltpu.PrefetchScalarGridSpec(
            num_scalar_prefetch=1,
            grid=grid,
            in_specs=in_specs,
            out_specs=out_specs,
            scratch_shapes=list(scratch),
        ),
        compiler_params=pltpu.CompilerParams(
            dimension_semantics=("arbitrary",) * len(grid), vmem_limit_bytes=limit
        ),
        cost_estimate=pl.CostEstimate(flops=flops, bytes_accessed=moved, transcendentals=0),
        name=name,
        input_output_aliases=aliases or {},
    )(here, *operands)


def store_spectrum(here, parts, keep_ref, send_ref):
    chips, width, _ = keep_ref.shape
    unit = width // len(parts)
    half = chips * unit
    own_first = here[0] % 2 == 0
    kept = [jnp.where(own_first, part[:half], part[half:]) for part in parts]
    sent = [jnp.where(own_first, part[half:], part[:half]) for part in parts]
    for chip in range(chips):
        rows = slice(chip * unit, (chip + 1) * unit)
        keep_ref[chip] = jnp.concatenate([part[rows] for part in kept], 0).astype(BF16)
        send_ref[chip] = jnp.concatenate([part[rows] for part in sent], 0).astype(BF16)


def forward_y(count, here, field_hbm, keep_ref, send_ref, buffer, table, sem):
    step = pl.program_id(0)
    steps, size = buffer.shape[:2]

    def copy(at):
        return pltpu.make_async_copy(field_hbm.at[pl.ds(at * size, size)], buffer.at[at], sem.at[at])

    @pl.when(step == 0)
    def _():
        for at in range(steps):
            copy(at).start()
        block = KY // count
        row = lax.broadcasted_iota(jnp.int32, table.shape, 0)
        y = lax.broadcasted_iota(jnp.int32, table.shape, 1)
        core, chip = row // KY, row % KY // (2 * block)
        k = (2 * chip + core) * block + row % block
        turn = (k * y + row // block % 2 * (NY // 4)) % NY
        angle = (2.0 * math.pi / NY) * turn.astype(F32)
        table[...] = (jnp.cos(angle) * (1.0 / math.sqrt(NY))).astype(BF16)

    copy(step).wait()
    value = table[...]
    parts = [dot_nt(value, buffer[step, x]) for x in range(size)]
    store_spectrum(here, parts, keep_ref, send_ref)


def forward_x(here, keep_ref, got_ref, own_ref, other_ref, *outs):
    chip = here[0] // 2
    for step, out in enumerate(outs):
        at = chip ^ step
        out[...] = (dot(own_ref[0], keep_ref[at]) + dot(other_ref[0], got_ref[at])).astype(BF16)


def total(refs):
    values = [ref[...].astype(F32) for ref in refs]
    while len(values) > 1:
        values = [a + b for a, b in zip(values[::2], values[1::2])]
    return values[0].astype(BF16).astype(F32)


def half_sign(shape):
    lane = lax.broadcasted_iota(jnp.int32, shape, 1)
    return jnp.where(lane % 128 < 64, -1.0, 1.0)


def low_half(shape):
    return lax.broadcasted_iota(jnp.int32, shape, 1) < 64


def mix_forward(count, zs, here, *refs):
    terms, (w_hbm, out_ref, spread_ref, coeff, prod, buffer, sem) = refs[:count], refs[count:]
    step = pl.program_id(0)
    per = buffer.shape[3]
    modes = coeff.shape[0] // 2
    first = step * per
    w_ref = streamed(w_hbm, buffer, sem, step, buffer.shape[0], 2, per)

    @pl.when(first == 0)
    def _():
        coeff[...] = total(terms)

    shape = (2 * zs, zs * 64)
    row = lax.broadcasted_iota(jnp.int32, shape, 0)
    keep = lax.broadcasted_iota(jnp.int32, shape, 1) // 64 == row % zs
    is_real = row < zs
    for pair in range(per // 2):
        lefts, weights = [], []
        for sub in range(2):
            at = first + 2 * pair + sub
            real = jnp.broadcast_to(coeff[pl.ds(at, 1), :], shape)
            imag = jnp.broadcast_to(coeff[pl.ds(modes + at, 1), :], shape)
            lefts.append(jnp.where(keep, jnp.where(is_real, real, imag), 0.0))
            weights.append(w_ref[:, 0, 2 * pair + sub].reshape(zs * 64, 128))
        left = jnp.concatenate(lefts, 0).astype(BF16)
        base = pl.multiple_of((first + 2 * pair) * 2 * zs, 4 * zs)
        spread_ref[pl.ds(base, 4 * zs), :] = left
        got = dot(left, jnp.concatenate(weights, 1))
        prod[pl.ds(base, 2 * zs), :] = got[: 2 * zs, :128]
        prod[pl.ds(base + 2 * zs, 2 * zs), :] = got[2 * zs :, 128:]

    @pl.when(first + per == modes)
    def _():
        sign = half_sign((modes, 128))
        low = low_half((modes, 128))
        for tile in range(zs // 2):
            rows = []
            for z in (2 * tile, 2 * tile + 1):
                real = prod[pl.ds(z, modes, stride=2 * zs), :]
                imag = prod[pl.ds(zs + z, modes, stride=2 * zs), :]
                rows.append(real + sign * pltpu.roll(imag, 64, 1))
            lanes = slice(tile * 128, (tile + 1) * 128)
            out_ref[:modes, lanes] = jnp.where(low, rows[0], pltpu.roll(rows[1], 64, 1)).astype(BF16)
            out_ref[modes:, lanes] = jnp.where(low, pltpu.roll(rows[0], 64, 1), rows[1]).astype(BF16)


def mix_backward(count, zs, here, *refs):
    terms, locals_ = refs[:count], refs[count:-6]
    w_hbm, out_ref, pair_ref, prod, buffer, sem = refs[-6:]
    step = pl.program_id(0)
    per = buffer.shape[3]
    modes = prod.shape[1] // (2 * zs)
    first = step * per
    w_ref = streamed(w_hbm, buffer, sem, step, buffer.shape[0], 2, per)

    @pl.when(first == 0)
    def _():
        parts = [ref[...] for ref in locals_]
        while len(parts) > 1:
            parts = [a + b for a, b in zip(parts[::2], parts[1::2])]
        extra = 64 // zs
        value = jnp.concatenate([parts[0][at * extra : (at + 1) * extra] for at in range(zs)], 1)
        coarse = value.astype(BF16)
        out_ref[2 * modes : 2 * modes + extra] = coarse
        out_ref[2 * modes + extra :] = (value - coarse.astype(F32)).astype(BF16)
        grad = total(terms)
        sign = half_sign((modes, 128))
        low = low_half((modes, 128))
        for tile in range(zs // 2):
            lanes = slice(tile * 128, (tile + 1) * 128)
            real, imag = grad[:modes, lanes], grad[modes:, lanes]
            even = jnp.where(low, real, pltpu.roll(imag, 64, 1))
            odd = jnp.where(low, pltpu.roll(real, 64, 1), imag)
            for z, value in ((2 * tile, even), (2 * tile + 1, odd)):
                pair_ref[pl.ds(z, modes, stride=2 * zs), :] = value
                pair_ref[pl.ds(zs + z, modes, stride=2 * zs), :] = -sign * pltpu.roll(value, 64, 1)

    for mode in range(per):
        base = pl.multiple_of((first + mode) * 2 * zs, 2 * zs)
        left = pair_ref[pl.ds(base, 2 * zs), :].astype(BF16)
        got = dot_nt(left, w_ref[:, 0, mode].reshape(zs * 64, 128))
        for tile in range(zs // 2):
            prod[tile, pl.ds(base, 2 * zs), :] = got[:, tile * 128 : (tile + 1) * 128]

    @pl.when(first + per == modes)
    def _():
        low = low_half((modes, 128))
        for part in range(2):
            for tile in range(zs // 2):
                at = part * zs + 2 * tile
                even = prod[tile, pl.ds(at, modes, stride=2 * zs), :]
                odd = prod[tile, pl.ds(at + 1, modes, stride=2 * zs), :]
                out_ref[part * modes : (part + 1) * modes, tile * 128 : (tile + 1) * 128] = jnp.where(
                    low, even, odd
                ).astype(BF16)


def gram(zs, start, here, spread_ref, pair_ref, *refs):
    out_hbm, buffer, sem = refs[-3:]
    step = pl.program_id(0)
    steps, per = buffer.shape[0], buffer.shape[3]
    group = 4
    unit = 2 * zs
    first = (start + step) * per
    out_ref = buffer.at[step]
    shape = (group * unit, 128)
    owner = lax.broadcasted_iota(jnp.int32, shape, 0) // unit

    def copy(step):
        rows = pl.ds((start + step) * per // KX, 1)
        return pltpu.make_async_copy(
            buffer.at[step], out_hbm.at[:, rows, pl.ds((start + step) * per % KX, per)], sem.at[step]
        )

    for at in range(0, per, group):
        base = pl.multiple_of((first + at) * unit, group * unit)
        left = jnp.transpose(spread_ref[pl.ds(base, group * unit), :].astype(F32)).astype(BF16)
        grad = pair_ref[pl.ds(base, group * unit), :]
        right = jnp.concatenate([jnp.where(owner == t, grad, 0.0) for t in range(group)], 1)
        got = dot(left, right.astype(BF16))
        for t in range(group):
            out_ref[:, 0, at + t] = got[:, t * 128 : (t + 1) * 128].reshape(zs, 64, 128)
    copy(step).start()

    @pl.when(step == steps - 1)
    def _():
        for at in range(steps):
            copy(at).wait()


def grid_rows(here, blocks, x_ref, rows):
    chips = rows.shape[1]
    core, chip = here[0] % 2, here[0] // 2
    for slot, block in enumerate(blocks):
        at_core = core if slot < chips else 1 - core
        rows[at_core, chip ^ (slot % chips)] = dot(x_ref[0], block[...])


def row_at(rows, count, x):
    cores, chips, height, _ = rows.shape
    per = height // (pl.num_programs(0) * count)
    start = pl.multiple_of(pl.program_id(0) * (count * per), count * per)
    step = [rows[core, chip, pl.ds(start, count * per), :] for core in range(cores) for chip in range(chips)]
    joined = jnp.concatenate([value[x * per : (x + 1) * per] for value in step], 0)
    return jnp.transpose(joined).astype(BF16)


def middle(count, here, *refs):
    blocks, rest = refs[:count], refs[count:]
    x_ref, y_ref, weight_ref, field_ref, cot_ref = rest[:5]
    out_ref, grad_ref, keep_ref, send_ref, term_ref, rows, mixing, acc = rest[5:]
    step = pl.program_id(0)
    size = field_ref.shape[0]
    columns = field_ref.shape[1]
    zs = columns // 64

    @pl.when(step == 0)
    def _():
        grid_rows(here, blocks, x_ref, rows)
        mixing[...] = jnp.transpose(weight_ref[...].astype(F32)).astype(BF16)
        acc[...] = jnp.zeros_like(acc)

    table = y_ref[...]
    lefts = [row_at(rows, size, x) for x in range(size)]
    low = low_half((64, 128))
    parts, sums = [], []

    def reduce(x):
        got = dot_nt(jnp.concatenate([table, field_ref[x]], 0), grad_ref[x])
        parts.append(got[: 2 * KY])
        for tile in range(zs // 2):
            lanes = slice(tile * 128, (tile + 1) * 128)
            at = 2 * KY + tile * 128
            sums.append((lanes, jnp.where(low, got[at : at + 64, lanes], got[at + 64 : at + 128, lanes])))

    for x in range(size):
        for at in range(0, columns, 64):
            part = slice(at, at + 64)
            p = dot(lefts[x][part], table) + dot(mixing[...], field_ref[x, part])
            square = p * p
            t = jnp.tanh(p * (ROOT + ROOT * CUBE * square))
            half = 0.5 + 0.5 * t
            out_ref[x, part] = (p * half).astype(BF16)
            slope = half + p * (1.0 - t * t) * (0.5 * ROOT + 1.5 * ROOT * CUBE * square)
            grad_ref[x, part] = (cot_ref[x, part].astype(F32) * slope).astype(BF16)
        if x:
            reduce(x - 1)
    reduce(size - 1)
    store_spectrum(here, parts, keep_ref, send_ref)
    for lanes, value in sums:
        acc[:, lanes] += value

    @pl.when(step == pl.num_programs(0) - 1)
    def _():
        value = acc[...]
        parts = [value[:, at : at + 64] for at in range(0, columns, 64)]
        while len(parts) > 1:
            parts = [a + b for a, b in zip(parts[::2], parts[1::2])]
        term_ref[...] = parts[0]


def last(count, scale, here, *refs):
    blocks, rest = refs[:count], refs[count:]
    x_ref, y_ref, weight_ref, grad_ref, out_ref, local_ref, rows = rest
    columns = grad_ref.shape[1]
    size = grad_ref.shape[0]

    @pl.when(pl.program_id(0) == 0)
    def _():
        height = x_ref.shape[2]
        extra = 64 * 64 // columns
        grid_rows(here, [block.at[pl.ds(0, height)] for block in blocks], x_ref, rows)
        parts = [
            block[pl.ds(height, extra), :].astype(F32) + block[pl.ds(height + extra, extra), :].astype(F32)
            for block in blocks
        ]
        while len(parts) > 1:
            parts = [a + b for a, b in zip(parts[::2], parts[1::2])]
        for at in range(columns // 64):
            local_ref[at * extra : (at + 1) * extra, :] = parts[0][:, at * 64 : (at + 1) * 64] * scale

    table = y_ref[...]
    weight = weight_ref[...]
    lefts = [row_at(rows, size, x) for x in range(size)]
    for x in range(size):
        for at in range(0, columns, 64):
            part = slice(at, at + 64)
            value = dot(lefts[x][part], table) + dot(weight, grad_ref[x, part])
            out_ref[x, part] = value.astype(BF16)


def flip(axis, size, bit):
    return functools.partial(lax.ppermute, axis_name=axis, perm=[(at, at ^ bit) for at in range(size)])


def body(features, out_grad, spectral_weight, local_weight):
    count = lax.axis_size("mp")
    dp_count = lax.axis_size("dp")
    chips = count // 2
    rows_here, grid_y, snaps, zs, channels = features.shape
    mode_rows = spectral_weight.shape[1]
    columns = snaps * zs * channels
    modes = mode_rows * KX
    unit = 2 * mode_rows
    here = lax.axis_index("mp").astype(jnp.int32).reshape(1)

    y_plain, y_weighted = y_tables(count)
    x_forward, x_back = x_tables(count)

    def inner(array):
        return jnp.transpose(array, (0, 2, 3, 4, 1)).reshape(rows_here, columns, grid_y)

    def outer(array):
        shaped = array.reshape(rows_here, snaps, zs, channels, grid_y)
        return jnp.transpose(shaped, (0, 4, 1, 2, 3))

    field, cot = inner(features), inner(out_grad)
    wide, chunk = min(16, rows_here), min(8, rows_here)

    def field_spec(size):
        return pl.BlockSpec((size, columns, grid_y), lambda g, _: (g, 0, 0))

    def half_spec(size):
        return pl.BlockSpec((chips, size * unit, columns), lambda g, _: (0, g, 0))

    field_shape = jax.ShapeDtypeStruct((rows_here, columns, grid_y), BF16)
    half_shape = jax.ShapeDtypeStruct((chips, rows_here * unit, columns), BF16)
    y_spec = whole((2 * KY, grid_y))
    mode_shape = jax.ShapeDtypeStruct((2 * modes, columns), BF16)
    mode_spec = whole((2 * modes, columns))
    weight_small = whole((channels, channels))
    small_shape = jax.ShapeDtypeStruct((channels, channels), F32)
    mixing_scratch = pltpu.VMEM((channels, channels), BF16)
    extra = 2 * channels * channels // columns
    back_spec = whole((2 * modes + extra, columns))
    back_shape = jax.ShapeDtypeStruct((2 * modes + extra, columns), BF16)
    field_bytes = rows_here * columns * grid_y * 2
    mode_bytes = 4 * modes * columns

    def to_chips(keep, send, beside=None):
        got = flip("mp", count, 1)(send)
        x_spec = (1, 2 * modes, rows_here * unit)
        outs = call(
            forward_x,
            here,
            (keep, got, x_forward, x_forward),
            (1,),
            [
                whole(keep.shape),
                whole(keep.shape),
                pl.BlockSpec(x_spec, lambda g, m: (m[0], 0, 0)),
                pl.BlockSpec(x_spec, lambda g, m: (m[0] ^ 1, 0, 0)),
            ],
            [mode_spec] * chips,
            [mode_shape] * chips,
            flops=8 * chips * modes * rows_here * unit * columns,
            moved=mode_bytes * 3 * chips,
            name="forward_x",
            limit=8 << 20,
        )
        outs = list(outs)
        if beside is not None:
            outs[-1], beside = lax.optimization_barrier((outs[-1], beside))
        return [outs[0]] + [flip("mp", count, 2 * bit)(outs[bit]) for bit in range(1, chips)], beside

    def to_all(block):
        mine = [block] + [flip("mp", count, 2 * bit)(block) for bit in range(1, chips)]
        return mine + [flip("mp", count, 1)(value) for value in mine]

    per = 16
    mode_steps = modes // per
    weight_spec = pl.BlockSpec(memory_space=pl.ANY)
    weight_scratch = [
        pltpu.VMEM((mode_steps, zs, 1, per, channels, 2 * channels), BF16),
        pltpu.SemaphoreType.DMA((mode_steps,)),
    ]
    spread_shape = (modes * 2 * zs, columns)
    pair_shape = (modes * 2 * zs, 2 * channels)
    weight_bytes = zs * modes * channels * 2 * channels * 2

    keep, send = call(
        functools.partial(forward_y, count),
        here,
        (field,),
        (rows_here // chunk,),
        [pl.BlockSpec(memory_space=pltpu.HBM)],
        [half_spec(chunk)] * 2,
        [half_shape] * 2,
        [
            pltpu.VMEM((rows_here // chunk, chunk, columns, grid_y), BF16),
            pltpu.VMEM((2 * KY, grid_y), BF16),
            pltpu.SemaphoreType.DMA((rows_here // chunk,)),
        ],
        flops=field_bytes * 2 * KY,
        moved=field_bytes + mode_bytes * count,
        name="forward_y",
    )
    terms, _ = to_chips(keep, send)
    mixed, spread = call(
        functools.partial(mix_forward, chips, zs),
        here,
        (*terms, spectral_weight),
        (mode_steps,),
        [mode_spec] * chips + [weight_spec],
        [mode_spec, whole(spread_shape)],
        [mode_shape, jax.ShapeDtypeStruct(spread_shape, BF16)],
        [pltpu.VMEM((2 * modes, columns), F32), pltpu.VMEM(pair_shape, F32)] + weight_scratch,
        flops=weight_bytes * 8,
        moved=weight_bytes + mode_bytes * chips,
        name="mix_forward",
    )
    blocks = to_all(mixed)
    x_back_spec = pl.BlockSpec((1, rows_here * unit, 2 * modes), lambda g, m: (m[0], 0, 0))
    rows_scratch = pltpu.VMEM((2, chips, rows_here * unit, columns), F32)
    output, preact_grad, keep, send, local_term = call(
        functools.partial(middle, count),
        here,
        (*blocks, x_back, y_weighted, local_weight, field, cot),
        (rows_here // chunk,),
        [mode_spec] * count + [x_back_spec, y_spec, weight_small] + [field_spec(chunk)] * 2,
        [field_spec(chunk)] * 2 + [half_spec(chunk)] * 2 + [weight_small],
        [field_shape, field_shape, half_shape, half_shape, small_shape],
        [rows_scratch, mixing_scratch, pltpu.VMEM((channels, columns), F32)],
        flops=field_bytes * (4 * KY + 2 * columns),
        moved=field_bytes * 4 + mode_bytes * count * 2,
        name="middle",
    )
    first_got = flip("dp", dp_count, 1)(local_term) if dp_count > 1 else jnp.zeros_like(local_term)
    terms, first_got = to_chips(keep, send, first_got)
    locals_, bit = [local_term, first_got], 2
    while bit < dp_count:
        local_term = locals_[0] + locals_[1]
        locals_ = [local_term, flip("dp", dp_count, bit)(local_term)]
        bit *= 2
    back, pairs = call(
        functools.partial(mix_backward, chips, zs),
        here,
        (*terms, *locals_, spectral_weight),
        (mode_steps,),
        [mode_spec] * chips + [weight_small] * len(locals_) + [weight_spec],
        [back_spec, whole(pair_shape)],
        [back_shape, jax.ShapeDtypeStruct(pair_shape, F32)],
        [pltpu.VMEM((zs // 2, modes * 2 * zs, 128), F32)] + weight_scratch,
        flops=weight_bytes * 8,
        moved=weight_bytes + mode_bytes * chips,
        name="mix_backward",
        limit=24 << 20,
    )
    gram_steps = modes // 8
    early = gram_steps * 3 // 4

    def gram_part(start, steps, before):
        per = 8
        return call(
            functools.partial(gram, zs, start),
            here,
            (spread, pairs, *before),
            (steps,),
            [whole(spread_shape), whole(pair_shape)] + [pl.BlockSpec(memory_space=pl.ANY)] * len(before),
            pl.BlockSpec(memory_space=pl.ANY),
            jax.ShapeDtypeStruct(spectral_weight.shape, F32),
            [
                pltpu.VMEM((steps, zs, 1, per, channels, 2 * channels), F32),
                pltpu.SemaphoreType.DMA((steps,)),
            ],
            flops=weight_bytes * 4,
            moved=weight_bytes,
            name="gram",
            aliases={3: 0} if before else {},
        )

    mine = [back] + [flip("mp", count, 2 * bit)(back) for bit in range(1, chips)]
    spectral_grad = gram_part(0, early, ())
    *others, spectral_grad = lax.optimization_barrier((*mine[1:], spectral_grad))
    blocks = [back, *others] + [flip("mp", count, 1)(value) for value in (back, *others)]
    spectral_grad = gram_part(early, gram_steps - early, (spectral_grad,))
    scale = 1.0 / math.sqrt(NX * NY * snaps * dp_count * zs)
    back_field, local_grad = call(
        functools.partial(last, count, scale),
        here,
        (*blocks, x_back, y_plain, local_weight, preact_grad),
        (rows_here // wide,),
        [back_spec] * count + [x_back_spec, y_spec, weight_small, field_spec(wide)],
        [field_spec(wide), weight_small],
        [field_shape, small_shape],
        [rows_scratch],
        flops=field_bytes * (2 * KY + columns),
        moved=field_bytes * 2 + mode_bytes * count,
        name="last",
    )
    return (outer(output), outer(back_field), spectral_grad, local_grad)


def solution(mesh):
    placed = (
        P("mp", None, None, "dp", None),
        P("mp", None, None, "dp", None),
        P("dp", "mp", None, None, None),
        P(),
    )
    return jax.shard_map(
        body,
        mesh=mesh,
        in_specs=placed,
        out_specs=(
            P("mp", None, None, "dp", None),
            P("mp", None, None, "dp", None),
            P("dp", "mp", None, None, None),
            P(),
        ),
        check_vma=False,
    )
```

```python
import functools
import math

import jax
import jax.numpy as jnp
import ml_dtypes
import numpy as np
from jax import lax
from jax.experimental import pallas as pl
from jax.experimental.pallas import tpu as pltpu
from jax.sharding import PartitionSpec as P

NX = 256
NY = 256
KX = 32
KY = 32
F32 = jnp.float32
BF16 = jnp.bfloat16
ROOT = math.sqrt(2.0 / math.pi)
CUBE = 0.044715
VMEM = 52 << 20


def to_bf16(values):
    return values.astype(np.float32).astype(ml_dtypes.bfloat16)


def y_tables(count):
    block = KY // count
    k_index = np.arange(KY)
    angle = 2.0 * math.pi / NY * (k_index[:, None] * np.arange(NY)[None, :] % NY)
    table = to_bf16(np.stack([np.cos(angle), -np.sin(angle)]) / math.sqrt(NY)).astype(np.float32)
    weight = np.where(k_index == 0, 1.0, 2.0)[None, :, None]

    def ordered(values):
        shaped = values.reshape(2, count // 2, 2, block, NY).transpose(2, 1, 0, 3, 4)
        return to_bf16(shaped.reshape(2 * KY, NY))

    return ordered(table), ordered(table * weight)


def x_tables(count):
    block = KY // count
    rows = NX // count
    stored = np.arange(NX)
    x_index = stored % rows * count + stored // rows
    frequency = np.arange(KX) - KX // 2
    angle = 2.0 * math.pi / NX * (frequency[:, None] * x_index[None, :] % NX)
    cosine = np.cos(angle) / math.sqrt(NX)
    sine = np.sin(angle) / math.sqrt(NX)
    table = np.stack([np.stack([cosine, sine], 1), np.stack([-sine, cosine], 1)])
    per = table.reshape(2, KX, 2, count, rows).transpose(3, 0, 1, 4, 2)
    spread = np.einsum("nojxr,ab->noajxrb", per, np.eye(block))
    spread = to_bf16(spread.reshape(count, 2 * block * KX, rows * 2 * block))
    return spread, np.ascontiguousarray(spread.transpose(0, 2, 1))


def dot(left, right):
    return lax.dot_general(left, right, (((1,), (0,)), ((), ())), preferred_element_type=F32)


def dot_nt(left, right):
    return lax.dot_general(left, right, (((1,), (1,)), ((), ())), preferred_element_type=F32)


def streamed(ref, buffer, sem, at, steps, axis, size):
    def copy(step):
        where = [slice(None)] * axis + [pl.ds(step % (KX // size) * size, size)]
        where[1] = pl.ds(step // (KX // size), 1)
        return pltpu.make_async_copy(ref.at[tuple(where)], buffer.at[step], sem.at[step])

    @pl.when(at == 0)
    def _():
        for step in range(steps):
            copy(step).start()

    copy(at).wait()
    return buffer.at[at]


def whole(shape):
    zeros = (0,) * len(shape)
    return pl.BlockSpec(shape, lambda *_: zeros)


def call(kernel, here, operands, grid, in_specs, out_specs, out_shape, scratch=(), flops=0, moved=0, name=None, aliases=None, limit=VMEM):
    return pl.pallas_call(
        kernel,
        out_shape=out_shape,
        grid_spec=pltpu.PrefetchScalarGridSpec(
            num_scalar_prefetch=1,
            grid=grid,
            in_specs=in_specs,
            out_specs=out_specs,
            scratch_shapes=list(scratch),
        ),
        compiler_params=pltpu.CompilerParams(
            dimension_semantics=("arbitrary",) * len(grid), vmem_limit_bytes=limit
        ),
        cost_estimate=pl.CostEstimate(flops=flops, bytes_accessed=moved, transcendentals=0),
        name=name,
        input_output_aliases=aliases or {},
    )(here, *operands)


def store_spectrum(here, parts, keep_ref, send_ref):
    chips, width, _ = keep_ref.shape
    unit = width // len(parts)
    half = chips * unit
    own_first = here[0] % 2 == 0
    kept = [jnp.where(own_first, part[:half], part[half:]) for part in parts]
    sent = [jnp.where(own_first, part[half:], part[:half]) for part in parts]
    for chip in range(chips):
        rows = slice(chip * unit, (chip + 1) * unit)
        keep_ref[chip] = jnp.concatenate([part[rows] for part in kept], 0).astype(BF16)
        send_ref[chip] = jnp.concatenate([part[rows] for part in sent], 0).astype(BF16)


def forward_y(count, here, field_hbm, keep_ref, send_ref, buffer, table, sem):
    step = pl.program_id(0)
    steps, size = buffer.shape[:2]

    def copy(at):
        return pltpu.make_async_copy(field_hbm.at[pl.ds(at * size, size)], buffer.at[at], sem.at[at])

    @pl.when(step == 0)
    def _():
        for at in range(steps):
            copy(at).start()
        block = KY // count
        row = lax.broadcasted_iota(jnp.int32, table.shape, 0)
        y = lax.broadcasted_iota(jnp.int32, table.shape, 1)
        core, chip = row // KY, row % KY // (2 * block)
        k = (2 * chip + core) * block + row % block
        turn = (k * y + row // block % 2 * (NY // 4)) % NY
        angle = (2.0 * math.pi / NY) * turn.astype(F32)
        table[...] = (jnp.cos(angle) * (1.0 / math.sqrt(NY))).astype(BF16)

    copy(step).wait()
    value = table[...]
    parts = [dot_nt(value, buffer[step, x]) for x in range(size)]
    store_spectrum(here, parts, keep_ref, send_ref)


def forward_x(here, keep_ref, got_ref, own_ref, other_ref, *outs):
    chip = here[0] // 2
    for step, out in enumerate(outs):
        at = chip ^ step
        out[...] = (dot(own_ref[0], keep_ref[at]) + dot(other_ref[0], got_ref[at])).astype(BF16)


def total(refs):
    values = [ref[...].astype(F32) for ref in refs]
    while len(values) > 1:
        values = [a + b for a, b in zip(values[::2], values[1::2])]
    return values[0].astype(BF16).astype(F32)


def half_sign(shape):
    lane = lax.broadcasted_iota(jnp.int32, shape, 1)
    return jnp.where(lane % 128 < 64, -1.0, 1.0)


def low_half(shape):
    return lax.broadcasted_iota(jnp.int32, shape, 1) < 64


def mix_forward(count, zs, here, *refs):
    terms, (w_hbm, out_ref, spread_ref, coeff, prod, buffer, sem) = refs[:count], refs[count:]
    step = pl.program_id(0)
    per = buffer.shape[3]
    modes = coeff.shape[0] // 2
    first = step * per
    w_ref = streamed(w_hbm, buffer, sem, step, buffer.shape[0], 2, per)

    @pl.when(first == 0)
    def _():
        coeff[...] = total(terms)

    shape = (2 * zs, zs * 64)
    row = lax.broadcasted_iota(jnp.int32, shape, 0)
    keep = lax.broadcasted_iota(jnp.int32, shape, 1) // 64 == row % zs
    is_real = row < zs
    for pair in range(per // 2):
        lefts, weights = [], []
        for sub in range(2):
            at = first + 2 * pair + sub
            real = jnp.broadcast_to(coeff[pl.ds(at, 1), :], shape)
            imag = jnp.broadcast_to(coeff[pl.ds(modes + at, 1), :], shape)
            lefts.append(jnp.where(keep, jnp.where(is_real, real, imag), 0.0))
            weights.append(w_ref[:, 0, 2 * pair + sub].reshape(zs * 64, 128))
        left = jnp.concatenate(lefts, 0).astype(BF16)
        base = pl.multiple_of((first + 2 * pair) * 2 * zs, 4 * zs)
        spread_ref[pl.ds(base, 4 * zs), :] = left
        got = dot(left, jnp.concatenate(weights, 1))
        prod[pl.ds(base, 2 * zs), :] = got[: 2 * zs, :128]
        prod[pl.ds(base + 2 * zs, 2 * zs), :] = got[2 * zs :, 128:]

    @pl.when(first + per == modes)
    def _():
        sign = half_sign((modes, 128))
        low = low_half((modes, 128))
        for tile in range(zs // 2):
            rows = []
            for z in (2 * tile, 2 * tile + 1):
                real = prod[pl.ds(z, modes, stride=2 * zs), :]
                imag = prod[pl.ds(zs + z, modes, stride=2 * zs), :]
                rows.append(real + sign * pltpu.roll(imag, 64, 1))
            lanes = slice(tile * 128, (tile + 1) * 128)
            out_ref[:modes, lanes] = jnp.where(low, rows[0], pltpu.roll(rows[1], 64, 1)).astype(BF16)
            out_ref[modes:, lanes] = jnp.where(low, pltpu.roll(rows[0], 64, 1), rows[1]).astype(BF16)


def mix_backward(count, zs, here, *refs):
    terms, locals_ = refs[:count], refs[count:-6]
    w_hbm, out_ref, pair_ref, prod, buffer, sem = refs[-6:]
    step = pl.program_id(0)
    per = buffer.shape[3]
    modes = prod.shape[1] // (2 * zs)
    first = step * per
    w_ref = streamed(w_hbm, buffer, sem, step, buffer.shape[0], 2, per)

    @pl.when(first == 0)
    def _():
        parts = [ref[...] for ref in locals_]
        while len(parts) > 1:
            parts = [a + b for a, b in zip(parts[::2], parts[1::2])]
        extra = 64 // zs
        value = jnp.concatenate([parts[0][at * extra : (at + 1) * extra] for at in range(zs)], 1)
        coarse = value.astype(BF16)
        out_ref[2 * modes : 2 * modes + extra] = coarse
        out_ref[2 * modes + extra :] = (value - coarse.astype(F32)).astype(BF16)
        grad = total(terms)
        sign = half_sign((modes, 128))
        low = low_half((modes, 128))
        for tile in range(zs // 2):
            lanes = slice(tile * 128, (tile + 1) * 128)
            real, imag = grad[:modes, lanes], grad[modes:, lanes]
            even = jnp.where(low, real, pltpu.roll(imag, 64, 1))
            odd = jnp.where(low, pltpu.roll(real, 64, 1), imag)
            for z, value in ((2 * tile, even), (2 * tile + 1, odd)):
                pair_ref[pl.ds(z, modes, stride=2 * zs), :] = value
                pair_ref[pl.ds(zs + z, modes, stride=2 * zs), :] = -sign * pltpu.roll(value, 64, 1)

    for mode in range(per):
        base = pl.multiple_of((first + mode) * 2 * zs, 2 * zs)
        left = pair_ref[pl.ds(base, 2 * zs), :].astype(BF16)
        got = dot_nt(left, w_ref[:, 0, mode].reshape(zs * 64, 128))
        for tile in range(zs // 2):
            prod[tile, pl.ds(base, 2 * zs), :] = got[:, tile * 128 : (tile + 1) * 128]

    @pl.when(first + per == modes)
    def _():
        low = low_half((modes, 128))
        for part in range(2):
            for tile in range(zs // 2):
                at = part * zs + 2 * tile
                even = prod[tile, pl.ds(at, modes, stride=2 * zs), :]
                odd = prod[tile, pl.ds(at + 1, modes, stride=2 * zs), :]
                out_ref[part * modes : (part + 1) * modes, tile * 128 : (tile + 1) * 128] = jnp.where(
                    low, even, odd
                ).astype(BF16)


def gram(zs, start, here, spread_ref, pair_ref, *refs):
    out_hbm, buffer, sem = refs[-3:]
    step = pl.program_id(0)
    steps, per = buffer.shape[0], buffer.shape[3]
    group = 4
    unit = 2 * zs
    first = (start + step) * per
    out_ref = buffer.at[step]
    shape = (group * unit, 128)
    owner = lax.broadcasted_iota(jnp.int32, shape, 0) // unit

    def copy(step):
        rows = pl.ds((start + step) * per // KX, 1)
        return pltpu.make_async_copy(
            buffer.at[step], out_hbm.at[:, rows, pl.ds((start + step) * per % KX, per)], sem.at[step]
        )

    for at in range(0, per, group):
        base = pl.multiple_of((first + at) * unit, group * unit)
        left = jnp.transpose(spread_ref[pl.ds(base, group * unit), :].astype(F32)).astype(BF16)
        grad = pair_ref[pl.ds(base, group * unit), :]
        right = jnp.concatenate([jnp.where(owner == t, grad, 0.0) for t in range(group)], 1)
        got = dot(left, right.astype(BF16))
        for t in range(group):
            out_ref[:, 0, at + t] = got[:, t * 128 : (t + 1) * 128].reshape(zs, 64, 128)
    copy(step).start()

    @pl.when(step == steps - 1)
    def _():
        for at in range(steps):
            copy(at).wait()


def grid_rows(here, blocks, x_ref, rows):
    chips = rows.shape[1]
    core, chip = here[0] % 2, here[0] // 2
    for slot, block in enumerate(blocks):
        at_core = core if slot < chips else 1 - core
        rows[at_core, chip ^ (slot % chips)] = dot(x_ref[0], block[...])


def row_at(rows, count, x):
    cores, chips, height, _ = rows.shape
    per = height // (pl.num_programs(0) * count)
    start = pl.multiple_of(pl.program_id(0) * (count * per), count * per)
    step = [rows[core, chip, pl.ds(start, count * per), :] for core in range(cores) for chip in range(chips)]
    joined = jnp.concatenate([value[x * per : (x + 1) * per] for value in step], 0)
    return jnp.transpose(joined).astype(BF16)


def middle(count, here, *refs):
    blocks, rest = refs[:count], refs[count:]
    x_ref, y_ref, weight_ref, field_ref, cot_ref = rest[:5]
    out_ref, grad_ref, keep_ref, send_ref, term_ref, rows, mixing, acc = rest[5:]
    step = pl.program_id(0)
    size = field_ref.shape[0]
    columns = field_ref.shape[1]
    zs = columns // 64

    @pl.when(step == 0)
    def _():
        grid_rows(here, blocks, x_ref, rows)
        mixing[...] = jnp.transpose(weight_ref[...].astype(F32)).astype(BF16)
        acc[...] = jnp.zeros_like(acc)

    table = y_ref[...]
    lefts = [row_at(rows, size, x) for x in range(size)]
    low = low_half((64, 128))
    parts, sums = [], []

    def reduce(x):
        got = dot_nt(jnp.concatenate([table, field_ref[x]], 0), grad_ref[x])
        parts.append(got[: 2 * KY])
        for tile in range(zs // 2):
            lanes = slice(tile * 128, (tile + 1) * 128)
            at = 2 * KY + tile * 128
            sums.append((lanes, jnp.where(low, got[at : at + 64, lanes], got[at + 64 : at + 128, lanes])))

    for x in range(size):
        for at in range(0, columns, 64):
            part = slice(at, at + 64)
            p = dot(lefts[x][part], table) + dot(mixing[...], field_ref[x, part])
            square = p * p
            t = jnp.tanh(p * (ROOT + ROOT * CUBE * square))
            half = 0.5 + 0.5 * t
            out_ref[x, part] = (p * half).astype(BF16)
            slope = half + p * (1.0 - t * t) * (0.5 * ROOT + 1.5 * ROOT * CUBE * square)
            grad_ref[x, part] = (cot_ref[x, part].astype(F32) * slope).astype(BF16)
        if x:
            reduce(x - 1)
    reduce(size - 1)
    store_spectrum(here, parts, keep_ref, send_ref)
    for lanes, value in sums:
        acc[:, lanes] += value

    @pl.when(step == pl.num_programs(0) - 1)
    def _():
        value = acc[...]
        parts = [value[:, at : at + 64] for at in range(0, columns, 64)]
        while len(parts) > 1:
            parts = [a + b for a, b in zip(parts[::2], parts[1::2])]
        term_ref[...] = parts[0]


def last(count, scale, here, *refs):
    blocks, rest = refs[:count], refs[count:]
    x_ref, y_ref, weight_ref, grad_ref, out_ref, local_ref, rows = rest
    columns = grad_ref.shape[1]
    size = grad_ref.shape[0]

    @pl.when(pl.program_id(0) == 0)
    def _():
        height = x_ref.shape[2]
        extra = 64 * 64 // columns
        grid_rows(here, [block.at[pl.ds(0, height)] for block in blocks], x_ref, rows)
        parts = [
            block[pl.ds(height, extra), :].astype(F32) + block[pl.ds(height + extra, extra), :].astype(F32)
            for block in blocks
        ]
        while len(parts) > 1:
            parts = [a + b for a, b in zip(parts[::2], parts[1::2])]
        for at in range(columns // 64):
            local_ref[at * extra : (at + 1) * extra, :] = parts[0][:, at * 64 : (at + 1) * 64] * scale

    table = y_ref[...]
    weight = weight_ref[...]
    lefts = [row_at(rows, size, x) for x in range(size)]
    for x in range(size):
        for at in range(0, columns, 64):
            part = slice(at, at + 64)
            value = dot(lefts[x][part], table) + dot(weight, grad_ref[x, part])
            out_ref[x, part] = value.astype(BF16)


def flip(axis, size, bit):
    return functools.partial(lax.ppermute, axis_name=axis, perm=[(at, at ^ bit) for at in range(size)])


def body(features, out_grad, spectral_weight, local_weight):
    count = lax.axis_size("mp")
    dp_count = lax.axis_size("dp")
    chips = count // 2
    rows_here, grid_y, snaps, zs, channels = features.shape
    mode_rows = spectral_weight.shape[1]
    columns = snaps * zs * channels
    modes = mode_rows * KX
    unit = 2 * mode_rows
    here = lax.axis_index("mp").astype(jnp.int32).reshape(1)

    y_plain, y_weighted = y_tables(count)
    x_forward, x_back = x_tables(count)

    def inner(array):
        return jnp.transpose(array, (0, 2, 3, 4, 1)).reshape(rows_here, columns, grid_y)

    def outer(array):
        shaped = array.reshape(rows_here, snaps, zs, channels, grid_y)
        return jnp.transpose(shaped, (0, 4, 1, 2, 3))

    field, cot = inner(features), inner(out_grad)
    wide, chunk = min(16, rows_here), min(8, rows_here)

    def field_spec(size):
        return pl.BlockSpec((size, columns, grid_y), lambda g, _: (g, 0, 0))

    def half_spec(size):
        return pl.BlockSpec((chips, size * unit, columns), lambda g, _: (0, g, 0))

    field_shape = jax.ShapeDtypeStruct((rows_here, columns, grid_y), BF16)
    half_shape = jax.ShapeDtypeStruct((chips, rows_here * unit, columns), BF16)
    y_spec = whole((2 * KY, grid_y))
    mode_shape = jax.ShapeDtypeStruct((2 * modes, columns), BF16)
    mode_spec = whole((2 * modes, columns))
    weight_small = whole((channels, channels))
    small_shape = jax.ShapeDtypeStruct((channels, channels), F32)
    mixing_scratch = pltpu.VMEM((channels, channels), BF16)
    extra = 2 * channels * channels // columns
    back_spec = whole((2 * modes + extra, columns))
    back_shape = jax.ShapeDtypeStruct((2 * modes + extra, columns), BF16)
    field_bytes = rows_here * columns * grid_y * 2
    mode_bytes = 4 * modes * columns

    def to_chips(keep, send, beside=None):
        got = flip("mp", count, 1)(send)
        x_spec = (1, 2 * modes, rows_here * unit)
        outs = call(
            forward_x,
            here,
            (keep, got, x_forward, x_forward),
            (1,),
            [
                whole(keep.shape),
                whole(keep.shape),
                pl.BlockSpec(x_spec, lambda g, m: (m[0], 0, 0)),
                pl.BlockSpec(x_spec, lambda g, m: (m[0] ^ 1, 0, 0)),
            ],
            [mode_spec] * chips,
            [mode_shape] * chips,
            flops=8 * chips * modes * rows_here * unit * columns,
            moved=mode_bytes * 3 * chips,
            name="forward_x",
            limit=8 << 20,
        )
        outs = list(outs)
        if beside is not None:
            outs[-1], beside = lax.optimization_barrier((outs[-1], beside))
        return [outs[0]] + [flip("mp", count, 2 * bit)(outs[bit]) for bit in range(1, chips)], beside

    def to_all(block):
        mine = [block] + [flip("mp", count, 2 * bit)(block) for bit in range(1, chips)]
        return mine + [flip("mp", count, 1)(value) for value in mine]

    weight_spec = pl.BlockSpec(memory_space=pl.ANY)

    def weight_scratch(per):
        return [
            pltpu.VMEM((modes // per, zs, 1, per, channels, 2 * channels), BF16),
            pltpu.SemaphoreType.DMA((modes // per,)),
        ]

    spread_shape = (modes * 2 * zs, columns)
    pair_shape = (modes * 2 * zs, 2 * channels)
    weight_bytes = zs * modes * channels * 2 * channels * 2

    keep, send = call(
        functools.partial(forward_y, count),
        here,
        (field,),
        (rows_here // chunk,),
        [pl.BlockSpec(memory_space=pltpu.HBM)],
        [half_spec(chunk)] * 2,
        [half_shape] * 2,
        [
            pltpu.VMEM((rows_here // chunk, chunk, columns, grid_y), BF16),
            pltpu.VMEM((2 * KY, grid_y), BF16),
            pltpu.SemaphoreType.DMA((rows_here // chunk,)),
        ],
        flops=field_bytes * 2 * KY,
        moved=field_bytes + mode_bytes * count,
        name="forward_y",
    )
    terms, _ = to_chips(keep, send)
    mixed, spread = call(
        functools.partial(mix_forward, chips, zs),
        here,
        (*terms, spectral_weight),
        (modes // 16,),
        [mode_spec] * chips + [weight_spec],
        [mode_spec, whole(spread_shape)],
        [mode_shape, jax.ShapeDtypeStruct(spread_shape, BF16)],
        [pltpu.VMEM((2 * modes, columns), F32), pltpu.VMEM(pair_shape, F32)] + weight_scratch(16),
        flops=weight_bytes * 8,
        moved=weight_bytes + mode_bytes * chips,
        name="mix_forward",
    )
    blocks = to_all(mixed)
    x_back_spec = pl.BlockSpec((1, rows_here * unit, 2 * modes), lambda g, m: (m[0], 0, 0))
    rows_scratch = pltpu.VMEM((2, chips, rows_here * unit, columns), F32)
    output, preact_grad, keep, send, local_term = call(
        functools.partial(middle, count),
        here,
        (*blocks, x_back, y_weighted, local_weight, field, cot),
        (rows_here // chunk,),
        [mode_spec] * count + [x_back_spec, y_spec, weight_small] + [field_spec(chunk)] * 2,
        [field_spec(chunk)] * 2 + [half_spec(chunk)] * 2 + [weight_small],
        [field_shape, field_shape, half_shape, half_shape, small_shape],
        [rows_scratch, mixing_scratch, pltpu.VMEM((channels, columns), F32)],
        flops=field_bytes * (4 * KY + 2 * columns),
        moved=field_bytes * 4 + mode_bytes * count * 2,
        name="middle",
    )
    first_got = flip("dp", dp_count, 1)(local_term) if dp_count > 1 else jnp.zeros_like(local_term)
    terms, first_got = to_chips(keep, send, first_got)
    locals_, bit = [local_term, first_got], 2
    while bit < dp_count:
        local_term = locals_[0] + locals_[1]
        locals_ = [local_term, flip("dp", dp_count, bit)(local_term)]
        bit *= 2
    back, pairs = call(
        functools.partial(mix_backward, chips, zs),
        here,
        (*terms, *locals_, spectral_weight),
        (modes // KX,),
        [mode_spec] * chips + [weight_small] * len(locals_) + [weight_spec],
        [back_spec, whole(pair_shape)],
        [back_shape, jax.ShapeDtypeStruct(pair_shape, F32)],
        [pltpu.VMEM((zs // 2, modes * 2 * zs, 128), F32)] + weight_scratch(KX),
        flops=weight_bytes * 8,
        moved=weight_bytes + mode_bytes * chips,
        name="mix_backward",
        limit=24 << 20,
    )
    gram_steps = modes // 8
    early = gram_steps * 3 // 4

    def gram_part(start, steps, before):
        per = 8
        return call(
            functools.partial(gram, zs, start),
            here,
            (spread, pairs, *before),
            (steps,),
            [whole(spread_shape), whole(pair_shape)] + [pl.BlockSpec(memory_space=pl.ANY)] * len(before),
            pl.BlockSpec(memory_space=pl.ANY),
            jax.ShapeDtypeStruct(spectral_weight.shape, F32),
            [
                pltpu.VMEM((steps, zs, 1, per, channels, 2 * channels), F32),
                pltpu.SemaphoreType.DMA((steps,)),
            ],
            flops=weight_bytes * 4,
            moved=weight_bytes,
            name="gram",
            aliases={3: 0} if before else {},
        )

    mine = [back] + [flip("mp", count, 2 * bit)(back) for bit in range(1, chips)]
    spectral_grad = gram_part(0, early, ())
    *others, spectral_grad = lax.optimization_barrier((*mine[1:], spectral_grad))
    blocks = [back, *others] + [flip("mp", count, 1)(value) for value in (back, *others)]
    spectral_grad = gram_part(early, gram_steps - early, (spectral_grad,))
    scale = 1.0 / math.sqrt(NX * NY * snaps * dp_count * zs)
    back_field, local_grad = call(
        functools.partial(last, count, scale),
        here,
        (*blocks, x_back, y_plain, local_weight, preact_grad),
        (rows_here // wide,),
        [back_spec] * count + [x_back_spec, y_spec, weight_small, field_spec(wide)],
        [field_spec(wide), weight_small],
        [field_shape, small_shape],
        [rows_scratch],
        flops=field_bytes * (2 * KY + columns),
        moved=field_bytes * 2 + mode_bytes * count,
        name="last",
    )
    return (outer(output), outer(back_field), spectral_grad, local_grad)


def solution(mesh):
    placed = (
        P("mp", None, None, "dp", None),
        P("mp", None, None, "dp", None),
        P("dp", "mp", None, None, None),
        P(),
    )
    return jax.shard_map(
        body,
        mesh=mesh,
        in_specs=placed,
        out_specs=(
            P("mp", None, None, "dp", None),
            P("mp", None, None, "dp", None),
            P("dp", "mp", None, None, None),
            P(),
        ),
        check_vma=False,
    )
```
